32 devices in a mesh: gx: 4 (over y, core), gy: 4 (over z), gz: 2 (over x).
Axes of the slice: x: 2, y: 2, z: 4, core: 2. Of those that a mesh axis runs over, the one named last changes fastest.
Arguments:
- orbital_values: bfloat16 [64, 64, 48, 384], P('gx', 'gy', 'gz'), may hold values from -6 to 6
- dm_slabs: bfloat16 [1536, 8, 384], P(('gx', 'gy', 'gz')), may hold values from -0.015625 to 0.015625
- slab_tile: int32 [1536], P(('gx', 'gy', 'gz')), may hold values from 0 to 15, as said below
- slab_place: int32 [1536], P(('gx', 'gy', 'gz')), may hold values from 0 to 47, as said below
Outputs:
- potential: float32 [64, 64, 48], P('gx', 'gy', 'gz')
- pot_slabs: bfloat16 [1536, 8, 384], P(('gx', 'gy', 'gz'))
The draws below stay inside these ranges and needn't reach their ends.
Inputs may be any that keep to these rules, and one draw needn't show every extreme that they name: `slab_tile`: within each layer along gz, every tile of that layer has exactly one slab for each place 0 .. 47, held by devices of the same layer; no device holds more than 6 slabs of one tile, and in every layer some device holds exactly 6 slabs of some tile. See slab_tile: the pair (slab_tile, slab_place) is different for all slabs of one layer.
All inputs are finite; a program needn't handle non-finite values.
Results may differ from the reference program's by a relative error of at most 0.0023.
Values may be sent and summed in bfloat16 or wider, within the bound.
No kernel may reach another device: no remote copies, remote signals or barrier semaphores. Data moves between devices by JAX's collectives and lax.ppermute only.
A program may use at most 64 MiB of HBM per device.

```python
import math
import jax
import jax.numpy as jnp
import numpy as np
from jax import lax

TX = 16
TY = 16
TZ = 24
RADIUS = 8
ATOM_ORB = 8
LIST_BLK = 48
LIST_ORB = 384
CAP = 6
NX = 64
NY = 64
NZ = 48
SLABS = 1536
N_GX = 4
N_GY = 4
N_GZ = 2


def route_tables(key):
    tile_count = N_GX * N_GY
    surplus = LIST_BLK - CAP
    spread = min(tile_count - 1, surplus)
    base_count = surplus // spread
    leftover = surplus - base_count * spread
    counts = [CAP] + [base_count + 1] * leftover + [base_count] * (spread - leftover)
    offset_index = jnp.asarray(np.repeat(np.arange(len(counts)), counts).astype(np.int32))

    def one_layer(layer_key):
        key_shift, key_label, key_order, key_list = jax.random.split(layer_key, 4)
        shifts = jax.random.permutation(key_shift, tile_count)[:len(counts)].astype(jnp.int32)
        relabel = jax.random.permutation(key_label, tile_count).astype(jnp.int32)
        scores = jax.random.randint(key_order, (tile_count, LIST_BLK), 0, 1 << 20) * LIST_BLK + jnp.arange(LIST_BLK, dtype=jnp.int32)[None, :]
        shuffled = jnp.argsort(scores, axis=1, stable=True).astype(jnp.int32)
        chosen = offset_index[shuffled]
        owners = relabel[(jnp.arange(tile_count, dtype=jnp.int32)[:, None] + shifts[chosen]) % tile_count]
        tiebreak = jax.random.permutation(key_list, tile_count * LIST_BLK).astype(jnp.int32)
        ordering = jnp.argsort(owners.reshape(-1) * (tile_count * LIST_BLK) + tiebreak, stable=True).astype(jnp.int32)
        return ((ordering // LIST_BLK).reshape(tile_count, LIST_BLK), (ordering % LIST_BLK).reshape(tile_count, LIST_BLK))
    tile_ids, place_ids = jax.vmap(one_layer)(jax.random.split(key, N_GZ))
    return (tile_ids.transpose(1, 0, 2).reshape(-1), place_ids.transpose(1, 0, 2).reshape(-1))


def draw_slab_tile(key, part):
    return route_tables(jax.random.fold_in(key, 11))[0]


def draw_slab_place(key, part):
    return route_tables(jax.random.fold_in(key, 11))[1]


def block_scale(key, extent, shards, least, largest):
    def one(axis_at, parts):
        heights = jax.random.uniform(jax.random.fold_in(jax.random.fold_in(key, 6), axis_at), (parts,), jnp.float32, least / len(shards), largest / len(shards))
        return jnp.repeat(jnp.exp(heights), extent[axis_at] // parts).reshape((-1,) + (1,) * (len(extent) - axis_at - 1))

    level = one(*shards[0])
    for cut in shards[1:]:
        level = level * one(*cut)
    return level


def centred(own_key, extent, scale, reach, shards=(), kind=jnp.bfloat16):
    entries = jax.random.normal(own_key, extent, jnp.float32) * scale
    if len(shards) > 0:
        entries = block_scale(own_key, extent, shards, -0.22, 0.18) * entries
    return jnp.clip(entries, min=-reach, max=reach).astype(kind)


def setup_inputs(seed: int = 0) -> dict:
    arg_keys = jax.random.split(jax.random.key(seed), 5)
    return {
        "orbital_values": centred(arg_keys[0], (NX, NY, NZ, LIST_ORB), 1.0, 6.0, ((0, 4), (1, 4), (2, 2))),
        "dm_slabs": centred(arg_keys[1], (SLABS, ATOM_ORB, LIST_ORB), (LIST_ORB * LIST_ORB) ** -0.5, 0.015625, ((0, 32),)),
        "slab_tile": draw_slab_tile(jax.random.fold_in(arg_keys[4], 71), 0),
        "slab_place": draw_slab_place(jax.random.fold_in(arg_keys[4], 71), 0),
    }


ALPHAS = (0.012, 0.025, 0.05, 0.1, 0.2, 0.4, 0.8, 1.6)
MIXES = (0.30, 0.30, 0.32, 0.34, 0.36, 0.38, 0.40, 0.42)


def kernel_tables(radius):
    tap_table = [[math.exp(-alpha * offset * offset) for offset in range(-radius, radius + 1)] for alpha in ALPHAS]
    mix = [MIXES[term] / (sum(tap * tap for tap in tap_table[term]) ** 1.5) for term in range(len(ALPHAS))]
    return tap_table, mix


def smooth_periodic(density, radius):
    tap_table, mix = kernel_tables(radius)
    potential = None
    for term_idx in range(len(ALPHAS)):
        current = density
        for axis_idx in range(3):
            running = None
            for offset in range(2 * radius + 1):
                addend = tap_table[term_idx][offset] * jnp.roll(current, radius - offset, axis=axis_idx)
                running = addend if running is None else running + addend
            current = running
        addend = mix[term_idx] * current
        potential = addend if potential is None else potential + addend
    return potential


def reference(orbital_values, dm_slabs, slab_tile, slab_place):
    devices = N_GX * N_GY * N_GZ
    tile_pts = TX * TY * TZ
    row_width = ATOM_ORB * LIST_ORB
    owner_dev = jnp.arange(devices * LIST_BLK, dtype=jnp.int32) // LIST_BLK
    layer_idx = owner_dev % N_GZ
    target_row = ((slab_tile * N_GZ + layer_idx) * LIST_BLK + slab_place).astype(jnp.int32)
    inverse = jnp.zeros((devices * LIST_BLK,), jnp.int32).at[target_row].set(jnp.arange(devices * LIST_BLK, dtype=jnp.int32))
    tile_matrices = dm_slabs.reshape(devices * LIST_BLK, row_width)[inverse].reshape(devices, LIST_ORB, LIST_ORB)
    tile_values = orbital_values.reshape(N_GX, TX, N_GY, TY, N_GZ, TZ, LIST_ORB).transpose(0, 2, 4, 1, 3, 5, 6).reshape(devices, tile_pts, LIST_ORB)

    def density_of(operands):
        values, matrix = operands
        product = jnp.dot(values, matrix, preferred_element_type=jnp.float32)
        return jnp.sum(product * values.astype(jnp.float32), axis=1)

    densities = lax.map(density_of, (tile_values, tile_matrices))
    grid_density = densities.reshape(N_GX, N_GY, N_GZ, TX, TY, TZ).transpose(0, 3, 1, 4, 2, 5).reshape(NX, NY, NZ)
    potential = smooth_periodic(grid_density, RADIUS)
    tile_field = potential.reshape(N_GX, TX, N_GY, TY, N_GZ, TZ).transpose(0, 2, 4, 1, 3, 5).reshape(devices, tile_pts)
    quad_weight = float(tile_pts) ** -0.5

    def potential_of(operands):
        values, field_vals = operands
        weighted = (field_vals[:, None] * values.astype(jnp.float32) * quad_weight).astype(jnp.bfloat16)
        return lax.dot_general(values, weighted, (((0,), (0,)), ((), ())), preferred_element_type=jnp.float32).astype(jnp.bfloat16)

    tile_potentials = lax.map(potential_of, (tile_values, tile_field))
    pot_slabs = tile_potentials.reshape(devices * LIST_BLK, ATOM_ORB, LIST_ORB)[target_row]
    return potential, pot_slabs
```

```python
import functools
import math

import jax
import jax.numpy as jnp
import numpy as np
from jax import lax
from jax.experimental import pallas as pl
from jax.experimental.pallas import tpu as pltpu
from jax.sharding import PartitionSpec as P

RADIUS = 8
LANES = 128

ALPHAS = (0.012, 0.025, 0.05, 0.1, 0.2, 0.4, 0.8, 1.6)
MIXES = (0.3, 0.3, 0.32, 0.34, 0.36, 0.38, 0.4, 0.42)

VMEM_SPEC = pl.BlockSpec(memory_space=pltpu.VMEM)
SMEM_SPEC = pl.BlockSpec(memory_space=pltpu.SMEM)


def kernel_tables(radius):
    tap_table = [
        [math.exp(-alpha * offset * offset) for offset in range(-radius, radius + 1)]
        for alpha in ALPHAS
    ]
    mix = [
        MIXES[term] / sum((tap * tap for tap in tap_table[term])) ** 1.5
        for term in range(len(ALPHAS))
    ]
    return (tap_table, mix)


def for_each_slab(tile_ref, count_ref, tile_count, slab_count, visit):
    for t in range(tile_count):
        count_ref[t] = 0

    def step(i, carry):
        t = tile_ref[i]
        slot = count_ref[t]
        count_ref[t] = slot + 1
        visit(i, t, slot)
        return carry

    lax.fori_loop(0, slab_count, step, 0, unroll=4)


def pack_kernel(capacity, chunks, tile_ref, place_ref, slab_ref, out_ref, count_ref, label_ref):
    tile_count = out_ref.shape[0]
    label_ref[...] = jnp.full(label_ref.shape, -1.0, jnp.float32)

    def visit(i, t, slot):
        slab = slab_ref[i]
        for c in range(chunks):
            out_ref[t, slot * chunks + c] = slab[:, c * LANES : (c + 1) * LANES]
        label = place_ref[i].astype(jnp.float32)
        label_ref[t, pl.ds(slot, 1), :] = jnp.full((1, LANES), label, jnp.float32)

    for_each_slab(tile_ref, count_ref, tile_count, slab_ref.shape[0], visit)
    out_ref[:, capacity * chunks] = label_ref[...].astype(jnp.bfloat16)


def density_kernel(
    capacity, chunks, rows, place_ref, arrived_ref, values_ref, out_ref, wide_ref, turned_ref
):
    tile_count = arrived_ref.shape[0]
    step = pl.program_id(0)
    list_orb = wide_ref.shape[0]

    @pl.when(step == 0)
    def _():
        def visit(j, carry):
            place = place_ref[j]

            @pl.when(place >= 0)
            def _():
                t, k = j // capacity, j % capacity
                row = pl.multiple_of(place * rows, rows)
                for c in range(chunks):
                    wide_ref[pl.ds(row, rows), c * LANES : (c + 1) * LANES] = arrived_ref[
                        t, k * chunks + c
                    ].astype(jnp.float32)

            return carry

        lax.fori_loop(0, tile_count * capacity, visit, 0, unroll=4)
        turned_ref[...] = wide_ref[...].T.astype(jnp.bfloat16)

    planes = values_ref.shape[1] // out_ref.shape[1]
    width = out_ref.shape[1]
    for q in range(planes):
        block = values_ref[:, q * width : (q + 1) * width]
        mixed = jnp.dot(turned_ref[...], block, preferred_element_type=jnp.float32)
        density = jnp.sum(mixed * block.astype(jnp.float32), axis=0, keepdims=True)
        out_ref[pl.ds(step * planes + q, 1), :] = density


def filter_kernel(parts, size_x, size_y, taps_ref, fold_ref, *refs):
    grids, bands = refs[:parts], refs[parts : 2 * parts]
    out_ref, first_ref, second_ref = refs[2 * parts :]
    wide_x, wide_y, size_z = grids[0].shape
    lanes = first_ref.shape[-1]
    total = None
    for grid_ref, band_ref in zip(grids, bands):
        term = jnp.dot(
            grid_ref[...].reshape(wide_x * wide_y, size_z),
            band_ref[...],
            precision=lax.Precision.HIGHEST,
            preferred_element_type=jnp.float32,
        )
        total = term if total is None else total + term
    first_ref[...] = total.reshape(wide_x, wide_y, lanes)

    def tap(distance):
        return jnp.broadcast_to(taps_ref[distance : distance + 1, :], (size_y, lanes))

    def along_y(x, carry):
        run = tap(0) * first_ref[x, RADIUS : RADIUS + size_y, :]
        for d in range(1, RADIUS + 1):
            pair = (
                first_ref[x, RADIUS - d : RADIUS - d + size_y, :]
                + first_ref[x, RADIUS + d : RADIUS + d + size_y, :]
            )
            run = run + tap(d) * pair
        second_ref[x] = run
        return carry

    lax.fori_loop(0, wide_x, along_y, 0)

    def along_x(x, carry):
        run = tap(0) * second_ref[x + RADIUS]
        for d in range(1, RADIUS + 1):
            pair = second_ref[x + (RADIUS - d)] + second_ref[x + (RADIUS + d)]
            run = run + tap(d) * pair
        first_ref[x, 0:size_y, :] = run
        return carry

    lax.fori_loop(0, size_x, along_x, 0)
    filtered = first_ref[0:size_x, 0:size_y, :].reshape(size_x * size_y, lanes)
    folded = jnp.dot(
        filtered,
        fold_ref[...],
        precision=lax.Precision.HIGHEST,
        preferred_element_type=jnp.float32,
    )
    out_ref[...] = folded.reshape(size_x, size_y, size_z)


def potential_kernel(
    capacity, chunks, rows, weight, place_ref, field_ref, values_ref, out_ref, total_ref
):
    step = pl.program_id(0)
    width = field_ref.shape[1]
    planes = values_ref.shape[1] // width
    total = None
    for q in range(planes):
        field = field_ref[pl.ds(step * planes + q, 1), :]
        block = values_ref[:, q * width : (q + 1) * width]
        weighted = (field * block.astype(jnp.float32) * weight).astype(jnp.bfloat16)
        term = lax.dot_general(
            block, weighted, (((1,), (1,)), ((), ())), preferred_element_type=jnp.float32
        )
        total = term if total is None else total + term

    @pl.when(step == 0)
    def _():
        total_ref[...] = total

    @pl.when(step > 0)
    def _():
        total_ref[...] += total

    @pl.when(step == pl.num_programs(0) - 1)
    def _():
        def visit(j, carry):
            t, k = j // capacity, j % capacity
            row = pl.multiple_of(jnp.maximum(place_ref[j], 0) * rows, rows)
            for c in range(chunks):
                out_ref[t, k * chunks + c] = total_ref[
                    pl.ds(row, rows), c * LANES : (c + 1) * LANES
                ].astype(jnp.bfloat16)
            return carry

        lax.fori_loop(0, out_ref.shape[0] * capacity, visit, 0, unroll=4)


def unpack_kernel(chunks, tile_count, tile_ref, back_ref, out_ref, count_ref):
    def visit(i, t, slot):
        for c in range(chunks):
            out_ref[i, :, c * LANES : (c + 1) * LANES] = back_ref[t, slot * chunks + c]

    for_each_slab(tile_ref, count_ref, tile_count, out_ref.shape[0], visit)


def ring(size, shift):
    return [(i, (i + shift) % size) for i in range(size)]


def both_sides(block, axis, dim, width):
    size, length = lax.axis_size(axis), block.shape[dim]
    before = lax.ppermute(
        lax.slice_in_dim(block, length - width, length, axis=dim), axis, ring(size, 1)
    )
    after = lax.ppermute(lax.slice_in_dim(block, 0, width, axis=dim), axis, ring(size, -1))
    return jnp.concatenate([before, block, after], axis=dim)


def band_tables(size_z, neighbours):
    tap_table, mix = kernel_tables(RADIUS)

    def band(shift):
        table = np.zeros((size_z, len(ALPHAS), size_z), np.float64)
        for m in range(len(ALPHAS)):
            for source in range(size_z):
                for target in range(size_z):
                    offset = source + shift - target
                    if abs(offset) <= RADIUS:
                        table[source, m, target] = tap_table[m][offset + RADIUS]
        return table.reshape(size_z, len(ALPHAS) * size_z)

    own, low, high = band(0), band(-size_z), band(size_z)
    bands = {0: [own + low + high], 1: [own, low + high], 2: [own, low, high]}[neighbours]
    taps = np.zeros((16, len(ALPHAS) * size_z), np.float64)
    for d in range(RADIUS + 1):
        taps[d] = np.repeat([row[RADIUS + d] for row in tap_table], size_z)
    fold = np.concatenate([mix[m] * np.eye(size_z) for m in range(len(ALPHAS))], axis=0)
    return (
        [b.astype(np.float32) for b in bands],
        taps.astype(np.float32),
        fold.astype(np.float32),
    )


def local(orbital_values, dm_slabs, slab_tile, slab_place):
    size_x, size_y, size_z, list_orb = orbital_values.shape
    slab_count, atom_orb, _ = dm_slabs.shape
    list_blk = list_orb // atom_orb
    tile_count = lax.axis_size("gx") * lax.axis_size("gy")
    capacity = max(2, 2 * ((list_blk + tile_count - 1) // tile_count))
    chunks = list_orb // LANES
    tile_points = size_x * size_y * size_z
    plane = size_y * size_z
    counts = pltpu.SMEM((tile_count,), jnp.int32)

    packed = pl.pallas_call(
        functools.partial(pack_kernel, capacity, chunks),
        out_shape=jax.ShapeDtypeStruct(
            (tile_count, capacity * chunks + 1, atom_orb, LANES), jnp.bfloat16
        ),
        in_specs=[SMEM_SPEC, SMEM_SPEC, VMEM_SPEC],
        out_specs=VMEM_SPEC,
        scratch_shapes=[counts, pltpu.VMEM((tile_count, atom_orb, LANES), jnp.float32)],
        name="pack",
    )(slab_tile, slab_place, dm_slabs)
    arrived = lax.all_to_all(packed, ("gx", "gy"), split_axis=0, concat_axis=0, tiled=True)
    places = arrived[:, capacity * chunks, :capacity, 0].astype(jnp.int32).reshape(-1)
    turned = orbital_values.reshape(tile_points, list_orb).T

    steps = 4
    slice_spec = pl.BlockSpec((list_orb, tile_points // steps), lambda i: (0, i))
    density = pl.pallas_call(
        functools.partial(density_kernel, capacity, chunks, atom_orb),
        grid=(steps,),
        out_shape=jax.ShapeDtypeStruct((size_x, plane), jnp.float32),
        in_specs=[SMEM_SPEC, VMEM_SPEC, slice_spec],
        out_specs=pl.BlockSpec((size_x, plane), lambda i: (0, 0)),
        scratch_shapes=[
            pltpu.VMEM((list_orb, list_orb), jnp.float32),
            pltpu.VMEM((list_orb, list_orb), jnp.bfloat16),
        ],
        name="density",
    )(places, arrived, turned)

    grid = both_sides(density, "gy", 1, RADIUS * size_z)
    wide_y = grid.shape[1] // size_z
    layers = lax.axis_size("gz")
    if layers == 1:
        stack = grid[None]
    elif layers == 2:
        stack = jnp.stack([grid, lax.ppermute(grid, "gz", ring(layers, 1))])
    else:
        low = lax.ppermute(grid, "gz", ring(layers, 1))
        high = lax.ppermute(grid, "gz", ring(layers, -1))
        stack = jnp.stack([grid, low, high])
    stack = both_sides(stack, "gx", 1, RADIUS)
    parts, wide_x, _ = stack.shape
    stack = stack.reshape(parts, wide_x, wide_y, size_z)
    bands, taps, fold = band_tables(size_z, parts - 1)
    lanes = taps.shape[1]
    potential = pl.pallas_call(
        functools.partial(filter_kernel, parts, size_x, size_y),
        out_shape=jax.ShapeDtypeStruct((size_x, size_y, size_z), jnp.float32),
        in_specs=[VMEM_SPEC] * (2 + 2 * parts),
        out_specs=VMEM_SPEC,
        scratch_shapes=[
            pltpu.VMEM((wide_x, wide_y, lanes), jnp.float32),
            pltpu.VMEM((wide_x, size_y, lanes), jnp.float32),
        ],
        name="filter",
    )(jnp.asarray(taps), jnp.asarray(fold), *[stack[i] for i in range(parts)], *map(jnp.asarray, bands))

    returned = pl.pallas_call(
        functools.partial(
            potential_kernel, capacity, chunks, atom_orb, float(tile_points) ** (-0.5)
        ),
        grid=(steps,),
        out_shape=jax.ShapeDtypeStruct(
            (tile_count, capacity * chunks, atom_orb, LANES), jnp.bfloat16
        ),
        in_specs=[SMEM_SPEC, pl.BlockSpec((size_x, plane), lambda i: (0, 0)), slice_spec],
        out_specs=pl.BlockSpec(
            (tile_count, capacity * chunks, atom_orb, LANES), lambda i: (0, 0, 0, 0)
        ),
        scratch_shapes=[pltpu.VMEM((list_orb, list_orb), jnp.float32)],
        name="potential",
    )(places, potential.reshape(size_x, plane), turned)
    back = lax.all_to_all(returned, ("gx", "gy"), split_axis=0, concat_axis=0, tiled=True)
    own_rows = pl.pallas_call(
        functools.partial(unpack_kernel, chunks, tile_count),
        out_shape=jax.ShapeDtypeStruct((slab_count, atom_orb, list_orb), jnp.bfloat16),
        in_specs=[SMEM_SPEC, VMEM_SPEC],
        out_specs=VMEM_SPEC,
        scratch_shapes=[counts],
        name="unpack",
    )(slab_tile, back)
    return (potential, own_rows)


def solution(mesh):
    placed = (
        P("gx", "gy", "gz", None),
        P(("gx", "gy", "gz"), None, None),
        P(("gx", "gy", "gz")),
        P(("gx", "gy", "gz")),
    )
    return jax.shard_map(
        local,
        mesh=mesh,
        in_specs=placed,
        out_specs=(P("gx", "gy", "gz"), P(("gx", "gy", "gz"), None, None)),
        check_vma=False,
    )
```

```python
import functools
import math

import jax
import jax.numpy as jnp
import numpy as np
from jax import lax
from jax.experimental import pallas as pl
from jax.experimental.pallas import tpu as pltpu
from jax.sharding import PartitionSpec as P

RADIUS = 8
LANES = 128

ALPHAS = (0.012, 0.025, 0.05, 0.1, 0.2, 0.4, 0.8, 1.6)
MIXES = (0.3, 0.3, 0.32, 0.34, 0.36, 0.38, 0.4, 0.42)

VMEM_SPEC = pl.BlockSpec(memory_space=pltpu.VMEM)
SMEM_SPEC = pl.BlockSpec(memory_space=pltpu.SMEM)


def grant(mebibytes):
    return pltpu.CompilerParams(vmem_limit_bytes=mebibytes << 20)


def kernel_tables(radius):
    tap_table = [
        [math.exp(-alpha * offset * offset) for offset in range(-radius, radius + 1)]
        for alpha in ALPHAS
    ]
    mix = [
        MIXES[term] / sum((tap * tap for tap in tap_table[term])) ** 1.5
        for term in range(len(ALPHAS))
    ]
    return (tap_table, mix)


def for_each_slab(tile_ref, count_ref, tile_count, slab_count, visit):
    for t in range(tile_count):
        count_ref[t] = 0

    def step(i, carry):
        t = tile_ref[i]
        slot = count_ref[t]
        count_ref[t] = slot + 1
        visit(i, t, slot)
        return carry

    lax.fori_loop(0, slab_count, step, 0, unroll=4)


def pack_kernel(capacity, chunks, empty, tile_ref, place_ref, slab_ref, out_ref, count_ref, label_ref):
    tile_count = out_ref.shape[0]
    label_ref[...] = jnp.full(label_ref.shape, empty, jnp.float32)
    out_ref[...] = jnp.zeros(out_ref.shape, out_ref.dtype)

    def visit(i, t, slot):
        slab = slab_ref[i]
        for c in range(chunks):
            out_ref[t, slot * chunks + c] = slab[:, c * LANES : (c + 1) * LANES]
        label = place_ref[i].astype(jnp.float32)
        label_ref[t, pl.ds(slot, 1), :] = jnp.full((1, LANES), label, jnp.float32)

    for_each_slab(tile_ref, count_ref, tile_count, slab_ref.shape[0], visit)
    out_ref[:, capacity * chunks] = label_ref[...].astype(jnp.bfloat16)


def density_kernel(
    capacity, chunks, piece, arrived_ref, values_ref, out_ref, low_ref, high_ref, wide_ref, turned_ref
):
    tile_count, _, rows, _ = arrived_ref.shape
    step = pl.program_id(0)
    list_orb = turned_ref.shape[0]
    slots = tile_count * capacity

    @pl.when(step == 0)
    def _():
        labels = arrived_ref[:, capacity * chunks].astype(jnp.float32)[:, :capacity]
        first_row = jnp.broadcast_to(labels.reshape(slots, 1, LANES) * rows, (slots, rows, LANES))
        source = first_row + lax.broadcasted_iota(jnp.int32, (slots, rows, LANES), 1).astype(
            jnp.float32
        )
        lane = lax.broadcasted_iota(jnp.int32, (slots, rows, LANES), 2).astype(jnp.float32)
        hot = []
        for c in range(chunks):
            match = jnp.where(source == lane + float(c * LANES), 1.0, 0.0)
            hot.append(match.reshape(slots * rows, LANES).astype(jnp.bfloat16))
        for c in range(chunks):
            for t in range(tile_count):
                for k in range(capacity):
                    row = (t * capacity + k) * rows
                    wide_ref[row : row + rows, :] = arrived_ref[t, k * chunks + c].astype(
                        jnp.float32
                    )
            across = wide_ref[...].T.astype(jnp.bfloat16)
            for d in range(chunks):
                turned_ref[c * LANES : (c + 1) * LANES, d * LANES : (d + 1) * LANES] = jnp.dot(
                    across, hot[d], preferred_element_type=jnp.float32
                ).astype(jnp.bfloat16)

    width = out_ref.shape[1]
    planes = piece // width
    pieces = values_ref.shape[1] // piece
    for q in range(pieces):
        block = values_ref[:, q * piece : (q + 1) * piece]
        mixed = jnp.dot(turned_ref[...], block, preferred_element_type=jnp.float32)
        density = jnp.sum(mixed * block.astype(jnp.float32), axis=0, keepdims=True)
        for p in range(planes):
            out_ref[pl.ds((step * pieces + q) * planes + p, 1), :] = density[
                :, p * width : (p + 1) * width
            ]

    @pl.when(step == pl.num_programs(0) - 1)
    def _():
        low_ref[...] = out_ref[:, : low_ref.shape[1]]
        high_ref[...] = out_ref[:, width - high_ref.shape[1] :]


def join_kernel(own_ref, before_ref, after_ref, out_ref, top_ref, bottom_ref):
    reach = before_ref.shape[1]
    width = own_ref.shape[1]
    out_ref[:, :reach] = before_ref[...]
    out_ref[:, reach : reach + width] = own_ref[...]
    out_ref[:, reach + width :] = after_ref[...]
    top_ref[...] = out_ref[: top_ref.shape[0], :]
    bottom_ref[...] = out_ref[out_ref.shape[0] - bottom_ref.shape[0] :, :]


def split_dot(left, high, low):
    left_high = left.astype(jnp.bfloat16)
    left_low = (left - left_high.astype(jnp.float32)).astype(jnp.bfloat16)
    out = jnp.dot(left_high, high, preferred_element_type=jnp.float32)
    out = out + jnp.dot(left_low, high, preferred_element_type=jnp.float32)
    return out + jnp.dot(left_high, low, preferred_element_type=jnp.float32)


def filter_kernel(parts, *refs):
    taps_ref, band_high, band_low, fold_high, fold_low = refs[:5]
    blocks = refs[5 : 5 + 3 * parts]
    out_ref, field_ref, grid_ref, first_ref, second_ref, third_ref = refs[5 + 3 * parts :]
    size_x, size_y, size_z = out_ref.shape
    wide_y, wide_x, lanes = first_ref.shape
    for part in range(parts):
        start = 0
        for block in blocks[3 * part : 3 * part + 3]:
            rows = block.shape[0]
            for y in range(wide_y):
                grid_ref[y, start : start + rows, part * size_z : (part + 1) * size_z] = block[
                    :, y * size_z : (y + 1) * size_z
                ]
            start += rows
    grid = grid_ref[...].reshape(wide_y * wide_x, parts * size_z)
    first_ref[...] = split_dot(grid, band_high[...], band_low[...]).reshape(wide_y, wide_x, lanes)

    def tap(distance, rows):
        return jnp.broadcast_to(taps_ref[distance : distance + 1, :], (rows, lanes))

    def along_y(y, carry):
        run = tap(0, wide_x) * first_ref[y + RADIUS]
        for d in range(1, RADIUS + 1):
            pair = first_ref[y + (RADIUS - d)] + first_ref[y + (RADIUS + d)]
            run = run + tap(d, wide_x) * pair
        second_ref[y] = run
        return carry

    lax.fori_loop(0, size_y, along_y, 0)

    def along_x(y, carry):
        run = tap(0, size_x) * second_ref[y, RADIUS : RADIUS + size_x, :]
        for d in range(1, RADIUS + 1):
            pair = (
                second_ref[y, RADIUS - d : RADIUS - d + size_x, :]
                + second_ref[y, RADIUS + d : RADIUS + d + size_x, :]
            )
            run = run + tap(d, size_x) * pair
        third_ref[y] = run
        return carry

    lax.fori_loop(0, size_y, along_x, 0)
    filtered = third_ref[...].reshape(size_y * size_x, lanes)
    folded = split_dot(filtered, fold_high[...], fold_low[...]).reshape(size_y, size_x, size_z)
    for y in range(size_y):
        out_ref[:, y, :] = folded[y]
        field_ref[:, y * size_z : (y + 1) * size_z] = folded[y]


def potential_kernel(
    capacity, chunks, rows, weight, place_ref, field_ref, values_ref, out_ref, total_ref
):
    step = pl.program_id(0)
    width = field_ref.shape[1]
    planes = values_ref.shape[1] // width
    list_orb = values_ref.shape[0]
    field = jnp.concatenate(
        [field_ref[pl.ds(step * planes + q, 1), :] for q in range(planes)], axis=1
    )
    block = values_ref[...]
    weighted = (field * block.astype(jnp.float32) * weight).astype(jnp.bfloat16)
    total = lax.dot_general(
        block, weighted, (((1,), (1,)), ((), ())), preferred_element_type=jnp.float32
    )

    @pl.when(step == 0)
    def _():
        total_ref[...] = total

    @pl.when(step > 0)
    def _():
        total_ref[...] += total

    @pl.when(step == pl.num_programs(0) - 1)
    def _():
        last = list_orb // rows - 1

        def visit(j, carry):
            t, k = j // capacity, j % capacity
            row = pl.multiple_of(jnp.minimum(place_ref[j], last) * rows, rows)
            for c in range(chunks):
                out_ref[t, k * chunks + c] = total_ref[
                    pl.ds(row, rows), c * LANES : (c + 1) * LANES
                ].astype(jnp.bfloat16)
            return carry

        lax.fori_loop(0, out_ref.shape[0] * capacity, visit, 0, unroll=4)


def unpack_kernel(chunks, tile_count, tile_ref, back_ref, out_ref, count_ref):
    def visit(i, t, slot):
        for c in range(chunks):
            out_ref[i, :, c * LANES : (c + 1) * LANES] = back_ref[t, slot * chunks + c]

    for_each_slab(tile_ref, count_ref, tile_count, out_ref.shape[0], visit)


def moved(block, shifts):
    axes = tuple(shifts)
    sizes = [lax.axis_size(axis) for axis in axes]
    pairs = []
    for source in np.ndindex(*sizes):
        target = [(s + shifts[axis]) % n for s, axis, n in zip(source, axes, sizes)]
        pairs.append(
            (int(np.ravel_multi_index(source, sizes)), int(np.ravel_multi_index(target, sizes)))
        )
    return lax.ppermute(block, axes, pairs)


def band_tables(size_z, neighbours):
    tap_table, mix = kernel_tables(RADIUS)

    def band(shift):
        table = np.zeros((size_z, len(ALPHAS), size_z), np.float64)
        for m in range(len(ALPHAS)):
            for source in range(size_z):
                for target in range(size_z):
                    offset = source + shift - target
                    if abs(offset) <= RADIUS:
                        table[source, m, target] = tap_table[m][offset + RADIUS]
        return table.reshape(size_z, len(ALPHAS) * size_z)

    own, low, high = band(0), band(-size_z), band(size_z)
    bands = {0: [own + low + high], 1: [own, low + high], 2: [own, low, high]}[neighbours]
    taps = np.zeros((16, len(ALPHAS) * size_z), np.float64)
    for d in range(RADIUS + 1):
        taps[d] = np.repeat([row[RADIUS + d] for row in tap_table], size_z)
    fold = np.concatenate([mix[m] * np.eye(size_z) for m in range(len(ALPHAS))], axis=0)

    def split(table):
        high = table.astype(np.float32).astype(jnp.bfloat16)
        low = (table - high.astype(np.float64)).astype(np.float32).astype(jnp.bfloat16)
        return [high, low]

    return [taps.astype(np.float32), *split(np.concatenate(bands, axis=0)), *split(fold)]


def local(orbital_values, dm_slabs, slab_tile, slab_place):
    size_x, size_y, size_z, list_orb = orbital_values.shape
    slab_count, atom_orb, _ = dm_slabs.shape
    list_blk = list_orb // atom_orb
    tile_count = lax.axis_size("gx") * lax.axis_size("gy")
    capacity = max(2, 2 * ((list_blk + tile_count - 1) // tile_count))
    chunks = list_orb // LANES
    tile_points = size_x * size_y * size_z
    plane = size_y * size_z
    counts = pltpu.SMEM((tile_count,), jnp.int32)

    packed = pl.pallas_call(
        functools.partial(pack_kernel, capacity, chunks, float(list_blk)),
        out_shape=jax.ShapeDtypeStruct(
            (tile_count, capacity * chunks + 1, atom_orb, LANES), jnp.bfloat16
        ),
        in_specs=[SMEM_SPEC, SMEM_SPEC, VMEM_SPEC],
        out_specs=VMEM_SPEC,
        scratch_shapes=[counts, pltpu.VMEM((tile_count, atom_orb, LANES), jnp.float32)],
        compiler_params=grant(4),
        name="pack",
    )(slab_tile, slab_place, dm_slabs)
    arrived = lax.all_to_all(packed, ("gx", "gy"), split_axis=0, concat_axis=0, tiled=True)
    turned = orbital_values.reshape(tile_points, list_orb).T

    steps = 4
    reach = RADIUS * size_z
    slice_spec = pl.BlockSpec((list_orb, tile_points // steps), lambda i: (0, i))
    f32 = lambda *shape: jax.ShapeDtypeStruct(shape, jnp.float32)
    whole = lambda *shape: pl.BlockSpec(shape, lambda i: (0,) * len(shape))
    density, low_y, high_y = pl.pallas_call(
        functools.partial(density_kernel, capacity, chunks, 2 * plane),
        grid=(steps,),
        out_shape=(f32(size_x, plane), f32(size_x, reach), f32(size_x, reach)),
        in_specs=[VMEM_SPEC, slice_spec],
        out_specs=(whole(size_x, plane), whole(size_x, reach), whole(size_x, reach)),
        scratch_shapes=[
            pltpu.VMEM((tile_count * capacity * atom_orb, LANES), jnp.float32),
            pltpu.VMEM((list_orb, list_orb), jnp.bfloat16),
        ],
        compiler_params=grant(20),
        name="density",
    )(arrived, turned)
    places = arrived[:, capacity * chunks, :capacity, 0].astype(jnp.int32).reshape(-1)

    wide = plane + 2 * reach
    own, top, bottom = pl.pallas_call(
        join_kernel,
        out_shape=(f32(size_x, wide), f32(RADIUS, wide), f32(RADIUS, wide)),
        in_specs=[VMEM_SPEC] * 3,
        out_specs=(VMEM_SPEC,) * 3,
        compiler_params=grant(2),
        name="join",
    )(density, moved(high_y, {"gy": 1}), moved(low_y, {"gy": -1}))
    layers = lax.axis_size("gz")
    blocks = []
    for shift in {1: [0], 2: [0, 1]}.get(layers, [0, 1, -1]):
        blocks.append(moved(bottom, {"gx": 1, "gz": shift}))
        blocks.append(moved(own, {"gz": shift}) if shift else own)
        blocks.append(moved(top, {"gx": -1, "gz": shift}))
    parts = len(blocks) // 3
    tables = band_tables(size_z, parts - 1)
    lanes = tables[0].shape[1]
    wide_x, wide_y = size_x + 2 * RADIUS, size_y + 2 * RADIUS
    potential, field = pl.pallas_call(
        functools.partial(filter_kernel, parts),
        out_shape=(f32(size_x, size_y, size_z), f32(size_x, plane)),
        in_specs=[VMEM_SPEC] * (len(tables) + len(blocks)),
        out_specs=(VMEM_SPEC,) * 2,
        scratch_shapes=[
            pltpu.VMEM((wide_y, wide_x, parts * size_z), jnp.float32),
            pltpu.VMEM((wide_y, wide_x, lanes), jnp.float32),
            pltpu.VMEM((size_y, wide_x, lanes), jnp.float32),
            pltpu.VMEM((size_y, size_x, lanes), jnp.float32),
        ],
        compiler_params=grant(12),
        name="filter",
    )(*map(jnp.asarray, tables), *blocks)

    out_shape = (tile_count, capacity * chunks, atom_orb, LANES)
    returned = pl.pallas_call(
        functools.partial(
            potential_kernel, capacity, chunks, atom_orb, float(tile_points) ** (-0.5)
        ),
        grid=(steps,),
        out_shape=jax.ShapeDtypeStruct(out_shape, jnp.bfloat16),
        in_specs=[SMEM_SPEC, whole(size_x, plane), slice_spec],
        out_specs=whole(*out_shape),
        scratch_shapes=[pltpu.VMEM((list_orb, list_orb), jnp.float32)],
        compiler_params=grant(20),
        name="potential",
    )(places, field, turned)
    back = lax.all_to_all(returned, ("gx", "gy"), split_axis=0, concat_axis=0, tiled=True)
    own_rows = pl.pallas_call(
        functools.partial(unpack_kernel, chunks, tile_count),
        out_shape=jax.ShapeDtypeStruct((slab_count, atom_orb, list_orb), jnp.bfloat16),
        in_specs=[SMEM_SPEC, VMEM_SPEC],
        out_specs=VMEM_SPEC,
        scratch_shapes=[counts],
        compiler_params=grant(4),
        name="unpack",
    )(slab_tile, back)
    return (potential, own_rows)


def solution(mesh):
    placed = (
        P("gx", "gy", "gz", None),
        P(("gx", "gy", "gz"), None, None),
        P(("gx", "gy", "gz")),
        P(("gx", "gy", "gz")),
    )
    return jax.shard_map(
        local,
        mesh=mesh,
        in_specs=placed,
        out_specs=(P("gx", "gy", "gz"), P(("gx", "gy", "gz"), None, None)),
        check_vma=False,
    )
```

```python
import functools
import math

import jax
import jax.numpy as jnp
import numpy as np
from jax import lax
from jax.experimental import pallas as pl
from jax.experimental.pallas import tpu as pltpu
from jax.sharding import PartitionSpec as P

RADIUS = 8
LANES = 128

ALPHAS = (0.012, 0.025, 0.05, 0.1, 0.2, 0.4, 0.8, 1.6)
MIXES = (0.3, 0.3, 0.32, 0.34, 0.36, 0.38, 0.4, 0.42)

VMEM_SPEC = pl.BlockSpec(memory_space=pltpu.VMEM)
SMEM_SPEC = pl.BlockSpec(memory_space=pltpu.SMEM)
HBM_SPEC = pl.BlockSpec(memory_space=pltpu.HBM)


def grant(mebibytes):
    return pltpu.CompilerParams(vmem_limit_bytes=mebibytes << 20)


def kernel_tables(radius):
    tap_table = [
        [math.exp(-alpha * offset * offset) for offset in range(-radius, radius + 1)]
        for alpha in ALPHAS
    ]
    mix = [
        MIXES[term] / sum((tap * tap for tap in tap_table[term])) ** 1.5
        for term in range(len(ALPHAS))
    ]
    return (tap_table, mix)


def for_each_slab(tile_ref, count_ref, tile_count, slab_count, visit):
    for t in range(tile_count):
        count_ref[t] = 0

    def step(i, carry):
        t = tile_ref[i]
        slot = count_ref[t]
        count_ref[t] = slot + 1
        visit(i, t, slot)
        return carry

    lax.fori_loop(0, slab_count, step, 0, unroll=4)


def pack_kernel(
    capacity, chunks, empty, tile_hbm, place_hbm, slab_hbm, out_ref,
    tile_ref, place_ref, slab_ref, count_ref, label_ref, sems,
):
    copies = [
        pltpu.make_async_copy(tile_hbm, tile_ref, sems.at[0]),
        pltpu.make_async_copy(place_hbm, place_ref, sems.at[1]),
        pltpu.make_async_copy(slab_hbm, slab_ref, sems.at[2]),
    ]
    for copy in copies:
        copy.start()
    tile_count = out_ref.shape[0]
    label_ref[...] = jnp.full(label_ref.shape, empty, jnp.float32)
    out_ref[...] = jnp.zeros(out_ref.shape, out_ref.dtype)
    for copy in copies:
        copy.wait()

    def visit(i, t, slot):
        slab = slab_ref[i]
        for c in range(chunks):
            out_ref[t, slot * chunks + c] = slab[:, c * LANES : (c + 1) * LANES]
        label = place_ref[i].astype(jnp.float32)
        label_ref[t, pl.ds(slot, 1), :] = jnp.full((1, LANES), label, jnp.float32)

    for_each_slab(tile_ref, count_ref, tile_count, slab_ref.shape[0], visit)
    out_ref[:, capacity * chunks] = label_ref[...].astype(jnp.bfloat16)


def density_kernel(
    capacity, chunks, piece, arrived_ref, values_hbm,
    out_ref, low_ref, high_ref, place_ref, held_ref, wide_ref, turned_ref, sems,
):
    tile_count, _, rows, _ = arrived_ref.shape
    slots = tile_count * capacity
    pieces = held_ref.shape[1] // piece
    copies = []
    for q in range(pieces):
        part = (slice(None), slice(q * piece, (q + 1) * piece))
        copies.append(
            pltpu.make_async_copy(values_hbm.at[part], held_ref.at[part], sems.at[q])
        )
        copies[q].start()

    labels = arrived_ref[:, capacity * chunks].astype(jnp.float32)[:, :capacity]
    labels = labels.reshape(slots, LANES)
    width = place_ref.shape[1]
    for g in range(width // LANES):
        group = labels[g * LANES : (g + 1) * LANES]
        here = lax.broadcasted_iota(jnp.int32, group.shape, 0) == lax.broadcasted_iota(
            jnp.int32, group.shape, 1
        )
        place_ref[:, g * LANES : (g + 1) * LANES] = jnp.sum(
            jnp.where(here, group, 0.0), axis=0, keepdims=True
        ).astype(jnp.int32)
    first_row = jnp.broadcast_to(labels.reshape(slots, 1, LANES) * rows, (slots, rows, LANES))
    source = first_row + lax.broadcasted_iota(jnp.int32, (slots, rows, LANES), 1).astype(
        jnp.float32
    )
    lane = lax.broadcasted_iota(jnp.int32, (slots, rows, LANES), 2).astype(jnp.float32)
    hot = []
    for c in range(chunks):
        match = jnp.where(source == lane + float(c * LANES), 1.0, 0.0)
        hot.append(match.reshape(slots * rows, LANES).astype(jnp.bfloat16))
    hot = jnp.concatenate(hot, axis=1)
    for c in range(chunks):
        for t in range(tile_count):
            for k in range(capacity):
                row = (t * capacity + k) * rows
                wide_ref[row : row + rows, :] = arrived_ref[t, k * chunks + c].astype(jnp.float32)
        across = wide_ref[...].T.astype(jnp.bfloat16)
        turned_ref[c * LANES : (c + 1) * LANES, :] = jnp.dot(
            across, hot, preferred_element_type=jnp.float32
        ).astype(jnp.bfloat16)

    plane = out_ref.shape[1]
    planes = piece // plane
    for q in range(pieces):
        copies[q].wait()
        block = held_ref[:, q * piece : (q + 1) * piece]
        mixed = jnp.dot(turned_ref[...], block, preferred_element_type=jnp.float32)
        density = jnp.sum(mixed * block.astype(jnp.float32), axis=0, keepdims=True)
        for p in range(planes):
            row = q * planes + p
            out_ref[row : row + 1, :] = density[:, p * plane : (p + 1) * plane]
    low_ref[...] = out_ref[:, : low_ref.shape[1]]
    high_ref[...] = out_ref[:, plane - high_ref.shape[1] :]


def join_kernel(own_ref, before_ref, after_ref, out_ref, top_ref, bottom_ref):
    reach = before_ref.shape[1]
    width = own_ref.shape[1]
    out_ref[:, :reach] = before_ref[...]
    out_ref[:, reach : reach + width] = own_ref[...]
    out_ref[:, reach + width :] = after_ref[...]
    top_ref[...] = out_ref[: top_ref.shape[0], :]
    bottom_ref[...] = out_ref[out_ref.shape[0] - bottom_ref.shape[0] :, :]


def split_dot(left, high, low):
    left_high = left.astype(jnp.bfloat16)
    left_low = (left - left_high.astype(jnp.float32)).astype(jnp.bfloat16)
    out = jnp.dot(left_high, high, preferred_element_type=jnp.float32)
    out = out + jnp.dot(left_low, high, preferred_element_type=jnp.float32)
    return out + jnp.dot(left_high, low, preferred_element_type=jnp.float32)


def filter_kernel(parts, *refs):
    taps_ref, band_high, band_low, fold_high, fold_low = refs[:5]
    blocks = refs[5 : 5 + 3 * parts]
    out_ref, field_ref, grid_ref, first_ref, second_ref, third_ref = refs[5 + 3 * parts :]
    size_x, size_y, size_z = out_ref.shape
    wide_y, wide_x, lanes = first_ref.shape
    for part in range(parts):
        start = 0
        for block in blocks[3 * part : 3 * part + 3]:
            rows = block.shape[0]
            for y in range(wide_y):
                grid_ref[y, start : start + rows, part * size_z : (part + 1) * size_z] = block[
                    :, y * size_z : (y + 1) * size_z
                ]
            start += rows
    grid = grid_ref[...].reshape(wide_y * wide_x, parts * size_z)
    first_ref[...] = split_dot(grid, band_high[...], band_low[...]).reshape(wide_y, wide_x, lanes)

    def tap(distance, rows):
        return jnp.broadcast_to(taps_ref[distance : distance + 1, :], (rows, lanes))

    def along_y(y, carry):
        run = tap(0, wide_x) * first_ref[y + RADIUS]
        for d in range(1, RADIUS + 1):
            pair = first_ref[y + (RADIUS - d)] + first_ref[y + (RADIUS + d)]
            run = run + tap(d, wide_x) * pair
        second_ref[y] = run
        return carry

    lax.fori_loop(0, size_y, along_y, 0)

    def along_x(y, carry):
        run = tap(0, size_x) * second_ref[y, RADIUS : RADIUS + size_x, :]
        for d in range(1, RADIUS + 1):
            pair = (
                second_ref[y, RADIUS - d : RADIUS - d + size_x, :]
                + second_ref[y, RADIUS + d : RADIUS + d + size_x, :]
            )
            run = run + tap(d, size_x) * pair
        third_ref[y] = run
        return carry

    lax.fori_loop(0, size_y, along_x, 0)
    filtered = third_ref[...].reshape(size_y * size_x, lanes)
    folded = split_dot(filtered, fold_high[...], fold_low[...]).reshape(size_y, size_x, size_z)
    for y in range(size_y):
        out_ref[:, y, :] = folded[y]
        field_ref[:, y * size_z : (y + 1) * size_z] = folded[y]


def potential_kernel(
    capacity, chunks, rows, weight, steps, place_ref, field_ref, values_ref, out_ref, total_ref
):
    size_x, plane = field_ref.shape
    list_orb, points = values_ref.shape
    piece = points // steps
    planes = piece // plane
    for q in range(steps):
        field = jnp.concatenate(
            [field_ref[q * planes + p : q * planes + p + 1, :] for p in range(planes)], axis=1
        )
        block = values_ref[:, q * piece : (q + 1) * piece]
        weighted = (field * block.astype(jnp.float32) * weight).astype(jnp.bfloat16)
        term = lax.dot_general(
            block, weighted, (((1,), (1,)), ((), ())), preferred_element_type=jnp.float32
        )
        total_ref[...] = term if q == 0 else total_ref[...] + term

    last = list_orb // rows - 1

    def visit(j, carry):
        t, k = j // capacity, j % capacity
        row = pl.multiple_of(jnp.minimum(place_ref[0, j], last) * rows, rows)
        for c in range(chunks):
            out_ref[t, k * chunks + c] = total_ref[
                pl.ds(row, rows), c * LANES : (c + 1) * LANES
            ].astype(jnp.bfloat16)
        return carry

    lax.fori_loop(0, out_ref.shape[0] * capacity, visit, 0, unroll=4)


def unpack_kernel(chunks, tile_count, tile_ref, back_ref, out_ref, count_ref):
    def visit(i, t, slot):
        for c in range(chunks):
            out_ref[i, :, c * LANES : (c + 1) * LANES] = back_ref[t, slot * chunks + c]

    for_each_slab(tile_ref, count_ref, tile_count, out_ref.shape[0], visit)


def moved(block, shifts):
    axes = tuple(shifts)
    sizes = [lax.axis_size(axis) for axis in axes]
    pairs = []
    for source in np.ndindex(*sizes):
        target = [(s + shifts[axis]) % n for s, axis, n in zip(source, axes, sizes)]
        pairs.append(
            (int(np.ravel_multi_index(source, sizes)), int(np.ravel_multi_index(target, sizes)))
        )
    return lax.ppermute(block, axes, pairs)


def band_tables(size_z, neighbours):
    tap_table, mix = kernel_tables(RADIUS)

    def band(shift):
        table = np.zeros((size_z, len(ALPHAS), size_z), np.float64)
        for m in range(len(ALPHAS)):
            for source in range(size_z):
                for target in range(size_z):
                    offset = source + shift - target
                    if abs(offset) <= RADIUS:
                        table[source, m, target] = tap_table[m][offset + RADIUS]
        return table.reshape(size_z, len(ALPHAS) * size_z)

    own, low, high = band(0), band(-size_z), band(size_z)
    bands = {0: [own + low + high], 1: [own, low + high], 2: [own, low, high]}[neighbours]
    taps = np.zeros((16, len(ALPHAS) * size_z), np.float64)
    for d in range(RADIUS + 1):
        taps[d] = np.repeat([row[RADIUS + d] for row in tap_table], size_z)
    fold = np.concatenate([mix[m] * np.eye(size_z) for m in range(len(ALPHAS))], axis=0)

    def split(table):
        high = table.astype(np.float32).astype(jnp.bfloat16)
        low = (table - high.astype(np.float64)).astype(np.float32).astype(jnp.bfloat16)
        return [high, low]

    return [taps.astype(np.float32), *split(np.concatenate(bands, axis=0)), *split(fold)]


def local(orbital_values, dm_slabs, slab_tile, slab_place):
    size_x, size_y, size_z, list_orb = orbital_values.shape
    slab_count, atom_orb, _ = dm_slabs.shape
    list_blk = list_orb // atom_orb
    tile_count = lax.axis_size("gx") * lax.axis_size("gy")
    capacity = max(2, 2 * ((list_blk + tile_count - 1) // tile_count))
    chunks = list_orb // LANES
    tile_points = size_x * size_y * size_z
    plane = size_y * size_z
    counts = pltpu.SMEM((tile_count,), jnp.int32)

    packed = pl.pallas_call(
        functools.partial(pack_kernel, capacity, chunks, float(list_blk)),
        out_shape=jax.ShapeDtypeStruct(
            (tile_count, capacity * chunks + 1, atom_orb, LANES), jnp.bfloat16
        ),
        in_specs=[HBM_SPEC] * 3,
        out_specs=VMEM_SPEC,
        scratch_shapes=[
            pltpu.SMEM((slab_count,), jnp.int32),
            pltpu.SMEM((slab_count,), jnp.int32),
            pltpu.VMEM(dm_slabs.shape, dm_slabs.dtype),
            counts,
            pltpu.VMEM((tile_count, atom_orb, LANES), jnp.float32),
            pltpu.SemaphoreType.DMA((3,)),
        ],
        compiler_params=grant(60),
        name="pack",
    )(slab_tile, slab_place, dm_slabs)
    arrived = lax.all_to_all(packed, ("gx", "gy"), split_axis=0, concat_axis=0, tiled=True)
    turned = orbital_values.reshape(tile_points, list_orb).T

    reach = RADIUS * size_z
    piece = 2 * plane
    slots = LANES * ((tile_count * capacity + LANES - 1) // LANES)
    f32 = lambda *shape: jax.ShapeDtypeStruct(shape, jnp.float32)
    density, low_y, high_y, places, held = pl.pallas_call(
        functools.partial(density_kernel, capacity, chunks, piece),
        out_shape=(
            f32(size_x, plane),
            f32(size_x, reach),
            f32(size_x, reach),
            jax.ShapeDtypeStruct((1, slots), jnp.int32),
            pltpu.VMEM((list_orb, tile_points), jnp.bfloat16),
        ),
        in_specs=[VMEM_SPEC, HBM_SPEC],
        out_specs=(VMEM_SPEC,) * 5,
        scratch_shapes=[
            pltpu.VMEM((tile_count * capacity * atom_orb, LANES), jnp.float32),
            pltpu.VMEM((list_orb, list_orb), jnp.bfloat16),
            pltpu.SemaphoreType.DMA((tile_points // piece,)),
        ],
        compiler_params=grant(57),
        name="density",
    )(arrived, turned)

    wide = plane + 2 * reach
    own, top, bottom = pl.pallas_call(
        join_kernel,
        out_shape=(f32(size_x, wide), f32(RADIUS, wide), f32(RADIUS, wide)),
        in_specs=[VMEM_SPEC] * 3,
        out_specs=(VMEM_SPEC,) * 3,
        compiler_params=grant(2),
        name="join",
    )(density, moved(high_y, {"gy": 1}), moved(low_y, {"gy": -1}))
    layers = lax.axis_size("gz")
    blocks = []
    for shift in {1: [0], 2: [0, 1]}.get(layers, [0, 1, -1]):
        blocks.append(moved(bottom, {"gx": 1, "gz": shift}))
        blocks.append(moved(own, {"gz": shift}) if shift else own)
        blocks.append(moved(top, {"gx": -1, "gz": shift}))
    parts = len(blocks) // 3
    tables = band_tables(size_z, parts - 1)
    lanes = tables[0].shape[1]
    wide_x, wide_y = size_x + 2 * RADIUS, size_y + 2 * RADIUS
    potential, field = pl.pallas_call(
        functools.partial(filter_kernel, parts),
        out_shape=(f32(size_x, size_y, size_z), f32(size_x, plane)),
        in_specs=[VMEM_SPEC] * (len(tables) + len(blocks)),
        out_specs=(VMEM_SPEC,) * 2,
        scratch_shapes=[
            pltpu.VMEM((wide_y, wide_x, parts * size_z), jnp.float32),
            pltpu.VMEM((wide_y, wide_x, lanes), jnp.float32),
            pltpu.VMEM((size_y, wide_x, lanes), jnp.float32),
            pltpu.VMEM((size_y, size_x, lanes), jnp.float32),
        ],
        compiler_params=grant(12),
        name="filter",
    )(*map(jnp.asarray, tables), *blocks)

    returned = pl.pallas_call(
        functools.partial(
            potential_kernel, capacity, chunks, atom_orb, float(tile_points) ** (-0.5), 4
        ),
        out_shape=jax.ShapeDtypeStruct(
            (tile_count, capacity * chunks, atom_orb, LANES), jnp.bfloat16
        ),
        in_specs=[SMEM_SPEC, VMEM_SPEC, VMEM_SPEC],
        out_specs=VMEM_SPEC,
        scratch_shapes=[pltpu.VMEM((list_orb, list_orb), jnp.float32)],
        compiler_params=grant(20),
        name="potential",
    )(places, field, held)
    back = lax.all_to_all(returned, ("gx", "gy"), split_axis=0, concat_axis=0, tiled=True)
    own_rows = pl.pallas_call(
        functools.partial(unpack_kernel, chunks, tile_count),
        out_shape=jax.ShapeDtypeStruct((slab_count, atom_orb, list_orb), jnp.bfloat16),
        in_specs=[SMEM_SPEC, VMEM_SPEC],
        out_specs=VMEM_SPEC,
        scratch_shapes=[counts],
        compiler_params=grant(4),
        name="unpack",
    )(slab_tile, back)
    return (potential, own_rows)


def solution(mesh):
    placed = (
        P("gx", "gy", "gz", None),
        P(("gx", "gy", "gz"), None, None),
        P(("gx", "gy", "gz")),
        P(("gx", "gy", "gz")),
    )
    return jax.shard_map(
        local,
        mesh=mesh,
        in_specs=placed,
        out_specs=(P("gx", "gy", "gz"), P(("gx", "gy", "gz"), None, None)),
        check_vma=False,
    )
```

```python
import functools
import math

import jax
import jax.numpy as jnp
import numpy as np
from jax import lax
from jax.experimental import pallas as pl
from jax.experimental.pallas import tpu as pltpu
from jax.sharding import PartitionSpec as P

RADIUS = 8
LANES = 128

ALPHAS = (0.012, 0.025, 0.05, 0.1, 0.2, 0.4, 0.8, 1.6)
MIXES = (0.3, 0.3, 0.32, 0.34, 0.36, 0.38, 0.4, 0.42)

VMEM_SPEC = pl.BlockSpec(memory_space=pltpu.VMEM)
SMEM_SPEC = pl.BlockSpec(memory_space=pltpu.SMEM)
HBM_SPEC = pl.BlockSpec(memory_space=pltpu.HBM)


def in_hbm(array):
    return pltpu.with_memory_space_constraint(array, pltpu.HBM)


def grant(mebibytes):
    return pltpu.CompilerParams(vmem_limit_bytes=mebibytes << 20)


def kernel_tables(radius):
    tap_table = [
        [math.exp(-alpha * offset * offset) for offset in range(-radius, radius + 1)]
        for alpha in ALPHAS
    ]
    mix = [
        MIXES[term] / sum((tap * tap for tap in tap_table[term])) ** 1.5
        for term in range(len(ALPHAS))
    ]
    return (tap_table, mix)


def for_each_slab(tile_ref, count_ref, tile_count, slab_count, visit):
    for t in range(tile_count):
        count_ref[t] = 0

    def step(i, carry):
        t = tile_ref[i]
        slot = count_ref[t]
        count_ref[t] = slot + 1
        visit(i, t, slot)
        return carry

    lax.fori_loop(0, slab_count, step, 0, unroll=4)


def pack_kernel(
    capacity, chunks, empty, tile_hbm, place_hbm, slab_hbm, out_ref,
    tile_ref, place_ref, slab_ref, count_ref, label_ref, sems,
):
    copies = [
        pltpu.make_async_copy(tile_hbm, tile_ref, sems.at[0]),
        pltpu.make_async_copy(place_hbm, place_ref, sems.at[1]),
        pltpu.make_async_copy(slab_hbm, slab_ref, sems.at[2]),
    ]
    for copy in copies:
        copy.start()
    tile_count = out_ref.shape[0]
    label_ref[...] = jnp.full(label_ref.shape, empty, jnp.float32)
    out_ref[...] = jnp.zeros(out_ref.shape, out_ref.dtype)
    for copy in copies:
        copy.wait()

    def visit(i, t, slot):
        slab = slab_ref[i]
        for c in range(chunks):
            out_ref[t, slot * chunks + c] = slab[:, c * LANES : (c + 1) * LANES]
        label = place_ref[i].astype(jnp.float32)
        label_ref[t, pl.ds(slot, 1), :] = jnp.full((1, LANES), label, jnp.float32)

    for_each_slab(tile_ref, count_ref, tile_count, slab_ref.shape[0], visit)
    out_ref[:, capacity * chunks] = label_ref[...].astype(jnp.bfloat16)


def density_kernel(
    capacity, chunks, piece, arrived_ref, values_hbm,
    out_ref, low_ref, high_ref, place_ref, held_ref, wide_ref, turned_ref, sems,
):
    tile_count, _, rows, _ = arrived_ref.shape
    slots = tile_count * capacity
    pieces = held_ref.shape[1] // piece
    copies = []
    for q in range(pieces):
        part = (slice(None), slice(q * piece, (q + 1) * piece))
        copies.append(
            pltpu.make_async_copy(values_hbm.at[part], held_ref.at[part], sems.at[q])
        )
        copies[q].start()

    labels = arrived_ref[:, capacity * chunks].astype(jnp.float32)[:, :capacity]
    labels = labels.reshape(slots, LANES)
    width = place_ref.shape[1]
    for g in range(width // LANES):
        group = labels[g * LANES : (g + 1) * LANES]
        here = lax.broadcasted_iota(jnp.int32, group.shape, 0) == lax.broadcasted_iota(
            jnp.int32, group.shape, 1
        )
        place_ref[:, g * LANES : (g + 1) * LANES] = jnp.sum(
            jnp.where(here, group, 0.0), axis=0, keepdims=True
        ).astype(jnp.int32)
    first_row = jnp.broadcast_to(labels.reshape(slots, 1, LANES) * rows, (slots, rows, LANES))
    source = first_row + lax.broadcasted_iota(jnp.int32, (slots, rows, LANES), 1).astype(
        jnp.float32
    )
    lane = lax.broadcasted_iota(jnp.int32, (slots, rows, LANES), 2).astype(jnp.float32)
    hot = []
    for c in range(chunks):
        match = jnp.where(source == lane + float(c * LANES), 1.0, 0.0)
        hot.append(match.reshape(slots * rows, LANES).astype(jnp.bfloat16))
    hot = jnp.concatenate(hot, axis=1)
    for c in range(chunks):
        for t in range(tile_count):
            for k in range(capacity):
                row = (t * capacity + k) * rows
                wide_ref[row : row + rows, :] = arrived_ref[t, k * chunks + c].astype(jnp.float32)
        across = wide_ref[...].T.astype(jnp.bfloat16)
        turned_ref[c * LANES : (c + 1) * LANES, :] = jnp.dot(
            across, hot, preferred_element_type=jnp.float32
        ).astype(jnp.bfloat16)

    plane = out_ref.shape[1]
    planes = piece // plane
    for q in range(pieces):
        copies[q].wait()
        block = held_ref[:, q * piece : (q + 1) * piece]
        mixed = jnp.dot(turned_ref[...], block, preferred_element_type=jnp.float32)
        density = jnp.sum(mixed * block.astype(jnp.float32), axis=0, keepdims=True)
        for p in range(planes):
            row = q * planes + p
            out_ref[row : row + 1, :] = density[:, p * plane : (p + 1) * plane]
    low_ref[...] = out_ref[:, : low_ref.shape[1]]
    high_ref[...] = out_ref[:, plane - high_ref.shape[1] :]


def join_kernel(own_ref, before_ref, after_ref, out_ref, top_ref, bottom_ref):
    reach = before_ref.shape[1]
    width = own_ref.shape[1]
    out_ref[:, :reach] = before_ref[...]
    out_ref[:, reach : reach + width] = own_ref[...]
    out_ref[:, reach + width :] = after_ref[...]
    top_ref[...] = out_ref[: top_ref.shape[0], :]
    bottom_ref[...] = out_ref[out_ref.shape[0] - bottom_ref.shape[0] :, :]


def split_dot(left, high, low):
    left_high = left.astype(jnp.bfloat16)
    left_low = (left - left_high.astype(jnp.float32)).astype(jnp.bfloat16)
    out = jnp.dot(left_high, high, preferred_element_type=jnp.float32)
    out = out + jnp.dot(left_low, high, preferred_element_type=jnp.float32)
    return out + jnp.dot(left_high, low, preferred_element_type=jnp.float32)


def filter_kernel(parts, *refs):
    taps_ref, band_high, band_low, fold_high, fold_low = refs[:5]
    blocks = refs[5 : 5 + 3 * parts]
    out_ref, field_ref, grid_ref, first_ref, second_ref, third_ref = refs[5 + 3 * parts :]
    size_x, size_y, size_z = out_ref.shape
    wide_y, wide_x, lanes = first_ref.shape
    for part in range(parts):
        start = 0
        for block in blocks[3 * part : 3 * part + 3]:
            rows = block.shape[0]
            for y in range(wide_y):
                grid_ref[y, start : start + rows, part * size_z : (part + 1) * size_z] = block[
                    :, y * size_z : (y + 1) * size_z
                ]
            start += rows
    grid = grid_ref[...].reshape(wide_y * wide_x, parts * size_z)
    first_ref[...] = split_dot(grid, band_high[...], band_low[...]).reshape(wide_y, wide_x, lanes)

    def tap(distance, rows):
        return jnp.broadcast_to(taps_ref[distance : distance + 1, :], (rows, lanes))

    def along_y(y, carry):
        run = tap(0, wide_x) * first_ref[y + RADIUS]
        for d in range(1, RADIUS + 1):
            pair = first_ref[y + (RADIUS - d)] + first_ref[y + (RADIUS + d)]
            run = run + tap(d, wide_x) * pair
        second_ref[y] = run
        return carry

    lax.fori_loop(0, size_y, along_y, 0)

    def along_x(y, carry):
        run = tap(0, size_x) * second_ref[y, RADIUS : RADIUS + size_x, :]
        for d in range(1, RADIUS + 1):
            pair = (
                second_ref[y, RADIUS - d : RADIUS - d + size_x, :]
                + second_ref[y, RADIUS + d : RADIUS + d + size_x, :]
            )
            run = run + tap(d, size_x) * pair
        third_ref[y] = run
        return carry

    lax.fori_loop(0, size_y, along_x, 0)
    filtered = third_ref[...].reshape(size_y * size_x, lanes)
    folded = split_dot(filtered, fold_high[...], fold_low[...]).reshape(size_y, size_x, size_z)
    for y in range(size_y):
        out_ref[:, y, :] = folded[y]
        field_ref[:, y * size_z : (y + 1) * size_z] = folded[y]


def potential_kernel(
    capacity, chunks, rows, weight, steps, place_ref, field_ref, values_ref, out_ref, total_ref
):
    size_x, plane = field_ref.shape
    list_orb, points = values_ref.shape
    piece = points // steps
    planes = piece // plane
    for q in range(steps):
        field = jnp.concatenate(
            [field_ref[q * planes + p : q * planes + p + 1, :] for p in range(planes)], axis=1
        )
        block = values_ref[:, q * piece : (q + 1) * piece]
        weighted = (field * block.astype(jnp.float32) * weight).astype(jnp.bfloat16)
        term = lax.dot_general(
            block, weighted, (((1,), (1,)), ((), ())), preferred_element_type=jnp.float32
        )
        total_ref[...] = term if q == 0 else total_ref[...] + term

    last = list_orb // rows - 1

    def visit(j, carry):
        t, k = j // capacity, j % capacity
        row = pl.multiple_of(jnp.minimum(place_ref[0, j], last) * rows, rows)
        for c in range(chunks):
            out_ref[t, k * chunks + c] = total_ref[
                pl.ds(row, rows), c * LANES : (c + 1) * LANES
            ].astype(jnp.bfloat16)
        return carry

    lax.fori_loop(0, out_ref.shape[0] * capacity, visit, 0, unroll=4)


def unpack_kernel(chunks, tile_count, tile_ref, back_ref, out_ref, count_ref):
    def visit(i, t, slot):
        for c in range(chunks):
            out_ref[i, :, c * LANES : (c + 1) * LANES] = back_ref[t, slot * chunks + c]

    for_each_slab(tile_ref, count_ref, tile_count, out_ref.shape[0], visit)


def moved(block, shifts):
    axes = tuple(shifts)
    sizes = [lax.axis_size(axis) for axis in axes]
    pairs = []
    for source in np.ndindex(*sizes):
        target = [(s + shifts[axis]) % n for s, axis, n in zip(source, axes, sizes)]
        pairs.append(
            (int(np.ravel_multi_index(source, sizes)), int(np.ravel_multi_index(target, sizes)))
        )
    return lax.ppermute(block, axes, pairs)


def band_tables(size_z, neighbours):
    tap_table, mix = kernel_tables(RADIUS)

    def band(shift):
        table = np.zeros((size_z, len(ALPHAS), size_z), np.float64)
        for m in range(len(ALPHAS)):
            for source in range(size_z):
                for target in range(size_z):
                    offset = source + shift - target
                    if abs(offset) <= RADIUS:
                        table[source, m, target] = tap_table[m][offset + RADIUS]
        return table.reshape(size_z, len(ALPHAS) * size_z)

    own, low, high = band(0), band(-size_z), band(size_z)
    bands = {0: [own + low + high], 1: [own, low + high], 2: [own, low, high]}[neighbours]
    taps = np.zeros((16, len(ALPHAS) * size_z), np.float64)
    for d in range(RADIUS + 1):
        taps[d] = np.repeat([row[RADIUS + d] for row in tap_table], size_z)
    fold = np.concatenate([mix[m] * np.eye(size_z) for m in range(len(ALPHAS))], axis=0)

    def split(table):
        high = table.astype(np.float32).astype(jnp.bfloat16)
        low = (table - high.astype(np.float64)).astype(np.float32).astype(jnp.bfloat16)
        return [high, low]

    return [taps.astype(np.float32), *split(np.concatenate(bands, axis=0)), *split(fold)]


def local(orbital_values, dm_slabs, slab_tile, slab_place):
    size_x, size_y, size_z, list_orb = orbital_values.shape
    slab_count, atom_orb, _ = dm_slabs.shape
    list_blk = list_orb // atom_orb
    tile_count = lax.axis_size("gx") * lax.axis_size("gy")
    capacity = max(2, 2 * ((list_blk + tile_count - 1) // tile_count))
    chunks = list_orb // LANES
    tile_points = size_x * size_y * size_z
    plane = size_y * size_z
    counts = pltpu.SMEM((tile_count,), jnp.int32)

    packed = pl.pallas_call(
        functools.partial(pack_kernel, capacity, chunks, float(list_blk)),
        out_shape=jax.ShapeDtypeStruct(
            (tile_count, capacity * chunks + 1, atom_orb, LANES), jnp.bfloat16
        ),
        in_specs=[HBM_SPEC] * 3,
        out_specs=VMEM_SPEC,
        scratch_shapes=[
            pltpu.SMEM((slab_count,), jnp.int32),
            pltpu.SMEM((slab_count,), jnp.int32),
            pltpu.VMEM(dm_slabs.shape, dm_slabs.dtype),
            counts,
            pltpu.VMEM((tile_count, atom_orb, LANES), jnp.float32),
            pltpu.SemaphoreType.DMA((3,)),
        ],
        compiler_params=grant(4),
        name="pack",
    )(in_hbm(slab_tile), in_hbm(slab_place), in_hbm(dm_slabs))
    arrived = lax.all_to_all(packed, ("gx", "gy"), split_axis=0, concat_axis=0, tiled=True)
    turned = orbital_values.reshape(tile_points, list_orb).T

    reach = RADIUS * size_z
    piece = 2 * plane
    slots = LANES * ((tile_count * capacity + LANES - 1) // LANES)
    f32 = lambda *shape: jax.ShapeDtypeStruct(shape, jnp.float32)
    density, low_y, high_y, places, held = pl.pallas_call(
        functools.partial(density_kernel, capacity, chunks, piece),
        out_shape=(
            f32(size_x, plane),
            f32(size_x, reach),
            f32(size_x, reach),
            jax.ShapeDtypeStruct((1, slots), jnp.int32),
            pltpu.VMEM((list_orb, tile_points), jnp.bfloat16),
        ),
        in_specs=[VMEM_SPEC, HBM_SPEC],
        out_specs=(VMEM_SPEC,) * 5,
        scratch_shapes=[
            pltpu.VMEM((tile_count * capacity * atom_orb, LANES), jnp.float32),
            pltpu.VMEM((list_orb, list_orb), jnp.bfloat16),
            pltpu.SemaphoreType.DMA((tile_points // piece,)),
        ],
        compiler_params=grant(24),
        name="density",
    )(arrived, in_hbm(turned))

    wide = plane + 2 * reach
    own, top, bottom = pl.pallas_call(
        join_kernel,
        out_shape=(f32(size_x, wide), f32(RADIUS, wide), f32(RADIUS, wide)),
        in_specs=[VMEM_SPEC] * 3,
        out_specs=(VMEM_SPEC,) * 3,
        compiler_params=grant(2),
        name="join",
    )(density, moved(high_y, {"gy": 1}), moved(low_y, {"gy": -1}))
    layers = lax.axis_size("gz")
    blocks = []
    for shift in {1: [0], 2: [0, 1]}.get(layers, [0, 1, -1]):
        blocks.append(moved(bottom, {"gx": 1, "gz": shift}))
        blocks.append(moved(own, {"gz": shift}) if shift else own)
        blocks.append(moved(top, {"gx": -1, "gz": shift}))
    parts = len(blocks) // 3
    tables = band_tables(size_z, parts - 1)
    lanes = tables[0].shape[1]
    wide_x, wide_y = size_x + 2 * RADIUS, size_y + 2 * RADIUS
    potential, field = pl.pallas_call(
        functools.partial(filter_kernel, parts),
        out_shape=(f32(size_x, size_y, size_z), f32(size_x, plane)),
        in_specs=[VMEM_SPEC] * (len(tables) + len(blocks)),
        out_specs=(VMEM_SPEC,) * 2,
        scratch_shapes=[
            pltpu.VMEM((wide_y, wide_x, parts * size_z), jnp.float32),
            pltpu.VMEM((wide_y, wide_x, lanes), jnp.float32),
            pltpu.VMEM((size_y, wide_x, lanes), jnp.float32),
            pltpu.VMEM((size_y, size_x, lanes), jnp.float32),
        ],
        compiler_params=grant(12),
        name="filter",
    )(*map(jnp.asarray, tables), *blocks)

    returned = pl.pallas_call(
        functools.partial(
            potential_kernel, capacity, chunks, atom_orb, float(tile_points) ** (-0.5), 4
        ),
        out_shape=jax.ShapeDtypeStruct(
            (tile_count, capacity * chunks, atom_orb, LANES), jnp.bfloat16
        ),
        in_specs=[SMEM_SPEC, VMEM_SPEC, VMEM_SPEC],
        out_specs=VMEM_SPEC,
        scratch_shapes=[pltpu.VMEM((list_orb, list_orb), jnp.float32)],
        compiler_params=grant(20),
        name="potential",
    )(places, field, held)
    back = lax.all_to_all(returned, ("gx", "gy"), split_axis=0, concat_axis=0, tiled=True)
    own_rows = pl.pallas_call(
        functools.partial(unpack_kernel, chunks, tile_count),
        out_shape=jax.ShapeDtypeStruct((slab_count, atom_orb, list_orb), jnp.bfloat16),
        in_specs=[SMEM_SPEC, VMEM_SPEC],
        out_specs=VMEM_SPEC,
        scratch_shapes=[counts],
        compiler_params=grant(4),
        name="unpack",
    )(slab_tile, back)
    return (potential, own_rows)


def solution(mesh):
    placed = (
        P("gx", "gy", "gz", None),
        P(("gx", "gy", "gz"), None, None),
        P(("gx", "gy", "gz")),
        P(("gx", "gy", "gz")),
    )
    return jax.shard_map(
        local,
        mesh=mesh,
        in_specs=placed,
        out_specs=(P("gx", "gy", "gz"), P(("gx", "gy", "gz"), None, None)),
        check_vma=False,
    )
```

```python
import functools
import math

import jax
import jax.numpy as jnp
import numpy as np
from jax import lax
from jax.experimental import pallas as pl
from jax.experimental.pallas import tpu as pltpu
from jax.sharding import PartitionSpec as P

RADIUS = 8
LANES = 128

ALPHAS = (0.012, 0.025, 0.05, 0.1, 0.2, 0.4, 0.8, 1.6)
MIXES = (0.3, 0.3, 0.32, 0.34, 0.36, 0.38, 0.4, 0.42)

VMEM_SPEC = pl.BlockSpec(memory_space=pltpu.VMEM)
SMEM_SPEC = pl.BlockSpec(memory_space=pltpu.SMEM)
HBM_SPEC = pl.BlockSpec(memory_space=pltpu.HBM)


def in_hbm(array):
    return pltpu.with_memory_space_constraint(array, pltpu.HBM)


def grant(mebibytes):
    return pltpu.CompilerParams(vmem_limit_bytes=mebibytes << 20)


def kernel_tables(radius):
    tap_table = [
        [math.exp(-alpha * offset * offset) for offset in range(-radius, radius + 1)]
        for alpha in ALPHAS
    ]
    mix = [
        MIXES[term] / sum((tap * tap for tap in tap_table[term])) ** 1.5
        for term in range(len(ALPHAS))
    ]
    return (tap_table, mix)


def cost(flops, moved_bytes):
    return pl.CostEstimate(flops=flops, bytes_accessed=moved_bytes, transcendentals=0)


def for_each_slab(tile_ref, count_ref, tile_count, slab_count, visit):
    for t in range(tile_count):
        count_ref[t] = 0

    def step(i, carry):
        t = tile_ref[i]
        slot = count_ref[t]
        count_ref[t] = slot + 1
        visit(i, t, slot)
        return carry

    lax.fori_loop(0, slab_count, step, 0, unroll=4)


def pack_kernel(
    capacity, chunks, empty, tile_hbm, place_hbm, slab_hbm, out_ref,
    tile_ref, place_ref, slab_ref, count_ref, label_ref, sems,
):
    copies = [
        pltpu.make_async_copy(tile_hbm, tile_ref, sems.at[0]),
        pltpu.make_async_copy(place_hbm, place_ref, sems.at[1]),
        pltpu.make_async_copy(slab_hbm, slab_ref, sems.at[2]),
    ]
    for copy in copies:
        copy.start()
    tile_count = out_ref.shape[0]
    label_ref[...] = jnp.full(label_ref.shape, empty, jnp.float32)
    out_ref[...] = jnp.zeros(out_ref.shape, out_ref.dtype)
    for copy in copies:
        copy.wait()

    def visit(i, t, slot):
        slab = slab_ref[i]
        for c in range(chunks):
            out_ref[t, slot * chunks + c] = slab[:, c * LANES : (c + 1) * LANES]
        label = place_ref[i].astype(jnp.float32)
        label_ref[t, pl.ds(slot, 1), :] = jnp.full((1, LANES), label, jnp.float32)

    for_each_slab(tile_ref, count_ref, tile_count, slab_ref.shape[0], visit)
    out_ref[:, capacity * chunks] = label_ref[...].astype(jnp.bfloat16)


def turn_kernel(planes, values_hbm, near_ref, far_hbm, values_ref, far_ref, sems, out_sem):
    points = values_ref.shape[0]
    plane = points // planes
    half = plane // 2
    copies = []
    for x in range(0, planes, 2):
        part = slice(x * plane, (x + 2) * plane)
        copies.append(
            pltpu.make_async_copy(values_hbm.at[part], values_ref.at[part], sems.at[x // 2])
        )
        copies[-1].start()
    for x in range(0, planes, 2):
        copies[x // 2].wait()
        for side, out_ref in enumerate((near_ref, far_ref)):
            rows = [
                values_ref[(x + i) * plane + side * half : (x + i) * plane + (side + 1) * half, :]
                for i in range(2)
            ]
            out_ref[:, x * half : (x + 2) * half] = jnp.concatenate(rows, axis=0).T
    copy = pltpu.make_async_copy(far_ref, far_hbm, out_sem.at[0])
    copy.start()
    copy.wait()


def arrange(capacity, chunks, arrived_ref, place_ref, wide_ref, turned_ref):
    tile_count, _, rows, _ = arrived_ref.shape
    slots = tile_count * capacity
    labels = arrived_ref[:, capacity * chunks].astype(jnp.float32)[:, :capacity]
    labels = labels.reshape(slots, LANES)
    width = place_ref.shape[1]
    for g in range(width // LANES):
        group = labels[g * LANES : (g + 1) * LANES]
        here = lax.broadcasted_iota(jnp.int32, group.shape, 0) == lax.broadcasted_iota(
            jnp.int32, group.shape, 1
        )
        place_ref[:, g * LANES : (g + 1) * LANES] = jnp.sum(
            jnp.where(here, group, 0.0), axis=0, keepdims=True
        ).astype(jnp.int32)
    first_row = jnp.broadcast_to(labels.reshape(slots, 1, LANES) * rows, (slots, rows, LANES))
    source = first_row + lax.broadcasted_iota(jnp.int32, (slots, rows, LANES), 1).astype(
        jnp.float32
    )
    lane = lax.broadcasted_iota(jnp.int32, (slots, rows, LANES), 2).astype(jnp.float32)
    hot = []
    for c in range(chunks):
        match = jnp.where(source == lane + float(c * LANES), 1.0, 0.0)
        hot.append(match.reshape(slots * rows, LANES).astype(jnp.bfloat16))
    hot = jnp.concatenate(hot, axis=1)
    for c in range(chunks):
        for t in range(tile_count):
            for k in range(capacity):
                row = (t * capacity + k) * rows
                wide_ref[row : row + rows, :] = arrived_ref[t, k * chunks + c].astype(jnp.float32)
        across = wide_ref[...].T.astype(jnp.bfloat16)
        turned_ref[c * LANES : (c + 1) * LANES, :] = jnp.dot(
            across, hot, preferred_element_type=jnp.float32
        ).astype(jnp.bfloat16)


def half_density(piece, turned_ref, values_ref, out_ref):
    half = out_ref.shape[1]
    for q in range(values_ref.shape[1] // piece):
        block = values_ref[:, q * piece : (q + 1) * piece]
        mixed = jnp.dot(turned_ref[...], block, preferred_element_type=jnp.float32)
        density = jnp.sum(mixed * block.astype(jnp.float32), axis=0, keepdims=True)
        for p in range(piece // half):
            row = q * (piece // half) + p
            out_ref[row : row + 1, :] = density[:, p * half : (p + 1) * half]


def near_kernel(
    capacity, chunks, piece, arrived_ref, near_ref, far_hbm,
    out_ref, place_ref, turned_ref, far_ref, wide_ref, sem,
):
    copy = pltpu.make_async_copy(far_hbm, far_ref, sem.at[0])
    copy.start()
    arrange(capacity, chunks, arrived_ref, place_ref, wide_ref, turned_ref)
    half_density(piece, turned_ref, near_ref, out_ref)
    copy.wait()


def far_kernel(piece, turned_ref, far_ref, out_ref):
    half_density(piece, turned_ref, far_ref, out_ref)


def join_kernel(before_ref, low_ref, high_ref, after_ref, out_ref, top_ref, bottom_ref):
    half = low_ref.shape[1]
    for i, ref in enumerate((before_ref, low_ref, high_ref, after_ref)):
        out_ref[:, i * half : (i + 1) * half] = ref[...]
    top_ref[...] = out_ref[: top_ref.shape[0], :]
    bottom_ref[...] = out_ref[out_ref.shape[0] - bottom_ref.shape[0] :, :]


def split_dot(left, high, low):
    left_high = left.astype(jnp.bfloat16)
    left_low = (left - left_high.astype(jnp.float32)).astype(jnp.bfloat16)
    out = jnp.dot(left_high, high, preferred_element_type=jnp.float32)
    out = out + jnp.dot(left_low, high, preferred_element_type=jnp.float32)
    return out + jnp.dot(left_high, low, preferred_element_type=jnp.float32)


def filter_kernel(parts, *refs):
    taps_ref, band_high, band_low, fold_high, fold_low = refs[:5]
    blocks = refs[5 : 5 + 3 * parts]
    out_ref, field_ref, grid_ref, first_ref, second_ref, third_ref = refs[5 + 3 * parts :]
    size_x, size_y, size_z = out_ref.shape
    wide_y, wide_x, lanes = first_ref.shape
    for part in range(parts):
        start = 0
        for block in blocks[3 * part : 3 * part + 3]:
            rows = block.shape[0]
            for y in range(wide_y):
                grid_ref[y, start : start + rows, part * size_z : (part + 1) * size_z] = block[
                    :, y * size_z : (y + 1) * size_z
                ]
            start += rows
    grid = grid_ref[...].reshape(wide_y * wide_x, parts * size_z)
    first_ref[...] = split_dot(grid, band_high[...], band_low[...]).reshape(wide_y, wide_x, lanes)

    def tap(distance, rows):
        return jnp.broadcast_to(taps_ref[distance : distance + 1, :], (rows, lanes))

    def along_y(y, carry):
        run = tap(0, wide_x) * first_ref[y + RADIUS]
        for d in range(1, RADIUS + 1):
            pair = first_ref[y + (RADIUS - d)] + first_ref[y + (RADIUS + d)]
            run = run + tap(d, wide_x) * pair
        second_ref[y] = run
        return carry

    lax.fori_loop(0, size_y, along_y, 0)

    def along_x(y, carry):
        run = tap(0, size_x) * second_ref[y, RADIUS : RADIUS + size_x, :]
        for d in range(1, RADIUS + 1):
            pair = (
                second_ref[y, RADIUS - d : RADIUS - d + size_x, :]
                + second_ref[y, RADIUS + d : RADIUS + d + size_x, :]
            )
            run = run + tap(d, size_x) * pair
        third_ref[y] = run
        return carry

    lax.fori_loop(0, size_y, along_x, 0)
    filtered = third_ref[...].reshape(size_y * size_x, lanes)
    folded = split_dot(filtered, fold_high[...], fold_low[...]).reshape(size_y, size_x, size_z)
    for y in range(size_y):
        out_ref[:, y, :] = folded[y]
        field_ref[:, y * size_z : (y + 1) * size_z] = folded[y]


def potential_kernel(
    capacity, chunks, rows, weight, piece, place_ref, field_ref, near_ref, far_ref, out_ref, total_ref
):
    list_orb, points = near_ref.shape
    half = field_ref.shape[1] // 2
    for side, values_ref in enumerate((near_ref, far_ref)):
        for q in range(points // piece):
            field = jnp.concatenate(
                [
                    field_ref[x : x + 1, side * half : (side + 1) * half]
                    for x in range(q * piece // half, (q + 1) * piece // half)
                ],
                axis=1,
            )
            block = values_ref[:, q * piece : (q + 1) * piece]
            weighted = (field * block.astype(jnp.float32) * weight).astype(jnp.bfloat16)
            term = lax.dot_general(
                block, weighted, (((1,), (1,)), ((), ())), preferred_element_type=jnp.float32
            )
            total_ref[...] = term if side + q == 0 else total_ref[...] + term

    last = list_orb // rows - 1

    def visit(j, carry):
        t, k = j // capacity, j % capacity
        row = pl.multiple_of(jnp.minimum(place_ref[0, j], last) * rows, rows)
        for c in range(chunks):
            lanes = slice(c * LANES, (c + 1) * LANES)
            out_ref[t, k, :, lanes] = total_ref[pl.ds(row, rows), lanes].astype(jnp.bfloat16)
        return carry

    lax.fori_loop(0, out_ref.shape[0] * capacity, visit, 0, unroll=4)


def unpack_kernel(tile_count, tile_ref, back_ref, out_hbm, count_ref, sem):
    def visit(i, t, slot):
        pltpu.make_async_copy(back_ref.at[t, slot], out_hbm.at[i], sem.at[0]).start()

    for_each_slab(tile_ref, count_ref, tile_count, out_hbm.shape[0], visit)
    pltpu.make_async_copy(out_hbm, out_hbm, sem.at[0]).wait()


def moved(block, shifts):
    axes = tuple(shifts)
    sizes = [lax.axis_size(axis) for axis in axes]
    pairs = []
    for source in np.ndindex(*sizes):
        target = [(s + shifts[axis]) % n for s, axis, n in zip(source, axes, sizes)]
        pairs.append(
            (int(np.ravel_multi_index(source, sizes)), int(np.ravel_multi_index(target, sizes)))
        )
    return lax.ppermute(block, axes, pairs)


def band_tables(size_z, neighbours):
    tap_table, mix = kernel_tables(RADIUS)

    def band(shift):
        table = np.zeros((size_z, len(ALPHAS), size_z), np.float64)
        for m in range(len(ALPHAS)):
            for source in range(size_z):
                for target in range(size_z):
                    offset = source + shift - target
                    if abs(offset) <= RADIUS:
                        table[source, m, target] = tap_table[m][offset + RADIUS]
        return table.reshape(size_z, len(ALPHAS) * size_z)

    own, low, high = band(0), band(-size_z), band(size_z)
    bands = {0: [own + low + high], 1: [own, low + high], 2: [own, low, high]}[neighbours]
    taps = np.zeros((16, len(ALPHAS) * size_z), np.float64)
    for d in range(RADIUS + 1):
        taps[d] = np.repeat([row[RADIUS + d] for row in tap_table], size_z)
    fold = np.concatenate([mix[m] * np.eye(size_z) for m in range(len(ALPHAS))], axis=0)

    def split(table):
        high = table.astype(np.float32).astype(jnp.bfloat16)
        low = (table - high.astype(np.float64)).astype(np.float32).astype(jnp.bfloat16)
        return [high, low]

    return [taps.astype(np.float32), *split(np.concatenate(bands, axis=0)), *split(fold)]


def local(orbital_values, dm_slabs, slab_tile, slab_place):
    size_x, size_y, size_z, list_orb = orbital_values.shape
    slab_count, atom_orb, _ = dm_slabs.shape
    list_blk = list_orb // atom_orb
    tile_count = lax.axis_size("gx") * lax.axis_size("gy")
    capacity = max(2, 2 * ((list_blk + tile_count - 1) // tile_count))
    chunks = list_orb // LANES
    tile_points = size_x * size_y * size_z
    plane = size_y * size_z
    counts = pltpu.SMEM((tile_count,), jnp.int32)

    packed = pl.pallas_call(
        functools.partial(pack_kernel, capacity, chunks, float(list_blk)),
        out_shape=jax.ShapeDtypeStruct(
            (tile_count, capacity * chunks + 1, atom_orb, LANES), jnp.bfloat16
        ),
        in_specs=[HBM_SPEC] * 3,
        out_specs=VMEM_SPEC,
        scratch_shapes=[
            pltpu.SMEM((slab_count,), jnp.int32),
            pltpu.SMEM((slab_count,), jnp.int32),
            pltpu.VMEM(dm_slabs.shape, dm_slabs.dtype),
            counts,
            pltpu.VMEM((tile_count, atom_orb, LANES), jnp.float32),
            pltpu.SemaphoreType.DMA((3,)),
        ],
        compiler_params=grant(4),
        name="pack",
    )(in_hbm(slab_tile), in_hbm(slab_place), in_hbm(dm_slabs))
    arrived = lax.all_to_all(packed, ("gx", "gy"), split_axis=0, concat_axis=0, tiled=True)
    half = plane // 2
    half_points = tile_points // 2
    piece = 4 * half
    bf16 = lambda *shape: jax.ShapeDtypeStruct(shape, jnp.bfloat16)
    f32 = lambda *shape: jax.ShapeDtypeStruct(shape, jnp.float32)
    near, far = pl.pallas_call(
        functools.partial(turn_kernel, size_x),
        out_shape=(
            pltpu.VMEM((list_orb, half_points), jnp.bfloat16),
            bf16(list_orb, half_points),
        ),
        in_specs=[HBM_SPEC],
        out_specs=(VMEM_SPEC, HBM_SPEC),
        scratch_shapes=[
            pltpu.VMEM((tile_points, list_orb), jnp.bfloat16),
            pltpu.VMEM((list_orb, half_points), jnp.bfloat16),
            pltpu.SemaphoreType.DMA((size_x // 2,)),
            pltpu.SemaphoreType.DMA((1,)),
        ],
        compiler_params=grant(20),
        cost_estimate=cost(0, 4 * tile_points * list_orb),
        name="turn",
    )(in_hbm(orbital_values.reshape(tile_points, list_orb)))

    slots = LANES * ((tile_count * capacity + LANES - 1) // LANES)
    product = 2 * half_points * list_orb * list_orb
    low_y, places, matrix, far = pl.pallas_call(
        functools.partial(near_kernel, capacity, chunks, piece),
        out_shape=(
            f32(size_x, half),
            jax.ShapeDtypeStruct((1, slots), jnp.int32),
            bf16(list_orb, list_orb),
            pltpu.VMEM((list_orb, half_points), jnp.bfloat16),
        ),
        in_specs=[VMEM_SPEC, VMEM_SPEC, HBM_SPEC],
        out_specs=(VMEM_SPEC,) * 4,
        scratch_shapes=[
            pltpu.VMEM((tile_count * capacity * atom_orb, LANES), jnp.float32),
            pltpu.SemaphoreType.DMA((1,)),
        ],
        compiler_params=grant(20),
        cost_estimate=cost(product, 2 * half_points * list_orb),
        name="near",
    )(arrived, near, in_hbm(far))
    after = moved(low_y, {"gy": -1})
    high_y = pl.pallas_call(
        functools.partial(far_kernel, piece),
        out_shape=f32(size_x, half),
        in_specs=[VMEM_SPEC, VMEM_SPEC],
        out_specs=VMEM_SPEC,
        compiler_params=grant(20),
        cost_estimate=cost(product, 2 * half_points * list_orb),
        name="far",
    )(matrix, far)
    before = moved(high_y, {"gy": 1})

    own, top, bottom = pl.pallas_call(
        join_kernel,
        out_shape=(f32(size_x, 2 * plane), f32(RADIUS, 2 * plane), f32(RADIUS, 2 * plane)),
        in_specs=[VMEM_SPEC] * 4,
        out_specs=(VMEM_SPEC,) * 3,
        compiler_params=grant(2),
        name="join",
    )(before, low_y, high_y, after)
    layers = lax.axis_size("gz")
    blocks = []
    for shift in {1: [0], 2: [0, 1]}.get(layers, [0, 1, -1]):
        blocks.append(moved(bottom, {"gx": 1, "gz": shift}))
        blocks.append(moved(own, {"gz": shift}) if shift else own)
        blocks.append(moved(top, {"gx": -1, "gz": shift}))
    parts = len(blocks) // 3
    tables = band_tables(size_z, parts - 1)
    lanes = tables[0].shape[1]
    wide_x, wide_y = size_x + 2 * RADIUS, size_y + 2 * RADIUS
    potential, field = pl.pallas_call(
        functools.partial(filter_kernel, parts),
        out_shape=(f32(size_x, size_y, size_z), f32(size_x, plane)),
        in_specs=[VMEM_SPEC] * (len(tables) + len(blocks)),
        out_specs=(VMEM_SPEC,) * 2,
        scratch_shapes=[
            pltpu.VMEM((wide_y, wide_x, parts * size_z), jnp.float32),
            pltpu.VMEM((wide_y, wide_x, lanes), jnp.float32),
            pltpu.VMEM((size_y, wide_x, lanes), jnp.float32),
            pltpu.VMEM((size_y, size_x, lanes), jnp.float32),
        ],
        compiler_params=grant(12),
        name="filter",
    )(*map(jnp.asarray, tables), *blocks)

    returned = pl.pallas_call(
        functools.partial(
            potential_kernel, capacity, chunks, atom_orb, float(tile_points) ** (-0.5), 2 * piece
        ),
        out_shape=bf16(tile_count, capacity, atom_orb, list_orb),
        in_specs=[SMEM_SPEC] + [VMEM_SPEC] * 3,
        out_specs=VMEM_SPEC,
        scratch_shapes=[pltpu.VMEM((list_orb, list_orb), jnp.float32)],
        compiler_params=grant(20),
        name="potential",
    )(places, field, near, far)
    back = lax.all_to_all(returned, ("gx", "gy"), split_axis=0, concat_axis=0, tiled=True)
    own_rows = pl.pallas_call(
        functools.partial(unpack_kernel, tile_count),
        out_shape=bf16(slab_count, atom_orb, list_orb),
        in_specs=[SMEM_SPEC, VMEM_SPEC],
        out_specs=HBM_SPEC,
        scratch_shapes=[counts, pltpu.SemaphoreType.DMA((1,))],
        compiler_params=grant(4),
        name="unpack",
    )(slab_tile, back)
    return (potential, own_rows)


def solution(mesh):
    placed = (
        P("gx", "gy", "gz", None),
        P(("gx", "gy", "gz"), None, None),
        P(("gx", "gy", "gz")),
        P(("gx", "gy", "gz")),
    )
    return jax.shard_map(
        local,
        mesh=mesh,
        in_specs=placed,
        out_specs=(P("gx", "gy", "gz"), P(("gx", "gy", "gz"), None, None)),
        check_vma=False,
    )
```

```python
import functools
import math

import jax
import jax.numpy as jnp
import numpy as np
from jax import lax
from jax.experimental import pallas as pl
from jax.experimental.pallas import tpu as pltpu
from jax.sharding import PartitionSpec as P


RADIUS = 8
LANES = 128

ALPHAS = (0.012, 0.025, 0.05, 0.1, 0.2, 0.4, 0.8, 1.6)
MIXES = (0.3, 0.3, 0.32, 0.34, 0.36, 0.38, 0.4, 0.42)

VMEM_SPEC = pl.BlockSpec(memory_space=pltpu.VMEM)
SMEM_SPEC = pl.BlockSpec(memory_space=pltpu.SMEM)
HBM_SPEC = pl.BlockSpec(memory_space=pltpu.HBM)


def in_hbm(array):
    return pltpu.with_memory_space_constraint(array, pltpu.HBM)


def grant(mebibytes):
    return pltpu.CompilerParams(vmem_limit_bytes=mebibytes << 20)


def kernel_tables(radius):
    tap_table = [
        [math.exp(-alpha * offset * offset) for offset in range(-radius, radius + 1)]
        for alpha in ALPHAS
    ]
    mix = [
        MIXES[term] / sum((tap * tap for tap in tap_table[term])) ** 1.5
        for term in range(len(ALPHAS))
    ]
    return (tap_table, mix)


def cost(flops, moved_bytes):
    return pl.CostEstimate(flops=flops, bytes_accessed=moved_bytes, transcendentals=0)


def for_each_slab(tile_ref, count_ref, tile_count, slab_count, visit):
    for t in range(tile_count):
        count_ref[t] = 0

    def step(i, carry):
        t = tile_ref[i]
        slot = count_ref[t]
        count_ref[t] = slot + 1
        visit(i, t, slot)
        return carry

    lax.fori_loop(0, slab_count, step, 0, unroll=4)


def pack_kernel(
    capacity, chunks, empty, tile_hbm, place_hbm, slab_hbm, out_ref,
    tile_ref, place_ref, slab_ref, count_ref, label_ref, sems,
):
    copies = [
        pltpu.make_async_copy(tile_hbm, tile_ref, sems.at[0]),
        pltpu.make_async_copy(place_hbm, place_ref, sems.at[1]),
        pltpu.make_async_copy(slab_hbm, slab_ref, sems.at[2]),
    ]
    for copy in copies:
        copy.start()
    tile_count = out_ref.shape[0]
    label_ref[...] = jnp.full(label_ref.shape, empty, jnp.float32)
    out_ref[...] = jnp.zeros(out_ref.shape, out_ref.dtype)
    for copy in copies:
        copy.wait()

    def visit(i, t, slot):
        slab = slab_ref[i]
        for c in range(chunks):
            out_ref[t, slot * chunks + c] = slab[:, c * LANES : (c + 1) * LANES]
        label = place_ref[i].astype(jnp.float32)
        label_ref[t, pl.ds(slot, 1), :] = jnp.full((1, LANES), label, jnp.float32)

    for_each_slab(tile_ref, count_ref, tile_count, slab_ref.shape[0], visit)
    out_ref[:, capacity * chunks] = label_ref[...].astype(jnp.bfloat16)


def odd_row():
    return lax.rem(lax.axis_index("gy"), 2)


def turn_kernel(planes, values_hbm, near_ref, far_hbm, values_ref, far_ref, sems, out_sem):
    points = values_ref.shape[0]
    plane = points // planes
    half = plane // 2
    copies = []
    for x in range(0, planes, 2):
        part = slice(x * plane, (x + 2) * plane)
        copies.append(
            pltpu.make_async_copy(values_hbm.at[part], values_ref.at[part], sems.at[x // 2])
        )
        copies[-1].start()
    near_start = odd_row() * half
    for x in range(0, planes, 2):
        copies[x // 2].wait()
        for start, out_ref in ((near_start, near_ref), (half - near_start, far_ref)):
            rows = [
                values_ref[pl.ds(pl.multiple_of((x + i) * plane + start, half), half), :]
                for i in range(2)
            ]
            out_ref[:, x * half : (x + 2) * half] = jnp.concatenate(rows, axis=0).T
    copy = pltpu.make_async_copy(far_ref, far_hbm, out_sem.at[0])
    copy.start()
    copy.wait()


def arrange(capacity, chunks, arrived_ref, place_ref, wide_ref, turned_ref):
    tile_count, _, rows, _ = arrived_ref.shape
    slots = tile_count * capacity
    labels = arrived_ref[:, capacity * chunks].astype(jnp.float32)[:, :capacity]
    labels = labels.reshape(slots, LANES)
    width = place_ref.shape[1]
    for g in range(width // LANES):
        group = labels[g * LANES : (g + 1) * LANES]
        here = lax.broadcasted_iota(jnp.int32, group.shape, 0) == lax.broadcasted_iota(
            jnp.int32, group.shape, 1
        )
        place_ref[:, g * LANES : (g + 1) * LANES] = jnp.sum(
            jnp.where(here, group, 0.0), axis=0, keepdims=True
        ).astype(jnp.int32)
    first_row = jnp.broadcast_to(labels.reshape(slots, 1, LANES) * rows, (slots, rows, LANES))
    source = first_row + lax.broadcasted_iota(jnp.int32, (slots, rows, LANES), 1).astype(
        jnp.float32
    )
    lane = lax.broadcasted_iota(jnp.int32, (slots, rows, LANES), 2).astype(jnp.float32)
    hot = []
    for c in range(chunks):
        match = jnp.where(source == lane + float(c * LANES), 1.0, 0.0)
        hot.append(match.reshape(slots * rows, LANES).astype(jnp.bfloat16))
    hot = jnp.concatenate(hot, axis=1)
    for c in range(chunks):
        for t in range(tile_count):
            for k in range(capacity):
                row = (t * capacity + k) * rows
                wide_ref[row : row + rows, :] = arrived_ref[t, k * chunks + c].astype(jnp.float32)
        across = wide_ref[...].T.astype(jnp.bfloat16)
        turned_ref[c * LANES : (c + 1) * LANES, :] = jnp.dot(
            across, hot, preferred_element_type=jnp.float32
        ).astype(jnp.bfloat16)


def half_density(piece, turned_ref, values_ref, out_ref):
    half = out_ref.shape[1]
    for q in range(values_ref.shape[1] // piece):
        block = values_ref[:, q * piece : (q + 1) * piece]
        mixed = jnp.dot(turned_ref[...], block, preferred_element_type=jnp.float32)
        density = jnp.sum(mixed * block.astype(jnp.float32), axis=0, keepdims=True)
        for p in range(piece // half):
            row = q * (piece // half) + p
            out_ref[row : row + 1, :] = density[:, p * half : (p + 1) * half]


def near_kernel(
    capacity, chunks, piece, arrived_ref, near_ref, far_hbm,
    out_ref, place_ref, turned_ref, far_ref, wide_ref, sem,
):
    copy = pltpu.make_async_copy(far_hbm, far_ref, sem.at[0])
    copy.start()
    arrange(capacity, chunks, arrived_ref, place_ref, wide_ref, turned_ref)
    half_density(piece, turned_ref, near_ref, out_ref)
    copy.wait()


def far_kernel(piece, turned_ref, far_ref, out_ref):
    half_density(piece, turned_ref, far_ref, out_ref)


def join_kernel(near_ref, far_ref, from_wrap_ref, from_pair_ref, out_ref):
    half = near_ref.shape[1]
    odd = odd_row() == 1
    before = jnp.where(odd, from_pair_ref[...], from_wrap_ref[...])
    low = jnp.where(odd, far_ref[...], near_ref[...])
    high = jnp.where(odd, near_ref[...], far_ref[...])
    after = jnp.where(odd, from_wrap_ref[...], from_pair_ref[...])
    for i, block in enumerate((before, low, high, after)):
        out_ref[:, i * half : (i + 1) * half] = block


def edge_kernel(*refs):
    *block_refs, top_ref, bottom_ref = refs
    rows = top_ref.shape[1]
    for i, ref in enumerate(block_refs):
        top_ref[i] = ref[:rows, :]
        bottom_ref[i] = ref[ref.shape[0] - rows :, :]


def split_dot(left, high, low):
    left_high = left.astype(jnp.bfloat16)
    left_low = (left - left_high.astype(jnp.float32)).astype(jnp.bfloat16)
    out = jnp.dot(left_high, high, preferred_element_type=jnp.float32)
    out = out + jnp.dot(left_low, high, preferred_element_type=jnp.float32)
    return out + jnp.dot(left_high, low, preferred_element_type=jnp.float32)


def filter_kernel(parts, *refs):
    taps_ref, band_high, band_low, fold_high, fold_low, before_ref, after_ref = refs[:7]
    own_refs = refs[7 : 7 + parts]
    out_ref, field_ref, grid_ref, first_ref, second_ref, third_ref = refs[7 + parts :]
    size_x, size_y, size_z = out_ref.shape
    wide_y, wide_x, lanes = first_ref.shape
    for part in range(parts):
        start = 0
        for block in (before_ref.at[part], own_refs[part], after_ref.at[part]):
            rows = block.shape[0]
            for y in range(wide_y):
                grid_ref[y, start : start + rows, part * size_z : (part + 1) * size_z] = block[
                    :, y * size_z : (y + 1) * size_z
                ]
            start += rows
    grid = grid_ref[...].reshape(wide_y * wide_x, parts * size_z)
    first_ref[...] = split_dot(grid, band_high[...], band_low[...]).reshape(wide_y, wide_x, lanes)

    def tap(distance, rows):
        return jnp.broadcast_to(taps_ref[distance : distance + 1, :], (rows, lanes))

    def smooth(y, carry):
        run = tap(0, wide_x) * first_ref[y + RADIUS]
        for d in range(1, RADIUS + 1):
            pair = first_ref[y + (RADIUS - d)] + first_ref[y + (RADIUS + d)]
            run = run + tap(d, wide_x) * pair
        second_ref[y] = run
        run = tap(0, size_x) * second_ref[y, RADIUS : RADIUS + size_x, :]
        for d in range(1, RADIUS + 1):
            pair = (
                second_ref[y, RADIUS - d : RADIUS - d + size_x, :]
                + second_ref[y, RADIUS + d : RADIUS + d + size_x, :]
            )
            run = run + tap(d, size_x) * pair
        third_ref[y] = run
        return carry

    lax.fori_loop(0, size_y, smooth, 0, unroll=4)
    filtered = third_ref[...].reshape(size_y * size_x, lanes)
    folded = split_dot(filtered, fold_high[...], fold_low[...]).reshape(size_y, size_x, size_z)
    for y in range(size_y):
        out_ref[:, y, :] = folded[y]
        field_ref[:, y * size_z : (y + 1) * size_z] = folded[y]


def potential_kernel(
    capacity, chunks, rows, weight, piece, place_vmem, grid_ref, field_ref, near_ref, far_ref,
    out_ref, grid_hbm, total_ref, place_ref, sems,
):
    copies = [
        pltpu.make_async_copy(place_vmem, place_ref, sems.at[0]),
        pltpu.make_async_copy(grid_ref, grid_hbm, sems.at[1]),
    ]
    for copy in copies:
        copy.start()
    list_orb, points = near_ref.shape
    half = field_ref.shape[1] // 2
    odd = odd_row() == 1
    low, high = field_ref[:, :half] * weight, field_ref[:, half:] * weight
    first = True
    for values_ref, source in (
        (near_ref, jnp.where(odd, high, low)),
        (far_ref, jnp.where(odd, low, high)),
    ):
        for q in range(points // piece):
            field = jnp.concatenate(
                [
                    source[x : x + 1, :]
                    for x in range(q * piece // half, (q + 1) * piece // half)
                ],
                axis=1,
            )
            block = values_ref[:, q * piece : (q + 1) * piece]
            weighted = (field * block.astype(jnp.float32)).astype(jnp.bfloat16)
            term = lax.dot_general(
                block, weighted, (((1,), (1,)), ((), ())), preferred_element_type=jnp.float32
            )
            total_ref[...] = term if first else total_ref[...] + term
            first = False

    for copy in copies:
        copy.wait()
    last = list_orb // rows - 1

    def visit(j, carry):
        t, k = j // capacity, j % capacity
        row = pl.multiple_of(jnp.minimum(place_ref[0, j], last) * rows, rows)
        for c in range(chunks):
            lanes = slice(c * LANES, (c + 1) * LANES)
            out_ref[t, k, :, lanes] = total_ref[pl.ds(row, rows), lanes].astype(jnp.bfloat16)
        return carry

    lax.fori_loop(0, out_ref.shape[0] * capacity, visit, 0, unroll=4)


def unpack_kernel(tile_count, tile_ref, back_ref, out_hbm, count_ref, sem):
    def visit(i, t, slot):
        pltpu.make_async_copy(back_ref.at[t, slot], out_hbm.at[i], sem.at[0]).start()

    for_each_slab(tile_ref, count_ref, tile_count, out_hbm.shape[0], visit)
    pltpu.make_async_copy(out_hbm, out_hbm, sem.at[0]).wait()


def moved(block, shifts):
    axes = tuple(shifts)
    sizes = [lax.axis_size(axis) for axis in axes]
    pairs = []
    for source in np.ndindex(*sizes):
        target = [(s + shifts[axis]) % n for s, axis, n in zip(source, axes, sizes)]
        pairs.append(
            (int(np.ravel_multi_index(source, sizes)), int(np.ravel_multi_index(target, sizes)))
        )
    return lax.ppermute(block, axes, pairs)


def band_tables(size_z, neighbours):
    tap_table, mix = kernel_tables(RADIUS)

    def band(shift):
        table = np.zeros((size_z, len(ALPHAS), size_z), np.float64)
        for m in range(len(ALPHAS)):
            for source in range(size_z):
                for target in range(size_z):
                    offset = source + shift - target
                    if abs(offset) <= RADIUS:
                        table[source, m, target] = tap_table[m][offset + RADIUS]
        return table.reshape(size_z, len(ALPHAS) * size_z)

    own, low, high = band(0), band(-size_z), band(size_z)
    bands = {0: [own + low + high], 1: [own, low + high], 2: [own, low, high]}[neighbours]
    taps = np.zeros((16, len(ALPHAS) * size_z), np.float64)
    for d in range(RADIUS + 1):
        taps[d] = np.repeat([row[RADIUS + d] for row in tap_table], size_z)
    fold = np.concatenate([mix[m] * np.eye(size_z) for m in range(len(ALPHAS))], axis=0)

    def split(table):
        high = table.astype(np.float32).astype(jnp.bfloat16)
        low = (table - high.astype(np.float64)).astype(np.float32).astype(jnp.bfloat16)
        return [high, low]

    return [taps.astype(np.float32), *split(np.concatenate(bands, axis=0)), *split(fold)]


def local(orbital_values, dm_slabs, slab_tile, slab_place):
    size_x, size_y, size_z, list_orb = orbital_values.shape
    slab_count, atom_orb, _ = dm_slabs.shape
    list_blk = list_orb // atom_orb
    tile_count = lax.axis_size("gx") * lax.axis_size("gy")
    capacity = max(2, 2 * ((list_blk + tile_count - 1) // tile_count))
    chunks = list_orb // LANES
    tile_points = size_x * size_y * size_z
    plane = size_y * size_z
    counts = pltpu.SMEM((tile_count,), jnp.int32)

    packed = pl.pallas_call(
        functools.partial(pack_kernel, capacity, chunks, float(list_blk)),
        out_shape=jax.ShapeDtypeStruct(
            (tile_count, capacity * chunks + 1, atom_orb, LANES), jnp.bfloat16
        ),
        in_specs=[HBM_SPEC] * 3,
        out_specs=VMEM_SPEC,
        scratch_shapes=[
            pltpu.SMEM((slab_count,), jnp.int32),
            pltpu.SMEM((slab_count,), jnp.int32),
            pltpu.VMEM(dm_slabs.shape, dm_slabs.dtype),
            counts,
            pltpu.VMEM((tile_count, atom_orb, LANES), jnp.float32),
            pltpu.SemaphoreType.DMA((3,)),
        ],
        compiler_params=grant(4),
        name="pack",
    )(in_hbm(slab_tile), in_hbm(slab_place), in_hbm(dm_slabs))
    arrived = lax.all_to_all(packed, ("gx", "gy"), split_axis=0, concat_axis=0, tiled=True)
    half = plane // 2
    half_points = tile_points // 2
    piece = 4 * half
    bf16 = lambda *shape: jax.ShapeDtypeStruct(shape, jnp.bfloat16)
    f32 = lambda *shape: jax.ShapeDtypeStruct(shape, jnp.float32)
    near, far = pl.pallas_call(
        functools.partial(turn_kernel, size_x),
        out_shape=(
            pltpu.VMEM((list_orb, half_points), jnp.bfloat16),
            bf16(list_orb, half_points),
        ),
        in_specs=[HBM_SPEC],
        out_specs=(VMEM_SPEC, HBM_SPEC),
        scratch_shapes=[
            pltpu.VMEM((tile_points, list_orb), jnp.bfloat16),
            pltpu.VMEM((list_orb, half_points), jnp.bfloat16),
            pltpu.SemaphoreType.DMA((size_x // 2,)),
            pltpu.SemaphoreType.DMA((1,)),
        ],
        compiler_params=grant(20),
        cost_estimate=cost(0, 4 * tile_points * list_orb),
        name="turn",
    )(in_hbm(orbital_values.reshape(tile_points, list_orb)))

    slots = LANES * ((tile_count * capacity + LANES - 1) // LANES)
    product = 2 * half_points * list_orb * list_orb
    near_y, places, matrix, far = pl.pallas_call(
        functools.partial(near_kernel, capacity, chunks, piece),
        out_shape=(
            f32(size_x, half),
            jax.ShapeDtypeStruct((1, slots), jnp.int32),
            bf16(list_orb, list_orb),
            pltpu.VMEM((list_orb, half_points), jnp.bfloat16),
        ),
        in_specs=[VMEM_SPEC, VMEM_SPEC, HBM_SPEC],
        out_specs=(VMEM_SPEC,) * 4,
        scratch_shapes=[
            pltpu.VMEM((tile_count * capacity * atom_orb, LANES), jnp.float32),
            pltpu.SemaphoreType.DMA((1,)),
        ],
        compiler_params=grant(20),
        cost_estimate=cost(product, 2 * half_points * list_orb),
        name="near",
    )(arrived, near, in_hbm(far))
    rows = lax.axis_size("gy")
    pair = [(i, i ^ 1) for i in range(rows)]
    wrap = [(i, (i - 1 + 2 * (i % 2)) % rows) for i in range(rows)]
    from_wrap = lax.ppermute(near_y, "gy", wrap)
    far_y = pl.pallas_call(
        functools.partial(far_kernel, piece),
        out_shape=f32(size_x, half),
        in_specs=[VMEM_SPEC, VMEM_SPEC],
        out_specs=VMEM_SPEC,
        compiler_params=grant(20),
        cost_estimate=cost(product, 2 * half_points * list_orb),
        name="far",
    )(matrix, far)
    from_pair = lax.ppermute(far_y, "gy", pair)

    grid = pl.pallas_call(
        join_kernel,
        out_shape=f32(size_x, 2 * plane),
        in_specs=[VMEM_SPEC] * 4,
        out_specs=VMEM_SPEC,
        compiler_params=grant(2),
        name="join",
    )(near_y, far_y, from_wrap, from_pair)
    layers = lax.axis_size("gz")
    blocks = [grid]
    for shift in {1: [], 2: [1]}.get(layers, [1, -1]):
        blocks.append(moved(grid, {"gz": shift}))
    parts = len(blocks)
    top, bottom = pl.pallas_call(
        edge_kernel,
        out_shape=(f32(parts, RADIUS, 2 * plane),) * 2,
        in_specs=[VMEM_SPEC] * parts,
        out_specs=(VMEM_SPEC,) * 2,
        compiler_params=grant(2),
        name="edge",
    )(*blocks)
    before, after = moved(bottom, {"gx": 1}), moved(top, {"gx": -1})
    tables = band_tables(size_z, parts - 1)
    lanes = tables[0].shape[1]
    wide_x, wide_y = size_x + 2 * RADIUS, size_y + 2 * RADIUS
    potential, field = pl.pallas_call(
        functools.partial(filter_kernel, parts),
        out_shape=(pltpu.VMEM((size_x, size_y, size_z), jnp.float32), f32(size_x, plane)),
        in_specs=[VMEM_SPEC] * (len(tables) + 2 + parts),
        out_specs=(VMEM_SPEC,) * 2,
        scratch_shapes=[
            pltpu.VMEM((wide_y, wide_x, parts * size_z), jnp.float32),
            pltpu.VMEM((wide_y, wide_x, lanes), jnp.float32),
            pltpu.VMEM((size_y, wide_x, lanes), jnp.float32),
            pltpu.VMEM((size_y, size_x, lanes), jnp.float32),
        ],
        compiler_params=grant(12),
        name="filter",
    )(*map(jnp.asarray, tables), before, after, *blocks)

    returned, potential = pl.pallas_call(
        functools.partial(
            potential_kernel, capacity, chunks, atom_orb, float(tile_points) ** (-0.5), 2 * piece
        ),
        out_shape=(
            bf16(tile_count, capacity, atom_orb, list_orb),
            f32(size_x, size_y, size_z),
        ),
        in_specs=[VMEM_SPEC] * 5,
        out_specs=(VMEM_SPEC, HBM_SPEC),
        scratch_shapes=[
            pltpu.VMEM((list_orb, list_orb), jnp.float32),
            pltpu.SMEM((1, slots), jnp.int32),
            pltpu.SemaphoreType.DMA((2,)),
        ],
        compiler_params=grant(20),
        name="potential",
    )(places, potential, field, near, far)
    back = lax.all_to_all(returned, ("gx", "gy"), split_axis=0, concat_axis=0, tiled=True)
    own_rows = pl.pallas_call(
        functools.partial(unpack_kernel, tile_count),
        out_shape=bf16(slab_count, atom_orb, list_orb),
        in_specs=[SMEM_SPEC, VMEM_SPEC],
        out_specs=HBM_SPEC,
        scratch_shapes=[counts, pltpu.SemaphoreType.DMA((1,))],
        compiler_params=grant(4),
        name="unpack",
    )(slab_tile, back)
    return (potential, own_rows)


def solution(mesh):
    placed = (
        P("gx", "gy", "gz", None),
        P(("gx", "gy", "gz"), None, None),
        P(("gx", "gy", "gz")),
        P(("gx", "gy", "gz")),
    )

    return jax.shard_map(
        local,
        mesh=mesh,
        in_specs=placed,
        out_specs=(P("gx", "gy", "gz"), P(("gx", "gy", "gz"), None, None)),
        check_vma=False,
    )
```

```python
import functools
import math

import jax
import jax.numpy as jnp
import numpy as np
from jax import lax
from jax.experimental import pallas as pl
from jax.experimental.pallas import tpu as pltpu
from jax.sharding import PartitionSpec as P


RADIUS = 8
LANES = 128

ALPHAS = (0.012, 0.025, 0.05, 0.1, 0.2, 0.4, 0.8, 1.6)
MIXES = (0.3, 0.3, 0.32, 0.34, 0.36, 0.38, 0.4, 0.42)

VMEM_SPEC = pl.BlockSpec(memory_space=pltpu.VMEM)
SMEM_SPEC = pl.BlockSpec(memory_space=pltpu.SMEM)
HBM_SPEC = pl.BlockSpec(memory_space=pltpu.HBM)


def in_hbm(array):
    return pltpu.with_memory_space_constraint(array, pltpu.HBM)


def grant(mebibytes):
    return pltpu.CompilerParams(vmem_limit_bytes=mebibytes << 20)


def kernel_tables(radius):
    tap_table = [
        [math.exp(-alpha * offset * offset) for offset in range(-radius, radius + 1)]
        for alpha in ALPHAS
    ]
    mix = [
        MIXES[term] / sum((tap * tap for tap in tap_table[term])) ** 1.5
        for term in range(len(ALPHAS))
    ]
    return (tap_table, mix)


def cost(flops, moved_bytes):
    return pl.CostEstimate(flops=flops, bytes_accessed=moved_bytes, transcendentals=0)


def for_each_slab(tile_ref, count_ref, tile_count, slab_count, visit):
    for t in range(tile_count):
        count_ref[t] = 0

    def step(i, carry):
        t = tile_ref[i]
        slot = count_ref[t]
        count_ref[t] = slot + 1
        visit(i, t, slot)
        return carry

    lax.fori_loop(0, slab_count, step, 0, unroll=4)


def pack_kernel(
    capacity, chunks, empty, tile_hbm, place_hbm, slab_hbm, out_ref,
    tile_ref, place_ref, slab_ref, count_ref, label_ref, sems,
):
    copies = [
        pltpu.make_async_copy(tile_hbm, tile_ref, sems.at[0]),
        pltpu.make_async_copy(place_hbm, place_ref, sems.at[1]),
        pltpu.make_async_copy(slab_hbm, slab_ref, sems.at[2]),
    ]
    for copy in copies:
        copy.start()
    tile_count = out_ref.shape[0]
    label_ref[...] = jnp.full(label_ref.shape, empty, jnp.float32)
    out_ref[...] = jnp.zeros(out_ref.shape, out_ref.dtype)
    for copy in copies:
        copy.wait()

    def visit(i, t, slot):
        slab = slab_ref[i]
        for c in range(chunks):
            out_ref[t, slot * chunks + c] = slab[:, c * LANES : (c + 1) * LANES]
        label = place_ref[i].astype(jnp.float32)
        label_ref[t, pl.ds(slot, 1), :] = jnp.full((1, LANES), label, jnp.float32)

    for_each_slab(tile_ref, count_ref, tile_count, slab_ref.shape[0], visit)
    out_ref[:, capacity * chunks] = label_ref[...].astype(jnp.bfloat16)


def odd_row():
    return lax.rem(lax.axis_index("gy"), 2)


def turn_kernel(planes, values_hbm, near_ref, far_hbm, values_ref, far_ref, sems, out_sem):
    points = values_ref.shape[0]
    plane = points // planes
    half = plane // 2
    copies = []
    for x in range(0, planes, 2):
        part = slice(x * plane, (x + 2) * plane)
        copies.append(
            pltpu.make_async_copy(values_hbm.at[part], values_ref.at[part], sems.at[x // 2])
        )
        copies[-1].start()
    near_start = odd_row() * half
    for x in range(0, planes, 2):
        copies[x // 2].wait()
        for start, out_ref in ((near_start, near_ref), (half - near_start, far_ref)):
            rows = [
                values_ref[pl.ds(pl.multiple_of((x + i) * plane + start, half), half), :]
                for i in range(2)
            ]
            out_ref[:, x * half : (x + 2) * half] = jnp.concatenate(rows, axis=0).T
    copy = pltpu.make_async_copy(far_ref, far_hbm, out_sem.at[0])
    copy.start()
    copy.wait()


def arrange(capacity, chunks, arrived_ref, place_ref, wide_ref, turned_ref):
    tile_count, _, rows, _ = arrived_ref.shape
    slots = tile_count * capacity
    labels = arrived_ref[:, capacity * chunks].astype(jnp.float32)[:, :capacity]
    labels = labels.reshape(slots, LANES)
    width = place_ref.shape[1]
    for g in range(width // LANES):
        group = labels[g * LANES : (g + 1) * LANES]
        here = lax.broadcasted_iota(jnp.int32, group.shape, 0) == lax.broadcasted_iota(
            jnp.int32, group.shape, 1
        )
        place_ref[:, g * LANES : (g + 1) * LANES] = jnp.sum(
            jnp.where(here, group, 0.0), axis=0, keepdims=True
        ).astype(jnp.int32)
    first_row = jnp.broadcast_to(labels.reshape(slots, 1, LANES) * rows, (slots, rows, LANES))
    source = first_row + lax.broadcasted_iota(jnp.int32, (slots, rows, LANES), 1).astype(
        jnp.float32
    )
    lane = lax.broadcasted_iota(jnp.int32, (slots, rows, LANES), 2).astype(jnp.float32)
    hot = []
    for c in range(chunks):
        match = jnp.where(source == lane + float(c * LANES), 1.0, 0.0)
        hot.append(match.reshape(slots * rows, LANES).astype(jnp.bfloat16))
    hot = jnp.concatenate(hot, axis=1)
    for c in range(chunks):
        for t in range(tile_count):
            for k in range(capacity):
                row = (t * capacity + k) * rows
                wide_ref[row : row + rows, :] = arrived_ref[t, k * chunks + c].astype(jnp.float32)
        across = wide_ref[...].T.astype(jnp.bfloat16)
        turned_ref[c * LANES : (c + 1) * LANES, :] = jnp.dot(
            across, hot, preferred_element_type=jnp.float32
        ).astype(jnp.bfloat16)


def half_density(piece, turned_ref, values_ref, out_ref):
    half = out_ref.shape[1]
    for q in range(values_ref.shape[1] // piece):
        block = values_ref[:, q * piece : (q + 1) * piece]
        mixed = jnp.dot(turned_ref[...], block, preferred_element_type=jnp.float32)
        density = jnp.sum(mixed * block.astype(jnp.float32), axis=0, keepdims=True)
        for p in range(piece // half):
            row = q * (piece // half) + p
            out_ref[row : row + 1, :] = density[:, p * half : (p + 1) * half]


def near_kernel(
    capacity, chunks, piece, arrived_ref, near_ref, far_hbm,
    out_ref, place_ref, turned_ref, far_ref, wide_ref, sem,
):
    copy = pltpu.make_async_copy(far_hbm, far_ref, sem.at[0])
    copy.start()
    arrange(capacity, chunks, arrived_ref, place_ref, wide_ref, turned_ref)
    half_density(piece, turned_ref, near_ref, out_ref)
    copy.wait()


def far_kernel(piece, turned_ref, far_ref, out_ref):
    half_density(piece, turned_ref, far_ref, out_ref)


def join_kernel(*refs):
    *half_refs, out_ref, top_ref, bottom_ref = refs
    parts, size_x, _ = out_ref.shape
    reach = top_ref.shape[1]
    half = half_refs[0].shape[1]
    odd = odd_row() == 1
    for part in range(parts):
        near, far, wrap, pair = (ref[...] for ref in half_refs[4 * part : 4 * part + 4])
        blocks = (
            jnp.where(odd, pair, wrap),
            jnp.where(odd, far, near),
            jnp.where(odd, near, far),
            jnp.where(odd, wrap, pair),
        )
        for i, block in enumerate(blocks):
            out_ref[part, :, i * half : (i + 1) * half] = block
        top_ref[part] = out_ref[part, :reach, :]
        bottom_ref[part] = out_ref[part, size_x - reach :, :]


def split_dot(left, high, low):
    left_high = left.astype(jnp.bfloat16)
    left_low = (left - left_high.astype(jnp.float32)).astype(jnp.bfloat16)
    out = jnp.dot(left_high, high, preferred_element_type=jnp.float32)
    out = out + jnp.dot(left_low, high, preferred_element_type=jnp.float32)
    return out + jnp.dot(left_high, low, preferred_element_type=jnp.float32)


def filter_kernel(parts, *refs):
    taps_ref, band_high, band_low, fold_high, fold_low, before_ref, after_ref = refs[:7]
    own_ref, out_ref, field_ref, grid_ref, first_ref, second_ref, third_ref = refs[7:]
    size_x, size_y, size_z = out_ref.shape
    wide_y, wide_x, lanes = first_ref.shape
    for part in range(parts):
        start = 0
        for block in (before_ref.at[part], own_ref.at[part], after_ref.at[part]):
            rows = block.shape[0]
            for y in range(wide_y):
                grid_ref[y, start : start + rows, part * size_z : (part + 1) * size_z] = block[
                    :, y * size_z : (y + 1) * size_z
                ]
            start += rows
    grid = grid_ref[...].reshape(wide_y * wide_x, parts * size_z)
    first_ref[...] = split_dot(grid, band_high[...], band_low[...]).reshape(wide_y, wide_x, lanes)

    def tap(distance, rows):
        return jnp.broadcast_to(taps_ref[distance : distance + 1, :], (rows, lanes))

    def smooth(y, carry):
        run = tap(0, wide_x) * first_ref[y + RADIUS]
        for d in range(1, RADIUS + 1):
            pair = first_ref[y + (RADIUS - d)] + first_ref[y + (RADIUS + d)]
            run = run + tap(d, wide_x) * pair
        second_ref[y] = run
        run = tap(0, size_x) * second_ref[y, RADIUS : RADIUS + size_x, :]
        for d in range(1, RADIUS + 1):
            pair = (
                second_ref[y, RADIUS - d : RADIUS - d + size_x, :]
                + second_ref[y, RADIUS + d : RADIUS + d + size_x, :]
            )
            run = run + tap(d, size_x) * pair
        third_ref[y] = run
        return carry

    lax.fori_loop(0, size_y, smooth, 0, unroll=4)
    filtered = third_ref[...].reshape(size_y * size_x, lanes)
    folded = split_dot(filtered, fold_high[...], fold_low[...]).reshape(size_y, size_x, size_z)
    for y in range(size_y):
        out_ref[:, y, :] = folded[y]
        field_ref[:, y * size_z : (y + 1) * size_z] = folded[y]


def potential_kernel(
    capacity, chunks, rows, weight, piece, place_vmem, grid_ref, field_ref, near_ref, far_ref,
    out_ref, grid_hbm, total_ref, place_ref, sems,
):
    copies = [
        pltpu.make_async_copy(place_vmem, place_ref, sems.at[0]),
        pltpu.make_async_copy(grid_ref, grid_hbm, sems.at[1]),
    ]
    for copy in copies:
        copy.start()
    list_orb, points = near_ref.shape
    half = field_ref.shape[1] // 2
    odd = odd_row() == 1
    low, high = field_ref[:, :half] * weight, field_ref[:, half:] * weight
    first = True
    for values_ref, source in (
        (near_ref, jnp.where(odd, high, low)),
        (far_ref, jnp.where(odd, low, high)),
    ):
        for q in range(points // piece):
            field = jnp.concatenate(
                [
                    source[x : x + 1, :]
                    for x in range(q * piece // half, (q + 1) * piece // half)
                ],
                axis=1,
            )
            block = values_ref[:, q * piece : (q + 1) * piece]
            weighted = (field * block.astype(jnp.float32)).astype(jnp.bfloat16)
            term = lax.dot_general(
                block, weighted, (((1,), (1,)), ((), ())), preferred_element_type=jnp.float32
            )
            total_ref[...] = term if first else total_ref[...] + term
            first = False

    for copy in copies:
        copy.wait()
    last = list_orb // rows - 1

    def visit(j, carry):
        t, k = j // capacity, j % capacity
        row = pl.multiple_of(jnp.minimum(place_ref[0, j], last) * rows, rows)
        for c in range(chunks):
            lanes = slice(c * LANES, (c + 1) * LANES)
            out_ref[t, k, :, lanes] = total_ref[pl.ds(row, rows), lanes].astype(jnp.bfloat16)
        return carry

    lax.fori_loop(0, out_ref.shape[0] * capacity, visit, 0, unroll=4)


def unpack_kernel(tile_count, tile_ref, back_ref, out_hbm, count_ref, sem):
    def visit(i, t, slot):
        pltpu.make_async_copy(back_ref.at[t, slot], out_hbm.at[i], sem.at[0]).start()

    for_each_slab(tile_ref, count_ref, tile_count, out_hbm.shape[0], visit)
    pltpu.make_async_copy(out_hbm, out_hbm, sem.at[0]).wait()


def moved(block, axes, targets):
    sizes = [lax.axis_size(axis) for axis in axes]
    pairs = []
    for place in np.ndindex(*sizes):
        target = [t % n for t, n in zip(targets(*place), sizes)]
        pairs.append(
            (int(np.ravel_multi_index(place, sizes)), int(np.ravel_multi_index(target, sizes)))
        )
    return lax.ppermute(block, axes, pairs)


def band_tables(size_z, neighbours):
    tap_table, mix = kernel_tables(RADIUS)

    def band(shift):
        table = np.zeros((size_z, len(ALPHAS), size_z), np.float64)
        for m in range(len(ALPHAS)):
            for source in range(size_z):
                for target in range(size_z):
                    offset = source + shift - target
                    if abs(offset) <= RADIUS:
                        table[source, m, target] = tap_table[m][offset + RADIUS]
        return table.reshape(size_z, len(ALPHAS) * size_z)

    own, low, high = band(0), band(-size_z), band(size_z)
    bands = {0: [own + low + high], 1: [own, low + high], 2: [own, low, high]}[neighbours]
    taps = np.zeros((16, len(ALPHAS) * size_z), np.float64)
    for d in range(RADIUS + 1):
        taps[d] = np.repeat([row[RADIUS + d] for row in tap_table], size_z)
    fold = np.concatenate([mix[m] * np.eye(size_z) for m in range(len(ALPHAS))], axis=0)

    def split(table):
        high = table.astype(np.float32).astype(jnp.bfloat16)
        low = (table - high.astype(np.float64)).astype(np.float32).astype(jnp.bfloat16)
        return [high, low]

    return [taps.astype(np.float32), *split(np.concatenate(bands, axis=0)), *split(fold)]


def local(orbital_values, dm_slabs, slab_tile, slab_place):
    size_x, size_y, size_z, list_orb = orbital_values.shape
    slab_count, atom_orb, _ = dm_slabs.shape
    list_blk = list_orb // atom_orb
    tile_count = lax.axis_size("gx") * lax.axis_size("gy")
    capacity = max(2, 2 * ((list_blk + tile_count - 1) // tile_count))
    chunks = list_orb // LANES
    tile_points = size_x * size_y * size_z
    plane = size_y * size_z
    counts = pltpu.SMEM((tile_count,), jnp.int32)

    packed = pl.pallas_call(
        functools.partial(pack_kernel, capacity, chunks, float(list_blk)),
        out_shape=jax.ShapeDtypeStruct(
            (tile_count, capacity * chunks + 1, atom_orb, LANES), jnp.bfloat16
        ),
        in_specs=[HBM_SPEC] * 3,
        out_specs=VMEM_SPEC,
        scratch_shapes=[
            pltpu.SMEM((slab_count,), jnp.int32),
            pltpu.SMEM((slab_count,), jnp.int32),
            pltpu.VMEM(dm_slabs.shape, dm_slabs.dtype),
            counts,
            pltpu.VMEM((tile_count, atom_orb, LANES), jnp.float32),
            pltpu.SemaphoreType.DMA((3,)),
        ],
        compiler_params=grant(4),
        name="pack",
    )(in_hbm(slab_tile), in_hbm(slab_place), in_hbm(dm_slabs))
    arrived = lax.all_to_all(packed, ("gx", "gy"), split_axis=0, concat_axis=0, tiled=True)
    half = plane // 2
    half_points = tile_points // 2
    piece = 4 * half
    bf16 = lambda *shape: jax.ShapeDtypeStruct(shape, jnp.bfloat16)
    f32 = lambda *shape: jax.ShapeDtypeStruct(shape, jnp.float32)
    near, far = pl.pallas_call(
        functools.partial(turn_kernel, size_x),
        out_shape=(
            pltpu.VMEM((list_orb, half_points), jnp.bfloat16),
            bf16(list_orb, half_points),
        ),
        in_specs=[HBM_SPEC],
        out_specs=(VMEM_SPEC, HBM_SPEC),
        scratch_shapes=[
            pltpu.VMEM((tile_points, list_orb), jnp.bfloat16),
            pltpu.VMEM((list_orb, half_points), jnp.bfloat16),
            pltpu.SemaphoreType.DMA((size_x // 2,)),
            pltpu.SemaphoreType.DMA((1,)),
        ],
        compiler_params=grant(20),
        cost_estimate=cost(0, 4 * tile_points * list_orb),
        name="turn",
    )(in_hbm(orbital_values.reshape(tile_points, list_orb)))

    slots = LANES * ((tile_count * capacity + LANES - 1) // LANES)
    product = 2 * half_points * list_orb * list_orb
    near_y, places, matrix, far = pl.pallas_call(
        functools.partial(near_kernel, capacity, chunks, piece),
        out_shape=(
            f32(size_x, half),
            jax.ShapeDtypeStruct((1, slots), jnp.int32),
            bf16(list_orb, list_orb),
            pltpu.VMEM((list_orb, half_points), jnp.bfloat16),
        ),
        in_specs=[VMEM_SPEC, VMEM_SPEC, HBM_SPEC],
        out_specs=(VMEM_SPEC,) * 4,
        scratch_shapes=[
            pltpu.VMEM((tile_count * capacity * atom_orb, LANES), jnp.float32),
            pltpu.SemaphoreType.DMA((1,)),
        ],
        compiler_params=grant(20),
        cost_estimate=cost(product, 2 * half_points * list_orb),
        name="near",
    )(arrived, near, in_hbm(far))
    shifts = {1: [], 2: [1]}.get(lax.axis_size("gz"), [1, -1])
    wrap = lambda row: row - 1 + 2 * (row % 2)
    pair = lambda row: row + 1 - 2 * (row % 2)
    near_wrap = [moved(near_y, ("gy",), lambda row: (wrap(row),))]
    near_own = [near_y]
    for shift in shifts:
        near_own.append(moved(near_y, ("gz",), lambda layer: (layer + shift,)))
        near_wrap.append(moved(near_y, ("gy", "gz"), lambda row, layer: (wrap(row), layer + shift)))
    far_y = pl.pallas_call(
        functools.partial(far_kernel, piece),
        out_shape=f32(size_x, half),
        in_specs=[VMEM_SPEC, VMEM_SPEC],
        out_specs=VMEM_SPEC,
        compiler_params=grant(20),
        cost_estimate=cost(product, 2 * half_points * list_orb),
        name="far",
    )(matrix, far)
    far_pair = [moved(far_y, ("gy",), lambda row: (pair(row),))]
    far_own = [far_y]
    for shift in shifts:
        far_own.append(moved(far_y, ("gz",), lambda layer: (layer + shift,)))
        far_pair.append(
            moved(far_y, ("gy", "gz"), lambda row, layer: (pair(row), layer + shift))
        )
    halves = [h for group in zip(near_own, far_own, near_wrap, far_pair) for h in group]
    parts = 1 + len(shifts)
    own, top, bottom = pl.pallas_call(
        join_kernel,
        out_shape=(
            f32(parts, size_x, 2 * plane),
            f32(parts, RADIUS, 2 * plane),
            f32(parts, RADIUS, 2 * plane),
        ),
        in_specs=[VMEM_SPEC] * len(halves),
        out_specs=(VMEM_SPEC,) * 3,
        compiler_params=grant(2),
        name="join",
    )(*halves)
    before = moved(bottom, ("gx",), lambda column: (column + 1,))
    after = moved(top, ("gx",), lambda column: (column - 1,))
    tables = band_tables(size_z, parts - 1)
    lanes = tables[0].shape[1]
    wide_x, wide_y = size_x + 2 * RADIUS, size_y + 2 * RADIUS
    potential, field = pl.pallas_call(
        functools.partial(filter_kernel, parts),
        out_shape=(pltpu.VMEM((size_x, size_y, size_z), jnp.float32), f32(size_x, plane)),
        in_specs=[VMEM_SPEC] * (len(tables) + 3),
        out_specs=(VMEM_SPEC,) * 2,
        scratch_shapes=[
            pltpu.VMEM((wide_y, wide_x, parts * size_z), jnp.float32),
            pltpu.VMEM((wide_y, wide_x, lanes), jnp.float32),
            pltpu.VMEM((size_y, wide_x, lanes), jnp.float32),
            pltpu.VMEM((size_y, size_x, lanes), jnp.float32),
        ],
        compiler_params=grant(12),
        name="filter",
    )(*map(jnp.asarray, tables), before, after, own)

    returned, potential = pl.pallas_call(
        functools.partial(
            potential_kernel, capacity, chunks, atom_orb, float(tile_points) ** (-0.5), 2 * piece
        ),
        out_shape=(
            bf16(tile_count, capacity, atom_orb, list_orb),
            f32(size_x, size_y, size_z),
        ),
        in_specs=[VMEM_SPEC] * 5,
        out_specs=(VMEM_SPEC, HBM_SPEC),
        scratch_shapes=[
            pltpu.VMEM((list_orb, list_orb), jnp.float32),
            pltpu.SMEM((1, slots), jnp.int32),
            pltpu.SemaphoreType.DMA((2,)),
        ],
        compiler_params=grant(20),
        name="potential",
    )(places, potential, field, near, far)
    back = lax.all_to_all(returned, ("gx", "gy"), split_axis=0, concat_axis=0, tiled=True)
    own_rows = pl.pallas_call(
        functools.partial(unpack_kernel, tile_count),
        out_shape=bf16(slab_count, atom_orb, list_orb),
        in_specs=[SMEM_SPEC, VMEM_SPEC],
        out_specs=HBM_SPEC,
        scratch_shapes=[counts, pltpu.SemaphoreType.DMA((1,))],
        compiler_params=grant(4),
        name="unpack",
    )(slab_tile, back)
    return (potential, own_rows)


def solution(mesh):
    placed = (
        P("gx", "gy", "gz", None),
        P(("gx", "gy", "gz"), None, None),
        P(("gx", "gy", "gz")),
        P(("gx", "gy", "gz")),
    )

    return jax.shard_map(
        local,
        mesh=mesh,
        in_specs=placed,
        out_specs=(P("gx", "gy", "gz"), P(("gx", "gy", "gz"), None, None)),
        check_vma=False,
    )
```

```python
import functools
import math

import jax
import jax.numpy as jnp
import numpy as np
from jax import lax
from jax.experimental import pallas as pl
from jax.experimental.pallas import tpu as pltpu
from jax.sharding import PartitionSpec as P


RADIUS = 8
LANES = 128

ALPHAS = (0.012, 0.025, 0.05, 0.1, 0.2, 0.4, 0.8, 1.6)
MIXES = (0.3, 0.3, 0.32, 0.34, 0.36, 0.38, 0.4, 0.42)

VMEM_SPEC = pl.BlockSpec(memory_space=pltpu.VMEM)
SMEM_SPEC = pl.BlockSpec(memory_space=pltpu.SMEM)
HBM_SPEC = pl.BlockSpec(memory_space=pltpu.HBM)


def in_hbm(array):
    return pltpu.with_memory_space_constraint(array, pltpu.HBM)


def grant(mebibytes):
    return pltpu.CompilerParams(vmem_limit_bytes=mebibytes << 20)


def kernel_tables(radius):
    tap_table = [
        [math.exp(-alpha * offset * offset) for offset in range(-radius, radius + 1)]
        for alpha in ALPHAS
    ]
    mix = [
        MIXES[term] / sum((tap * tap for tap in tap_table[term])) ** 1.5
        for term in range(len(ALPHAS))
    ]
    return (tap_table, mix)


def cost(flops, moved_bytes):
    return pl.CostEstimate(flops=flops, bytes_accessed=moved_bytes, transcendentals=0)


def for_each_slab(tile_ref, count_ref, tile_count, slab_count, visit):
    for t in range(tile_count):
        count_ref[t] = 0

    def step(i, carry):
        t = tile_ref[i]
        slot = count_ref[t]
        count_ref[t] = slot + 1
        visit(i, t, slot)
        return carry

    lax.fori_loop(0, slab_count, step, 0, unroll=4)


def pack_kernel(
    capacity, chunks, empty, tile_hbm, place_hbm, slab_hbm, out_ref,
    tile_ref, place_ref, slab_ref, count_ref, label_ref, sems,
):
    copies = [
        pltpu.make_async_copy(tile_hbm, tile_ref, sems.at[0]),
        pltpu.make_async_copy(place_hbm, place_ref, sems.at[1]),
        pltpu.make_async_copy(slab_hbm, slab_ref, sems.at[2]),
    ]
    for copy in copies:
        copy.start()
    tile_count = out_ref.shape[0]
    label_ref[...] = jnp.full(label_ref.shape, empty, jnp.float32)
    out_ref[...] = jnp.zeros(out_ref.shape, out_ref.dtype)
    for copy in copies:
        copy.wait()

    def visit(i, t, slot):
        slab = slab_ref[i]
        for c in range(chunks):
            out_ref[t, slot * chunks + c] = slab[:, c * LANES : (c + 1) * LANES]
        label = place_ref[i].astype(jnp.float32)
        label_ref[t, pl.ds(slot, 1), :] = jnp.full((1, LANES), label, jnp.float32)

    for_each_slab(tile_ref, count_ref, tile_count, slab_ref.shape[0], visit)
    out_ref[:, capacity * chunks] = label_ref[...].astype(jnp.bfloat16)


def odd_row():
    return lax.rem(lax.axis_index("gy"), 2)


def turn_kernel(planes, values_hbm, near_ref, far_hbm, values_ref, far_ref, sems, out_sem):
    points = values_ref.shape[0]
    plane = points // planes
    half = plane // 2
    copies = []
    for x in range(0, planes, 2):
        part = slice(x * plane, (x + 2) * plane)
        copies.append(
            pltpu.make_async_copy(values_hbm.at[part], values_ref.at[part], sems.at[x // 2])
        )
        copies[-1].start()
    near_start = odd_row() * half
    for x in range(0, planes, 2):
        copies[x // 2].wait()
        for start, out_ref in ((near_start, near_ref), (half - near_start, far_ref)):
            rows = [
                values_ref[pl.ds(pl.multiple_of((x + i) * plane + start, half), half), :]
                for i in range(2)
            ]
            out_ref[:, x * half : (x + 2) * half] = jnp.concatenate(rows, axis=0).T
    copy = pltpu.make_async_copy(far_ref, far_hbm, out_sem.at[0])
    copy.start()
    copy.wait()


def arrange(capacity, chunks, arrived_ref, place_ref, wide_ref, turned_ref):
    tile_count, _, rows, _ = arrived_ref.shape
    slots = tile_count * capacity
    labels = arrived_ref[:, capacity * chunks].astype(jnp.float32)[:, :capacity]
    labels = labels.reshape(slots, LANES)
    width = place_ref.shape[1]
    for g in range(width // LANES):
        group = labels[g * LANES : (g + 1) * LANES]
        here = lax.broadcasted_iota(jnp.int32, group.shape, 0) == lax.broadcasted_iota(
            jnp.int32, group.shape, 1
        )
        place_ref[:, g * LANES : (g + 1) * LANES] = jnp.sum(
            jnp.where(here, group, 0.0), axis=0, keepdims=True
        ).astype(jnp.int32)
    first_row = jnp.broadcast_to(labels.reshape(slots, 1, LANES) * rows, (slots, rows, LANES))
    source = first_row + lax.broadcasted_iota(jnp.int32, (slots, rows, LANES), 1).astype(
        jnp.float32
    )
    lane = lax.broadcasted_iota(jnp.int32, (slots, rows, LANES), 2).astype(jnp.float32)
    hot = []
    for c in range(chunks):
        match = jnp.where(source == lane + float(c * LANES), 1.0, 0.0)
        hot.append(match.reshape(slots * rows, LANES).astype(jnp.bfloat16))
    hot = jnp.concatenate(hot, axis=1)
    for c in range(chunks):
        for t in range(tile_count):
            for k in range(capacity):
                row = (t * capacity + k) * rows
                wide_ref[row : row + rows, :] = arrived_ref[t, k * chunks + c].astype(jnp.float32)
        across = wide_ref[...].T.astype(jnp.bfloat16)
        turned_ref[c * LANES : (c + 1) * LANES, :] = jnp.dot(
            across, hot, preferred_element_type=jnp.float32
        ).astype(jnp.bfloat16)


def half_density(piece, turned_ref, values_ref, out_ref):
    half = out_ref.shape[1]
    for q in range(values_ref.shape[1] // piece):
        block = values_ref[:, q * piece : (q + 1) * piece]
        mixed = jnp.dot(turned_ref[...], block, preferred_element_type=jnp.float32)
        density = jnp.sum(mixed * block.astype(jnp.float32), axis=0, keepdims=True)
        for p in range(piece // half):
            row = q * (piece // half) + p
            out_ref[row : row + 1, :] = density[:, p * half : (p + 1) * half]


def near_kernel(
    capacity, chunks, piece, arrived_ref, near_ref, far_hbm,
    out_ref, place_ref, turned_ref, far_ref, wide_ref, sem,
):
    copy = pltpu.make_async_copy(far_hbm, far_ref, sem.at[0])
    copy.start()
    arrange(capacity, chunks, arrived_ref, place_ref, wide_ref, turned_ref)
    half_density(piece, turned_ref, near_ref, out_ref)
    copy.wait()


def far_kernel(piece, turned_ref, far_ref, out_ref):
    half_density(piece, turned_ref, far_ref, out_ref)


def join_kernel(near_ref, far_ref, wrap_ref, pair_ref, out_ref, top_ref, bottom_ref):
    half = near_ref.shape[1]
    odd = odd_row() == 1
    blocks = (
        jnp.where(odd, pair_ref[...], wrap_ref[...]),
        jnp.where(odd, far_ref[...], near_ref[...]),
        jnp.where(odd, near_ref[...], far_ref[...]),
        jnp.where(odd, wrap_ref[...], pair_ref[...]),
    )
    for i, block in enumerate(blocks):
        out_ref[:, i * half : (i + 1) * half] = block
    top_ref[...] = out_ref[: top_ref.shape[0], :]
    bottom_ref[...] = out_ref[out_ref.shape[0] - bottom_ref.shape[0] :, :]


def split_dot(left, high, low):
    left_high = left.astype(jnp.bfloat16)
    left_low = (left - left_high.astype(jnp.float32)).astype(jnp.bfloat16)
    out = jnp.dot(left_high, high, preferred_element_type=jnp.float32)
    out = out + jnp.dot(left_low, high, preferred_element_type=jnp.float32)
    return out + jnp.dot(left_high, low, preferred_element_type=jnp.float32)


def filter_kernel(parts, *refs):
    taps_ref, band_high, band_low, fold_high, fold_low = refs[:5]
    blocks = refs[5 : 5 + 3 * parts]
    out_ref, field_ref, grid_ref, first_ref, second_ref, third_ref = refs[5 + 3 * parts :]
    size_x, size_y, size_z = out_ref.shape
    wide_y, wide_x, lanes = first_ref.shape
    for part in range(parts):
        start = 0
        for block in blocks[3 * part : 3 * part + 3]:
            rows = block.shape[0]
            for y in range(wide_y):
                grid_ref[y, start : start + rows, part * size_z : (part + 1) * size_z] = block[
                    :, y * size_z : (y + 1) * size_z
                ]
            start += rows
    grid = grid_ref[...].reshape(wide_y * wide_x, parts * size_z)
    first_ref[...] = split_dot(grid, band_high[...], band_low[...]).reshape(wide_y, wide_x, lanes)

    def tap(distance, rows):
        return jnp.broadcast_to(taps_ref[distance : distance + 1, :], (rows, lanes))

    def smooth(y, carry):
        run = tap(0, wide_x) * first_ref[y + RADIUS]
        for d in range(1, RADIUS + 1):
            pair = first_ref[y + (RADIUS - d)] + first_ref[y + (RADIUS + d)]
            run = run + tap(d, wide_x) * pair
        second_ref[y] = run
        run = tap(0, size_x) * second_ref[y, RADIUS : RADIUS + size_x, :]
        for d in range(1, RADIUS + 1):
            pair = (
                second_ref[y, RADIUS - d : RADIUS - d + size_x, :]
                + second_ref[y, RADIUS + d : RADIUS + d + size_x, :]
            )
            run = run + tap(d, size_x) * pair
        third_ref[y] = run
        return carry

    lax.fori_loop(0, size_y, smooth, 0, unroll=4)
    filtered = third_ref[...].reshape(size_y * size_x, lanes)
    folded = split_dot(filtered, fold_high[...], fold_low[...]).reshape(size_y, size_x, size_z)
    for y in range(size_y):
        out_ref[:, y, :] = folded[y]
        field_ref[:, y * size_z : (y + 1) * size_z] = folded[y]


def potential_kernel(
    capacity, chunks, rows, weight, piece, place_vmem, field_ref, near_ref, far_ref,
    out_ref, total_ref, place_ref, sem,
):
    copy = pltpu.make_async_copy(place_vmem, place_ref, sem.at[0])
    copy.start()
    list_orb, points = near_ref.shape
    half = field_ref.shape[1] // 2
    odd = odd_row() == 1
    low, high = field_ref[:, :half] * weight, field_ref[:, half:] * weight
    first = True
    for values_ref, source in (
        (near_ref, jnp.where(odd, high, low)),
        (far_ref, jnp.where(odd, low, high)),
    ):
        for q in range(points // piece):
            field = jnp.concatenate(
                [
                    source[x : x + 1, :]
                    for x in range(q * piece // half, (q + 1) * piece // half)
                ],
                axis=1,
            )
            block = values_ref[:, q * piece : (q + 1) * piece]
            weighted = (field * block.astype(jnp.float32)).astype(jnp.bfloat16)
            term = lax.dot_general(
                block, weighted, (((1,), (1,)), ((), ())), preferred_element_type=jnp.float32
            )
            total_ref[...] = term if first else total_ref[...] + term
            first = False

    copy.wait()
    last = list_orb // rows - 1

    def visit(j, carry):
        t, k = j // capacity, j % capacity
        row = pl.multiple_of(jnp.minimum(place_ref[0, j], last) * rows, rows)
        for c in range(chunks):
            lanes = slice(c * LANES, (c + 1) * LANES)
            out_ref[t, k, :, lanes] = total_ref[pl.ds(row, rows), lanes].astype(jnp.bfloat16)
        return carry

    lax.fori_loop(0, out_ref.shape[0] * capacity, visit, 0, unroll=4)


def write_kernel(grid_ref, grid_hbm, sem):
    copy = pltpu.make_async_copy(grid_ref, grid_hbm, sem.at[0])
    copy.start()
    copy.wait()


def unpack_kernel(tile_count, tile_ref, back_ref, out_hbm, count_ref, sem):
    def visit(i, t, slot):
        pltpu.make_async_copy(back_ref.at[t, slot], out_hbm.at[i], sem.at[0]).start()

    for_each_slab(tile_ref, count_ref, tile_count, out_hbm.shape[0], visit)
    pltpu.make_async_copy(out_hbm, out_hbm, sem.at[0]).wait()


def moved(block, shifts):
    axes = tuple(shifts)
    sizes = [lax.axis_size(axis) for axis in axes]
    pairs = []
    for source in np.ndindex(*sizes):
        target = [(s + shifts[axis]) % n for s, axis, n in zip(source, axes, sizes)]
        pairs.append(
            (int(np.ravel_multi_index(source, sizes)), int(np.ravel_multi_index(target, sizes)))
        )
    return lax.ppermute(block, axes, pairs)


def band_tables(size_z, neighbours):
    tap_table, mix = kernel_tables(RADIUS)

    def band(shift):
        table = np.zeros((size_z, len(ALPHAS), size_z), np.float64)
        for m in range(len(ALPHAS)):
            for source in range(size_z):
                for target in range(size_z):
                    offset = source + shift - target
                    if abs(offset) <= RADIUS:
                        table[source, m, target] = tap_table[m][offset + RADIUS]
        return table.reshape(size_z, len(ALPHAS) * size_z)

    own, low, high = band(0), band(-size_z), band(size_z)
    bands = {0: [own + low + high], 1: [own, low + high], 2: [own, low, high]}[neighbours]
    taps = np.zeros((16, len(ALPHAS) * size_z), np.float64)
    for d in range(RADIUS + 1):
        taps[d] = np.repeat([row[RADIUS + d] for row in tap_table], size_z)
    fold = np.concatenate([mix[m] * np.eye(size_z) for m in range(len(ALPHAS))], axis=0)

    def split(table):
        high = table.astype(np.float32).astype(jnp.bfloat16)
        low = (table - high.astype(np.float64)).astype(np.float32).astype(jnp.bfloat16)
        return [high, low]

    return [taps.astype(np.float32), *split(np.concatenate(bands, axis=0)), *split(fold)]


def local(orbital_values, dm_slabs, slab_tile, slab_place):
    size_x, size_y, size_z, list_orb = orbital_values.shape
    slab_count, atom_orb, _ = dm_slabs.shape
    list_blk = list_orb // atom_orb
    tile_count = lax.axis_size("gx") * lax.axis_size("gy")
    capacity = max(2, 2 * ((list_blk + tile_count - 1) // tile_count))
    chunks = list_orb // LANES
    tile_points = size_x * size_y * size_z
    plane = size_y * size_z
    counts = pltpu.SMEM((tile_count,), jnp.int32)

    packed = pl.pallas_call(
        functools.partial(pack_kernel, capacity, chunks, float(list_blk)),
        out_shape=jax.ShapeDtypeStruct(
            (tile_count, capacity * chunks + 1, atom_orb, LANES), jnp.bfloat16
        ),
        in_specs=[HBM_SPEC] * 3,
        out_specs=VMEM_SPEC,
        scratch_shapes=[
            pltpu.SMEM((slab_count,), jnp.int32),
            pltpu.SMEM((slab_count,), jnp.int32),
            pltpu.VMEM(dm_slabs.shape, dm_slabs.dtype),
            counts,
            pltpu.VMEM((tile_count, atom_orb, LANES), jnp.float32),
            pltpu.SemaphoreType.DMA((3,)),
        ],
        compiler_params=grant(4),
        name="pack",
    )(in_hbm(slab_tile), in_hbm(slab_place), in_hbm(dm_slabs))
    arrived = lax.all_to_all(packed, ("gx", "gy"), split_axis=0, concat_axis=0, tiled=True)
    half = plane // 2
    half_points = tile_points // 2
    piece = 4 * half
    bf16 = lambda *shape: jax.ShapeDtypeStruct(shape, jnp.bfloat16)
    f32 = lambda *shape: jax.ShapeDtypeStruct(shape, jnp.float32)
    near, far = pl.pallas_call(
        functools.partial(turn_kernel, size_x),
        out_shape=(
            pltpu.VMEM((list_orb, half_points), jnp.bfloat16),
            bf16(list_orb, half_points),
        ),
        in_specs=[HBM_SPEC],
        out_specs=(VMEM_SPEC, HBM_SPEC),
        scratch_shapes=[
            pltpu.VMEM((tile_points, list_orb), jnp.bfloat16),
            pltpu.VMEM((list_orb, half_points), jnp.bfloat16),
            pltpu.SemaphoreType.DMA((size_x // 2,)),
            pltpu.SemaphoreType.DMA((1,)),
        ],
        compiler_params=grant(20),
        cost_estimate=cost(0, 4 * tile_points * list_orb),
        name="turn",
    )(in_hbm(orbital_values.reshape(tile_points, list_orb)))

    slots = LANES * ((tile_count * capacity + LANES - 1) // LANES)
    product = 2 * half_points * list_orb * list_orb
    near_y, places, matrix, far = pl.pallas_call(
        functools.partial(near_kernel, capacity, chunks, piece),
        out_shape=(
            f32(size_x, half),
            jax.ShapeDtypeStruct((1, slots), jnp.int32),
            bf16(list_orb, list_orb),
            pltpu.VMEM((list_orb, half_points), jnp.bfloat16),
        ),
        in_specs=[VMEM_SPEC, VMEM_SPEC, HBM_SPEC],
        out_specs=(VMEM_SPEC,) * 4,
        scratch_shapes=[
            pltpu.VMEM((tile_count * capacity * atom_orb, LANES), jnp.float32),
            pltpu.SemaphoreType.DMA((1,)),
        ],
        compiler_params=grant(20),
        cost_estimate=cost(product, 2 * half_points * list_orb),
        name="near",
    )(arrived, near, in_hbm(far))
    rows = lax.axis_size("gy")
    pair = [(i, i ^ 1) for i in range(rows)]
    wrap = [(i, (i - 1 + 2 * (i % 2)) % rows) for i in range(rows)]
    from_wrap = lax.ppermute(near_y, "gy", wrap)
    far_y = pl.pallas_call(
        functools.partial(far_kernel, piece),
        out_shape=f32(size_x, half),
        in_specs=[VMEM_SPEC, VMEM_SPEC],
        out_specs=VMEM_SPEC,
        compiler_params=grant(20),
        cost_estimate=cost(product, 2 * half_points * list_orb),
        name="far",
    )(matrix, far)
    from_pair = lax.ppermute(far_y, "gy", pair)

    wide = 2 * plane
    own, top, bottom = pl.pallas_call(
        join_kernel,
        out_shape=(f32(size_x, wide), f32(RADIUS, wide), f32(RADIUS, wide)),
        in_specs=[VMEM_SPEC] * 4,
        out_specs=(VMEM_SPEC,) * 3,
        compiler_params=grant(2),
        name="join",
    )(near_y, far_y, from_wrap, from_pair)
    layers = lax.axis_size("gz")
    blocks = []
    for shift in {1: [0], 2: [0, 1]}.get(layers, [0, 1, -1]):
        blocks.append(moved(bottom, {"gx": 1, "gz": shift}))
        blocks.append(moved(own, {"gz": shift}) if shift else own)
        blocks.append(moved(top, {"gx": -1, "gz": shift}))
    parts = len(blocks) // 3
    tables = band_tables(size_z, parts - 1)
    lanes = tables[0].shape[1]
    wide_x, wide_y = size_x + 2 * RADIUS, size_y + 2 * RADIUS
    potential, field = pl.pallas_call(
        functools.partial(filter_kernel, parts),
        out_shape=(pltpu.VMEM((size_x, size_y, size_z), jnp.float32), f32(size_x, plane)),
        in_specs=[VMEM_SPEC] * (len(tables) + len(blocks)),
        out_specs=(VMEM_SPEC,) * 2,
        scratch_shapes=[
            pltpu.VMEM((wide_y, wide_x, parts * size_z), jnp.float32),
            pltpu.VMEM((wide_y, wide_x, lanes), jnp.float32),
            pltpu.VMEM((size_y, wide_x, lanes), jnp.float32),
            pltpu.VMEM((size_y, size_x, lanes), jnp.float32),
        ],
        compiler_params=grant(12),
        name="filter",
    )(*map(jnp.asarray, tables), *blocks)

    returned = pl.pallas_call(
        functools.partial(
            potential_kernel, capacity, chunks, atom_orb, float(tile_points) ** (-0.5), 2 * piece
        ),
        out_shape=bf16(tile_count, capacity, atom_orb, list_orb),
        in_specs=[VMEM_SPEC] * 4,
        out_specs=VMEM_SPEC,
        scratch_shapes=[
            pltpu.VMEM((list_orb, list_orb), jnp.float32),
            pltpu.SMEM((1, slots), jnp.int32),
            pltpu.SemaphoreType.DMA((1,)),
        ],
        compiler_params=grant(20),
        name="potential",
    )(places, field, near, far)
    back = lax.all_to_all(returned, ("gx", "gy"), split_axis=0, concat_axis=0, tiled=True)
    potential = pl.pallas_call(
        write_kernel,
        out_shape=f32(size_x, size_y, size_z),
        in_specs=[VMEM_SPEC],
        out_specs=HBM_SPEC,
        scratch_shapes=[pltpu.SemaphoreType.DMA((1,))],
        compiler_params=grant(2),
        name="write",
    )(potential)
    own_rows = pl.pallas_call(
        functools.partial(unpack_kernel, tile_count),
        out_shape=bf16(slab_count, atom_orb, list_orb),
        in_specs=[SMEM_SPEC, VMEM_SPEC],
        out_specs=HBM_SPEC,
        scratch_shapes=[counts, pltpu.SemaphoreType.DMA((1,))],
        compiler_params=grant(4),
        name="unpack",
    )(slab_tile, back)
    return (potential, own_rows)


def solution(mesh):
    placed = (
        P("gx", "gy", "gz", None),
        P(("gx", "gy", "gz"), None, None),
        P(("gx", "gy", "gz")),
        P(("gx", "gy", "gz")),
    )

    return jax.shard_map(
        local,
        mesh=mesh,
        in_specs=placed,
        out_specs=(P("gx", "gy", "gz"), P(("gx", "gy", "gz"), None, None)),
        check_vma=False,
    )
```

```python
import functools
import math

import jax
import jax.numpy as jnp
import numpy as np
from jax import lax
from jax.experimental import pallas as pl
from jax.experimental.pallas import tpu as pltpu
from jax.sharding import PartitionSpec as P


RADIUS = 8
LANES = 128

ALPHAS = (0.012, 0.025, 0.05, 0.1, 0.2, 0.4, 0.8, 1.6)
MIXES = (0.3, 0.3, 0.32, 0.34, 0.36, 0.38, 0.4, 0.42)

VMEM_SPEC = pl.BlockSpec(memory_space=pltpu.VMEM)
SMEM_SPEC = pl.BlockSpec(memory_space=pltpu.SMEM)
HBM_SPEC = pl.BlockSpec(memory_space=pltpu.HBM)


def in_hbm(array):
    return pltpu.with_memory_space_constraint(array, pltpu.HBM)


def grant(mebibytes):
    return pltpu.CompilerParams(vmem_limit_bytes=mebibytes << 20)


def kernel_tables(radius):
    tap_table = [
        [math.exp(-alpha * offset * offset) for offset in range(-radius, radius + 1)]
        for alpha in ALPHAS
    ]
    mix = [
        MIXES[term] / sum((tap * tap for tap in tap_table[term])) ** 1.5
        for term in range(len(ALPHAS))
    ]
    return (tap_table, mix)


def cost(flops, moved_bytes):
    return pl.CostEstimate(flops=flops, bytes_accessed=moved_bytes, transcendentals=0)


def for_each_slab(tile_ref, count_ref, tile_count, slab_count, visit):
    for t in range(tile_count):
        count_ref[t] = 0

    def step(i, carry):
        t = tile_ref[i]
        slot = count_ref[t]
        count_ref[t] = slot + 1
        visit(i, t, slot)
        return carry

    lax.fori_loop(0, slab_count, step, 0, unroll=4)


def pack_kernel(
    capacity, chunks, empty, tile_hbm, place_hbm, slab_hbm, out_ref,
    tile_ref, place_ref, slab_ref, count_ref, label_ref, sems,
):
    copies = [
        pltpu.make_async_copy(tile_hbm, tile_ref, sems.at[0]),
        pltpu.make_async_copy(place_hbm, place_ref, sems.at[1]),
        pltpu.make_async_copy(slab_hbm, slab_ref, sems.at[2]),
    ]
    for copy in copies:
        copy.start()
    tile_count = out_ref.shape[0]
    label_ref[...] = jnp.full(label_ref.shape, empty, jnp.float32)
    out_ref[...] = jnp.zeros(out_ref.shape, out_ref.dtype)
    for copy in copies:
        copy.wait()

    def visit(i, t, slot):
        slab = slab_ref[i]
        for c in range(chunks):
            out_ref[t, slot * chunks + c] = slab[:, c * LANES : (c + 1) * LANES]
        label = place_ref[i].astype(jnp.float32)
        label_ref[t, pl.ds(slot, 1), :] = jnp.full((1, LANES), label, jnp.float32)

    for_each_slab(tile_ref, count_ref, tile_count, slab_ref.shape[0], visit)
    out_ref[:, capacity * chunks] = label_ref[...].astype(jnp.bfloat16)


def odd_row():
    return lax.rem(lax.axis_index("gy"), 2)


def turn_kernel(planes, values_hbm, near_ref, far_hbm, values_ref, far_ref, sems, out_sem):
    points = values_ref.shape[0]
    plane = points // planes
    half = plane // 2
    copies = []
    for x in range(0, planes, 2):
        part = slice(x * plane, (x + 2) * plane)
        copies.append(
            pltpu.make_async_copy(values_hbm.at[part], values_ref.at[part], sems.at[x // 2])
        )
        copies[-1].start()
    near_start = odd_row() * half
    for x in range(0, planes, 2):
        copies[x // 2].wait()
        for start, out_ref in ((near_start, near_ref), (half - near_start, far_ref)):
            rows = [
                values_ref[pl.ds(pl.multiple_of((x + i) * plane + start, half), half), :]
                for i in range(2)
            ]
            out_ref[:, x * half : (x + 2) * half] = jnp.concatenate(rows, axis=0).T
    copy = pltpu.make_async_copy(far_ref, far_hbm, out_sem.at[0])
    copy.start()
    copy.wait()


def arrange(capacity, chunks, arrived_ref, place_ref, wide_ref, turned_ref):
    tile_count, _, rows, _ = arrived_ref.shape
    slots = tile_count * capacity
    labels = arrived_ref[:, capacity * chunks].astype(jnp.float32)[:, :capacity]
    labels = labels.reshape(slots, LANES)
    width = place_ref.shape[1]
    for g in range(width // LANES):
        group = labels[g * LANES : (g + 1) * LANES]
        here = lax.broadcasted_iota(jnp.int32, group.shape, 0) == lax.broadcasted_iota(
            jnp.int32, group.shape, 1
        )
        place_ref[:, g * LANES : (g + 1) * LANES] = jnp.sum(
            jnp.where(here, group, 0.0), axis=0, keepdims=True
        ).astype(jnp.int32)
    first_row = jnp.broadcast_to(labels.reshape(slots, 1, LANES) * rows, (slots, rows, LANES))
    source = first_row + lax.broadcasted_iota(jnp.int32, (slots, rows, LANES), 1).astype(
        jnp.float32
    )
    lane = lax.broadcasted_iota(jnp.int32, (slots, rows, LANES), 2).astype(jnp.float32)
    hot = []
    for c in range(chunks):
        match = jnp.where(source == lane + float(c * LANES), 1.0, 0.0)
        hot.append(match.reshape(slots * rows, LANES).astype(jnp.bfloat16))
    hot = jnp.concatenate(hot, axis=1)
    for c in range(chunks):
        for t in range(tile_count):
            for k in range(capacity):
                row = (t * capacity + k) * rows
                wide_ref[row : row + rows, :] = arrived_ref[t, k * chunks + c].astype(jnp.float32)
        across = wide_ref[...].T.astype(jnp.bfloat16)
        turned_ref[c * LANES : (c + 1) * LANES, :] = jnp.dot(
            across, hot, preferred_element_type=jnp.float32
        ).astype(jnp.bfloat16)


def half_density(piece, turned_ref, values_ref, out_ref):
    half = out_ref.shape[1]
    for q in range(values_ref.shape[1] // piece):
        block = values_ref[:, q * piece : (q + 1) * piece]
        mixed = jnp.dot(turned_ref[...], block, preferred_element_type=jnp.float32)
        density = jnp.sum(mixed * block.astype(jnp.float32), axis=0, keepdims=True)
        for p in range(piece // half):
            row = q * (piece // half) + p
            out_ref[row : row + 1, :] = density[:, p * half : (p + 1) * half]


def near_kernel(
    capacity, chunks, piece, arrived_ref, near_ref, far_hbm,
    out_ref, place_ref, turned_ref, far_ref, wide_ref, sem,
):
    copy = pltpu.make_async_copy(far_hbm, far_ref, sem.at[0])
    copy.start()
    arrange(capacity, chunks, arrived_ref, place_ref, wide_ref, turned_ref)
    half_density(piece, turned_ref, near_ref, out_ref)
    copy.wait()


def far_kernel(piece, turned_ref, far_ref, out_ref):
    half_density(piece, turned_ref, far_ref, out_ref)


def join_kernel(near_ref, far_ref, wrap_ref, pair_ref, out_ref, top_ref, bottom_ref):
    half = near_ref.shape[1]
    odd = odd_row() == 1
    blocks = (
        jnp.where(odd, pair_ref[...], wrap_ref[...]),
        jnp.where(odd, far_ref[...], near_ref[...]),
        jnp.where(odd, near_ref[...], far_ref[...]),
        jnp.where(odd, wrap_ref[...], pair_ref[...]),
    )
    for i, block in enumerate(blocks):
        out_ref[:, i * half : (i + 1) * half] = block
    top_ref[...] = out_ref[: top_ref.shape[0], :]
    bottom_ref[...] = out_ref[out_ref.shape[0] - bottom_ref.shape[0] :, :]


def split_dot(left, high, low):
    left_high = left.astype(jnp.bfloat16)
    left_low = (left - left_high.astype(jnp.float32)).astype(jnp.bfloat16)
    out = jnp.dot(left_high, high, preferred_element_type=jnp.float32)
    out = out + jnp.dot(left_low, high, preferred_element_type=jnp.float32)
    return out + jnp.dot(left_high, low, preferred_element_type=jnp.float32)


def filter_kernel(parts, *refs):
    taps_ref, band_high, band_low, fold_high, fold_low = refs[:5]
    blocks = refs[5 : 5 + 3 * parts]
    out_ref, field_ref, grid_ref, first_ref, second_ref, third_ref = refs[5 + 3 * parts :]
    size_x, size_y, size_z = out_ref.shape
    wide_y, wide_x, lanes = first_ref.shape
    for part in range(parts):
        start = 0
        for block in blocks[3 * part : 3 * part + 3]:
            rows = block.shape[0]
            for y in range(wide_y):
                grid_ref[y, start : start + rows, part * size_z : (part + 1) * size_z] = block[
                    :, y * size_z : (y + 1) * size_z
                ]
            start += rows
    grid = grid_ref[...].reshape(wide_y * wide_x, parts * size_z)
    first_ref[...] = split_dot(grid, band_high[...], band_low[...]).reshape(wide_y, wide_x, lanes)

    def tap(distance, rows):
        return jnp.broadcast_to(taps_ref[distance : distance + 1, :], (rows, lanes))

    def smooth(y, carry):
        run = tap(0, wide_x) * first_ref[y + RADIUS]
        for d in range(1, RADIUS + 1):
            pair = first_ref[y + (RADIUS - d)] + first_ref[y + (RADIUS + d)]
            run = run + tap(d, wide_x) * pair
        second_ref[y] = run
        run = tap(0, size_x) * second_ref[y, RADIUS : RADIUS + size_x, :]
        for d in range(1, RADIUS + 1):
            pair = (
                second_ref[y, RADIUS - d : RADIUS - d + size_x, :]
                + second_ref[y, RADIUS + d : RADIUS + d + size_x, :]
            )
            run = run + tap(d, size_x) * pair
        third_ref[y] = run
        return carry

    lax.fori_loop(0, size_y, smooth, 0, unroll=4)
    filtered = third_ref[...].reshape(size_y * size_x, lanes)
    folded = split_dot(filtered, fold_high[...], fold_low[...]).reshape(size_y, size_x, size_z)
    for y in range(size_y):
        out_ref[:, y, :] = folded[y]
        field_ref[:, y * size_z : (y + 1) * size_z] = folded[y]


def potential_kernel(
    capacity, weight, piece, place_vmem, grid_ref, field_ref, near_ref, far_ref,
    out_ref, grid_hbm, right_ref, corner_ref, whole_ref, place_ref, sems,
):
    copies = [
        pltpu.make_async_copy(place_vmem, place_ref, sems.at[0]),
        pltpu.make_async_copy(grid_ref, grid_hbm, sems.at[1]),
    ]
    for copy in copies:
        copy.start()
    points = near_ref.shape[1]
    half = field_ref.shape[1] // 2
    odd = odd_row() == 1
    low, high = field_ref[:, :half] * weight, field_ref[:, half:] * weight
    first = True
    over_points = (((1,), (1,)), ((), ()))
    for values_ref, source in (
        (near_ref, jnp.where(odd, high, low)),
        (far_ref, jnp.where(odd, low, high)),
    ):
        for q in range(points // piece):
            field = jnp.concatenate(
                [
                    source[x : x + 1, :]
                    for x in range(q * piece // half, (q + 1) * piece // half)
                ],
                axis=1,
            )
            block = values_ref[:, q * piece : (q + 1) * piece]
            weighted = (field * block.astype(jnp.float32)).astype(jnp.bfloat16)
            right = lax.dot_general(
                block, weighted[LANES:], over_points, preferred_element_type=jnp.float32
            )
            corner = lax.dot_general(
                block[:LANES], weighted[:LANES], over_points, preferred_element_type=jnp.float32
            )
            right_ref[...] = right if first else right_ref[...] + right
            corner_ref[...] = corner if first else corner_ref[...] + corner
            first = False

    blocks, rows, _ = whole_ref.shape
    edge = LANES // rows
    whole_ref[:edge, :, :LANES] = corner_ref[...].reshape(edge, rows, -1).astype(jnp.bfloat16)
    whole_ref[edge:, :, :LANES] = (
        right_ref[:LANES].T.reshape(blocks - edge, rows, -1).astype(jnp.bfloat16)
    )
    whole_ref[:, :, LANES:] = right_ref[...].reshape(blocks, rows, -1).astype(jnp.bfloat16)
    for copy in copies:
        copy.wait()

    def visit(j, carry):
        t, k = j // capacity, j % capacity
        out_ref[t, k] = whole_ref[jnp.minimum(place_ref[0, j], blocks - 1)]
        return carry

    lax.fori_loop(0, out_ref.shape[0] * capacity, visit, 0, unroll=16)


def unpack_kernel(tile_count, tile_ref, back_ref, out_hbm, count_ref, sem):
    def visit(i, t, slot):
        pltpu.make_async_copy(back_ref.at[t, slot], out_hbm.at[i], sem.at[0]).start()

    for_each_slab(tile_ref, count_ref, tile_count, out_hbm.shape[0], visit)
    pltpu.make_async_copy(out_hbm, out_hbm, sem.at[0]).wait()


def moved(block, shifts):
    axes = tuple(shifts)
    sizes = [lax.axis_size(axis) for axis in axes]
    pairs = []
    for source in np.ndindex(*sizes):
        target = [(s + shifts[axis]) % n for s, axis, n in zip(source, axes, sizes)]
        pairs.append(
            (int(np.ravel_multi_index(source, sizes)), int(np.ravel_multi_index(target, sizes)))
        )
    return lax.ppermute(block, axes, pairs)


def band_tables(size_z, neighbours):
    tap_table, mix = kernel_tables(RADIUS)

    def band(shift):
        table = np.zeros((size_z, len(ALPHAS), size_z), np.float64)
        for m in range(len(ALPHAS)):
            for source in range(size_z):
                for target in range(size_z):
                    offset = source + shift - target
                    if abs(offset) <= RADIUS:
                        table[source, m, target] = tap_table[m][offset + RADIUS]
        return table.reshape(size_z, len(ALPHAS) * size_z)

    own, low, high = band(0), band(-size_z), band(size_z)
    bands = {0: [own + low + high], 1: [own, low + high], 2: [own, low, high]}[neighbours]
    taps = np.zeros((16, len(ALPHAS) * size_z), np.float64)
    for d in range(RADIUS + 1):
        taps[d] = np.repeat([row[RADIUS + d] for row in tap_table], size_z)
    fold = np.concatenate([mix[m] * np.eye(size_z) for m in range(len(ALPHAS))], axis=0)

    def split(table):
        high = table.astype(np.float32).astype(jnp.bfloat16)
        low = (table - high.astype(np.float64)).astype(np.float32).astype(jnp.bfloat16)
        return [high, low]

    return [taps.astype(np.float32), *split(np.concatenate(bands, axis=0)), *split(fold)]


def local(orbital_values, dm_slabs, slab_tile, slab_place):
    size_x, size_y, size_z, list_orb = orbital_values.shape
    slab_count, atom_orb, _ = dm_slabs.shape
    list_blk = list_orb // atom_orb
    tile_count = lax.axis_size("gx") * lax.axis_size("gy")
    capacity = max(2, 2 * ((list_blk + tile_count - 1) // tile_count))
    chunks = list_orb // LANES
    tile_points = size_x * size_y * size_z
    plane = size_y * size_z
    counts = pltpu.SMEM((tile_count,), jnp.int32)

    packed = pl.pallas_call(
        functools.partial(pack_kernel, capacity, chunks, float(list_blk)),
        out_shape=jax.ShapeDtypeStruct(
            (tile_count, capacity * chunks + 1, atom_orb, LANES), jnp.bfloat16
        ),
        in_specs=[HBM_SPEC] * 3,
        out_specs=VMEM_SPEC,
        scratch_shapes=[
            pltpu.SMEM((slab_count,), jnp.int32),
            pltpu.SMEM((slab_count,), jnp.int32),
            pltpu.VMEM(dm_slabs.shape, dm_slabs.dtype),
            counts,
            pltpu.VMEM((tile_count, atom_orb, LANES), jnp.float32),
            pltpu.SemaphoreType.DMA((3,)),
        ],
        compiler_params=grant(4),
        name="pack",
    )(in_hbm(slab_tile), in_hbm(slab_place), in_hbm(dm_slabs))
    arrived = lax.all_to_all(packed, ("gx", "gy"), split_axis=0, concat_axis=0, tiled=True)
    half = plane // 2
    half_points = tile_points // 2
    piece = 4 * half
    bf16 = lambda *shape: jax.ShapeDtypeStruct(shape, jnp.bfloat16)
    f32 = lambda *shape: jax.ShapeDtypeStruct(shape, jnp.float32)
    near, far = pl.pallas_call(
        functools.partial(turn_kernel, size_x),
        out_shape=(
            pltpu.VMEM((list_orb, half_points), jnp.bfloat16),
            bf16(list_orb, half_points),
        ),
        in_specs=[HBM_SPEC],
        out_specs=(VMEM_SPEC, HBM_SPEC),
        scratch_shapes=[
            pltpu.VMEM((tile_points, list_orb), jnp.bfloat16),
            pltpu.VMEM((list_orb, half_points), jnp.bfloat16),
            pltpu.SemaphoreType.DMA((size_x // 2,)),
            pltpu.SemaphoreType.DMA((1,)),
        ],
        compiler_params=grant(20),
        cost_estimate=cost(0, 4 * tile_points * list_orb),
        name="turn",
    )(in_hbm(orbital_values.reshape(tile_points, list_orb)))

    slots = LANES * ((tile_count * capacity + LANES - 1) // LANES)
    product = 2 * half_points * list_orb * list_orb
    near_y, places, matrix, far = pl.pallas_call(
        functools.partial(near_kernel, capacity, chunks, piece),
        out_shape=(
            f32(size_x, half),
            jax.ShapeDtypeStruct((1, slots), jnp.int32),
            bf16(list_orb, list_orb),
            pltpu.VMEM((list_orb, half_points), jnp.bfloat16),
        ),
        in_specs=[VMEM_SPEC, VMEM_SPEC, HBM_SPEC],
        out_specs=(VMEM_SPEC,) * 4,
        scratch_shapes=[
            pltpu.VMEM((tile_count * capacity * atom_orb, LANES), jnp.float32),
            pltpu.SemaphoreType.DMA((1,)),
        ],
        compiler_params=grant(20),
        cost_estimate=cost(product, 2 * half_points * list_orb),
        name="near",
    )(arrived, near, in_hbm(far))
    rows = lax.axis_size("gy")
    pair = [(i, i ^ 1) for i in range(rows)]
    wrap = [(i, (i - 1 + 2 * (i % 2)) % rows) for i in range(rows)]
    from_wrap = lax.ppermute(near_y, "gy", wrap)
    far_y = pl.pallas_call(
        functools.partial(far_kernel, piece),
        out_shape=f32(size_x, half),
        in_specs=[VMEM_SPEC, VMEM_SPEC],
        out_specs=VMEM_SPEC,
        compiler_params=grant(20),
        cost_estimate=cost(product, 2 * half_points * list_orb),
        name="far",
    )(matrix, far)
    from_pair = lax.ppermute(far_y, "gy", pair)

    wide = 2 * plane
    own, top, bottom = pl.pallas_call(
        join_kernel,
        out_shape=(f32(size_x, wide), f32(RADIUS, wide), f32(RADIUS, wide)),
        in_specs=[VMEM_SPEC] * 4,
        out_specs=(VMEM_SPEC,) * 3,
        compiler_params=grant(2),
        name="join",
    )(near_y, far_y, from_wrap, from_pair)
    layers = lax.axis_size("gz")
    blocks = []
    for shift in {1: [0], 2: [0, 1]}.get(layers, [0, 1, -1]):
        blocks.append(moved(bottom, {"gx": 1, "gz": shift}))
        blocks.append(moved(own, {"gz": shift}) if shift else own)
        blocks.append(moved(top, {"gx": -1, "gz": shift}))
    parts = len(blocks) // 3
    tables = band_tables(size_z, parts - 1)
    lanes = tables[0].shape[1]
    wide_x, wide_y = size_x + 2 * RADIUS, size_y + 2 * RADIUS
    potential, field = pl.pallas_call(
        functools.partial(filter_kernel, parts),
        out_shape=(pltpu.VMEM((size_x, size_y, size_z), jnp.float32), f32(size_x, plane)),
        in_specs=[VMEM_SPEC] * (len(tables) + len(blocks)),
        out_specs=(VMEM_SPEC,) * 2,
        scratch_shapes=[
            pltpu.VMEM((wide_y, wide_x, parts * size_z), jnp.float32),
            pltpu.VMEM((wide_y, wide_x, lanes), jnp.float32),
            pltpu.VMEM((size_y, wide_x, lanes), jnp.float32),
            pltpu.VMEM((size_y, size_x, lanes), jnp.float32),
        ],
        compiler_params=grant(12),
        name="filter",
    )(*map(jnp.asarray, tables), *blocks)

    returned, potential = pl.pallas_call(
        functools.partial(
            potential_kernel, capacity, float(tile_points) ** (-0.5), 2 * piece
        ),
        out_shape=(
            bf16(tile_count, capacity, atom_orb, list_orb),
            f32(size_x, size_y, size_z),
        ),
        in_specs=[VMEM_SPEC] * 5,
        out_specs=(VMEM_SPEC, HBM_SPEC),
        scratch_shapes=[
            pltpu.VMEM((list_orb, list_orb - LANES), jnp.float32),
            pltpu.VMEM((LANES, LANES), jnp.float32),
            pltpu.VMEM((list_blk, atom_orb, list_orb), jnp.bfloat16),
            pltpu.SMEM((1, slots), jnp.int32),
            pltpu.SemaphoreType.DMA((2,)),
        ],
        compiler_params=grant(20),
        name="potential",
    )(places, potential, field, near, far)
    back = lax.all_to_all(returned, ("gx", "gy"), split_axis=0, concat_axis=0, tiled=True)
    own_rows = pl.pallas_call(
        functools.partial(unpack_kernel, tile_count),
        out_shape=bf16(slab_count, atom_orb, list_orb),
        in_specs=[SMEM_SPEC, VMEM_SPEC],
        out_specs=HBM_SPEC,
        scratch_shapes=[counts, pltpu.SemaphoreType.DMA((1,))],
        compiler_params=grant(4),
        name="unpack",
    )(slab_tile, back)
    return (potential, own_rows)


def solution(mesh):
    placed = (
        P("gx", "gy", "gz", None),
        P(("gx", "gy", "gz"), None, None),
        P(("gx", "gy", "gz")),
        P(("gx", "gy", "gz")),
    )

    return jax.shard_map(
        local,
        mesh=mesh,
        in_specs=placed,
        out_specs=(P("gx", "gy", "gz"), P(("gx", "gy", "gz"), None, None)),
        check_vma=False,
    )
```

```python
import functools
import math

import jax
import jax.numpy as jnp
import numpy as np
from jax import lax
from jax.experimental import pallas as pl
from jax.experimental.pallas import tpu as pltpu
from jax.sharding import PartitionSpec as P


RADIUS = 8
LANES = 128

ALPHAS = (0.012, 0.025, 0.05, 0.1, 0.2, 0.4, 0.8, 1.6)
MIXES = (0.3, 0.3, 0.32, 0.34, 0.36, 0.38, 0.4, 0.42)

VMEM_SPEC = pl.BlockSpec(memory_space=pltpu.VMEM)
SMEM_SPEC = pl.BlockSpec(memory_space=pltpu.SMEM)
HBM_SPEC = pl.BlockSpec(memory_space=pltpu.HBM)


def in_hbm(array):
    return pltpu.with_memory_space_constraint(array, pltpu.HBM)


def grant(mebibytes):
    return pltpu.CompilerParams(vmem_limit_bytes=mebibytes << 20)


def kernel_tables(radius):
    tap_table = [
        [math.exp(-alpha * offset * offset) for offset in range(-radius, radius + 1)]
        for alpha in ALPHAS
    ]
    mix = [
        MIXES[term] / sum((tap * tap for tap in tap_table[term])) ** 1.5
        for term in range(len(ALPHAS))
    ]
    return (tap_table, mix)


def cost(flops, moved_bytes):
    return pl.CostEstimate(flops=flops, bytes_accessed=moved_bytes, transcendentals=0)


def for_each_slab(tile_ref, count_ref, tile_count, slab_count, visit):
    for t in range(tile_count):
        count_ref[t] = 0

    def step(i, carry):
        t = tile_ref[i]
        slot = count_ref[t]
        count_ref[t] = slot + 1
        visit(i, t, slot)
        return carry

    lax.fori_loop(0, slab_count, step, 0, unroll=4)


def pack_kernel(
    capacity, chunks, empty, groups, tile_hbm, place_hbm, slab_hbm, out_hbm,
    tile_ref, place_ref, slab_ref, count_ref, index_ref, label_ref, out_ref, sems, out_sems,
):
    copies = [
        pltpu.make_async_copy(tile_hbm, tile_ref, sems.at[0]),
        pltpu.make_async_copy(place_hbm, place_ref, sems.at[1]),
        pltpu.make_async_copy(slab_hbm, slab_ref, sems.at[2]),
    ]
    for copy in copies:
        copy.start()
    tile_count = out_ref.shape[0]
    label_ref[...] = jnp.full(label_ref.shape, empty, jnp.float32)
    for j in range(tile_count * capacity):
        index_ref[j] = 0
    for copy in copies[:2]:
        copy.wait()

    def rank(i, t, slot):
        index_ref[t * capacity + slot] = i
        label = place_ref[i].astype(jnp.float32)
        label_ref[t, pl.ds(slot, 1), :] = jnp.full((1, LANES), label, jnp.float32)

    for_each_slab(tile_ref, count_ref, tile_count, slab_ref.shape[0], rank)
    copies[2].wait()

    def fill(t, carry):
        for k in range(capacity):
            slab = slab_ref[index_ref[t * capacity + k]]
            for c in range(chunks):
                out_ref[t, k * chunks + c] = slab[:, c * LANES : (c + 1) * LANES]
        out_ref[t, capacity * chunks] = label_ref[t].astype(jnp.bfloat16)
        return carry

    share = tile_count // groups
    for g in range(groups):
        lax.fori_loop(g * share, (g + 1) * share, fill, 0, unroll=min(share, 4))
        part = slice(g * share, (g + 1) * share)
        copies.append(pltpu.make_async_copy(out_ref.at[part], out_hbm.at[part], out_sems.at[g]))
        copies[-1].start()
    for copy in copies[3:]:
        copy.wait()


def odd_row():
    return lax.rem(lax.axis_index("gy"), 2)


def turn_kernel(planes, values_hbm, near_ref, far_hbm, values_ref, far_ref, sems, out_sem):
    points = values_ref.shape[0]
    plane = points // planes
    half = plane // 2
    copies = []
    for x in range(0, planes, 2):
        part = slice(x * plane, (x + 2) * plane)
        copies.append(
            pltpu.make_async_copy(values_hbm.at[part], values_ref.at[part], sems.at[x // 2])
        )
        copies[-1].start()
    near_start = odd_row() * half
    for x in range(0, planes, 2):
        copies[x // 2].wait()
        for start, out_ref in ((near_start, near_ref), (half - near_start, far_ref)):
            rows = [
                values_ref[pl.ds(pl.multiple_of((x + i) * plane + start, half), half), :]
                for i in range(2)
            ]
            out_ref[:, x * half : (x + 2) * half] = jnp.concatenate(rows, axis=0).T
    copy = pltpu.make_async_copy(far_ref, far_hbm, out_sem.at[0])
    copy.start()
    copy.wait()


def arrange(capacity, chunks, arrived_ref, place_ref, square_ref, last_ref, wide_ref, turned_ref):
    tile_count, _, rows, _ = arrived_ref.shape
    slots = tile_count * capacity
    labels = arrived_ref[:, capacity * chunks].astype(jnp.float32)[:, :capacity]
    labels = labels.reshape(slots, LANES)
    width = place_ref.shape[1]
    for g in range(width // LANES):
        group = labels[g * LANES : (g + 1) * LANES]
        here = lax.broadcasted_iota(jnp.int32, group.shape, 0) == lax.broadcasted_iota(
            jnp.int32, group.shape, 1
        )
        place_ref[:, g * LANES : (g + 1) * LANES] = jnp.sum(
            jnp.where(here, group, 0.0), axis=0, keepdims=True
        ).astype(jnp.int32)
    first_row = jnp.broadcast_to(labels.reshape(slots, 1, LANES) * rows, (slots, rows, LANES))
    source = first_row + lax.broadcasted_iota(jnp.int32, (slots, rows, LANES), 1).astype(
        jnp.float32
    )
    lane = lax.broadcasted_iota(jnp.int32, (slots, rows, LANES), 2).astype(jnp.float32)
    hot = []
    for c in range(chunks):
        match = jnp.where(source == lane + float(c * LANES), 1.0, 0.0)
        hot.append(match.reshape(slots * rows, LANES).astype(jnp.bfloat16))
    hot = jnp.concatenate(hot, axis=1)
    for c in range(chunks):
        for t in range(tile_count):
            for k in range(capacity):
                row = (t * capacity + k) * rows
                wide_ref[row : row + rows, :] = arrived_ref[t, k * chunks + c].astype(jnp.float32)
        across = wide_ref[...].T.astype(jnp.bfloat16)
        turned_ref[c * LANES : (c + 1) * LANES, :] = jnp.dot(
            across, hot, preferred_element_type=jnp.float32
        )
    size = square_ref.shape[0]
    square_ref[...] = turned_ref[:size, :size].astype(jnp.bfloat16)
    column = turned_ref[:size, size:] + turned_ref[size:, :size].T
    high = column.astype(jnp.bfloat16)
    last_ref[:size, :LANES] = high
    last_ref[:size, LANES:] = (column - high.astype(jnp.float32)).astype(jnp.bfloat16)
    last_ref[size:, :LANES] = turned_ref[size:, size:].astype(jnp.bfloat16)
    last_ref[size:, LANES:] = jnp.zeros((LANES, LANES), jnp.bfloat16)


def half_density(piece, square_ref, last_ref, values_ref, out_ref):
    half = out_ref.shape[1]
    size = square_ref.shape[0]
    for q in range(values_ref.shape[1] // piece):
        lanes = slice(q * piece, (q + 1) * piece)
        block, end = values_ref[:size, lanes], values_ref[size:, lanes]
        mixed = jnp.dot(
            last_ref[...],
            jnp.concatenate([end, end], axis=0),
            preferred_element_type=jnp.float32,
        )
        inner = mixed[:size] + jnp.dot(
            square_ref[...], block, preferred_element_type=jnp.float32
        )
        density = jnp.sum(inner * block.astype(jnp.float32), axis=0, keepdims=True)
        density += jnp.sum(mixed[size:] * end.astype(jnp.float32), axis=0, keepdims=True)
        for p in range(piece // half):
            row = q * (piece // half) + p
            out_ref[row : row + 1, :] = density[:, p * half : (p + 1) * half]


def near_kernel(
    capacity, chunks, piece, arrived_ref, near_ref, far_hbm,
    out_ref, place_ref, square_ref, last_ref, far_ref, wide_ref, turned_ref, sem,
):
    copy = pltpu.make_async_copy(far_hbm, far_ref, sem.at[0])
    copy.start()
    arrange(capacity, chunks, arrived_ref, place_ref, square_ref, last_ref, wide_ref, turned_ref)
    half_density(piece, square_ref, last_ref, near_ref, out_ref)
    copy.wait()


def far_kernel(piece, square_ref, last_ref, far_ref, out_ref):
    half_density(piece, square_ref, last_ref, far_ref, out_ref)


def join_kernel(near_ref, far_ref, wrap_ref, pair_ref, out_ref, top_ref, bottom_ref):
    half = near_ref.shape[1]
    odd = odd_row() == 1
    blocks = (
        jnp.where(odd, pair_ref[...], wrap_ref[...]),
        jnp.where(odd, far_ref[...], near_ref[...]),
        jnp.where(odd, near_ref[...], far_ref[...]),
        jnp.where(odd, wrap_ref[...], pair_ref[...]),
    )
    for i, block in enumerate(blocks):
        out_ref[:, i * half : (i + 1) * half] = block
    top_ref[...] = out_ref[: top_ref.shape[0], :]
    bottom_ref[...] = out_ref[out_ref.shape[0] - bottom_ref.shape[0] :, :]


def split_dot(left, high, low):
    left_high = left.astype(jnp.bfloat16)
    left_low = (left - left_high.astype(jnp.float32)).astype(jnp.bfloat16)
    out = jnp.dot(left_high, high, preferred_element_type=jnp.float32)
    out = out + jnp.dot(left_low, high, preferred_element_type=jnp.float32)
    return out + jnp.dot(left_high, low, preferred_element_type=jnp.float32)


def filter_kernel(parts, *refs):
    taps_ref, band_high, band_low, fold_high, fold_low = refs[:5]
    blocks = refs[5 : 5 + 3 * parts]
    out_ref, field_ref, grid_ref, first_ref, second_ref, third_ref = refs[5 + 3 * parts :]
    size_x, size_y, size_z = out_ref.shape
    wide_y, wide_x, lanes = first_ref.shape
    for part in range(parts):
        start = 0
        for block in blocks[3 * part : 3 * part + 3]:
            rows = block.shape[0]
            for y in range(wide_y):
                grid_ref[y, start : start + rows, part * size_z : (part + 1) * size_z] = block[
                    :, y * size_z : (y + 1) * size_z
                ]
            start += rows
    grid = grid_ref[...].reshape(wide_y * wide_x, parts * size_z)
    first_ref[...] = split_dot(grid, band_high[...], band_low[...]).reshape(wide_y, wide_x, lanes)

    def tap(distance, rows):
        return jnp.broadcast_to(taps_ref[distance : distance + 1, :], (rows, lanes))

    def smooth(y, carry):
        run = tap(0, wide_x) * first_ref[y + RADIUS]
        for d in range(1, RADIUS + 1):
            pair = first_ref[y + (RADIUS - d)] + first_ref[y + (RADIUS + d)]
            run = run + tap(d, wide_x) * pair
        second_ref[y] = run
        run = tap(0, size_x) * second_ref[y, RADIUS : RADIUS + size_x, :]
        for d in range(1, RADIUS + 1):
            pair = (
                second_ref[y, RADIUS - d : RADIUS - d + size_x, :]
                + second_ref[y, RADIUS + d : RADIUS + d + size_x, :]
            )
            run = run + tap(d, size_x) * pair
        third_ref[y] = run
        return carry

    lax.fori_loop(0, size_y, smooth, 0, unroll=4)
    filtered = third_ref[...].reshape(size_y * size_x, lanes)
    folded = split_dot(filtered, fold_high[...], fold_low[...]).reshape(size_y, size_x, size_z)
    for y in range(size_y):
        out_ref[:, y, :] = folded[y]
        field_ref[:, y * size_z : (y + 1) * size_z] = folded[y]


def potential_kernel(
    capacity, weight, piece, place_vmem, grid_ref, field_ref, near_ref, far_ref,
    out_ref, grid_hbm, right_ref, corner_ref, whole_ref, place_ref, sems,
):
    copies = [
        pltpu.make_async_copy(place_vmem, place_ref, sems.at[0]),
        pltpu.make_async_copy(grid_ref, grid_hbm, sems.at[1]),
    ]
    for copy in copies:
        copy.start()
    points = near_ref.shape[1]
    half = field_ref.shape[1] // 2
    odd = odd_row() == 1
    low, high = field_ref[:, :half] * weight, field_ref[:, half:] * weight
    first = True
    over_points = (((1,), (1,)), ((), ()))
    for values_ref, source in (
        (near_ref, jnp.where(odd, high, low)),
        (far_ref, jnp.where(odd, low, high)),
    ):
        for q in range(points // piece):
            field = jnp.concatenate(
                [
                    source[x : x + 1, :]
                    for x in range(q * piece // half, (q + 1) * piece // half)
                ],
                axis=1,
            )
            block = values_ref[:, q * piece : (q + 1) * piece]
            weighted = (field * block.astype(jnp.float32)).astype(jnp.bfloat16)
            right = lax.dot_general(
                block, weighted[LANES:], over_points, preferred_element_type=jnp.float32
            )
            corner = lax.dot_general(
                block[:LANES], weighted[:LANES], over_points, preferred_element_type=jnp.float32
            )
            right_ref[...] = right if first else right_ref[...] + right
            corner_ref[...] = corner if first else corner_ref[...] + corner
            first = False

    blocks, rows, _ = whole_ref.shape
    edge = LANES // rows
    whole_ref[:edge, :, :LANES] = corner_ref[...].reshape(edge, rows, -1).astype(jnp.bfloat16)
    whole_ref[edge:, :, :LANES] = (
        right_ref[:LANES].T.reshape(blocks - edge, rows, -1).astype(jnp.bfloat16)
    )
    whole_ref[:, :, LANES:] = right_ref[...].reshape(blocks, rows, -1).astype(jnp.bfloat16)
    for copy in copies:
        copy.wait()

    def visit(j, carry):
        t, k = j // capacity, j % capacity
        out_ref[t, k] = whole_ref[jnp.minimum(place_ref[0, j], blocks - 1)]
        return carry

    lax.fori_loop(0, out_ref.shape[0] * capacity, visit, 0, unroll=16)


def unpack_kernel(tile_count, tile_ref, back_ref, out_hbm, count_ref, sem):
    def visit(i, t, slot):
        pltpu.make_async_copy(back_ref.at[t, slot], out_hbm.at[i], sem.at[0]).start()

    for_each_slab(tile_ref, count_ref, tile_count, out_hbm.shape[0], visit)
    pltpu.make_async_copy(out_hbm, out_hbm, sem.at[0]).wait()


def moved(block, shifts):
    axes = tuple(shifts)
    sizes = [lax.axis_size(axis) for axis in axes]
    pairs = []
    for source in np.ndindex(*sizes):
        target = [(s + shifts[axis]) % n for s, axis, n in zip(source, axes, sizes)]
        pairs.append(
            (int(np.ravel_multi_index(source, sizes)), int(np.ravel_multi_index(target, sizes)))
        )
    return lax.ppermute(block, axes, pairs)


def band_tables(size_z, neighbours):
    tap_table, mix = kernel_tables(RADIUS)

    def band(shift):
        table = np.zeros((size_z, len(ALPHAS), size_z), np.float64)
        for m in range(len(ALPHAS)):
            for source in range(size_z):
                for target in range(size_z):
                    offset = source + shift - target
                    if abs(offset) <= RADIUS:
                        table[source, m, target] = tap_table[m][offset + RADIUS]
        return table.reshape(size_z, len(ALPHAS) * size_z)

    own, low, high = band(0), band(-size_z), band(size_z)
    bands = {0: [own + low + high], 1: [own, low + high], 2: [own, low, high]}[neighbours]
    taps = np.zeros((16, len(ALPHAS) * size_z), np.float64)
    for d in range(RADIUS + 1):
        taps[d] = np.repeat([row[RADIUS + d] for row in tap_table], size_z)
    fold = np.concatenate([mix[m] * np.eye(size_z) for m in range(len(ALPHAS))], axis=0)

    def split(table):
        high = table.astype(np.float32).astype(jnp.bfloat16)
        low = (table - high.astype(np.float64)).astype(np.float32).astype(jnp.bfloat16)
        return [high, low]

    return [taps.astype(np.float32), *split(np.concatenate(bands, axis=0)), *split(fold)]


def local(orbital_values, dm_slabs, slab_tile, slab_place):
    size_x, size_y, size_z, list_orb = orbital_values.shape
    slab_count, atom_orb, _ = dm_slabs.shape
    list_blk = list_orb // atom_orb
    tile_count = lax.axis_size("gx") * lax.axis_size("gy")
    capacity = max(2, 2 * ((list_blk + tile_count - 1) // tile_count))
    chunks = list_orb // LANES
    tile_points = size_x * size_y * size_z
    plane = size_y * size_z
    counts = pltpu.SMEM((tile_count,), jnp.int32)

    groups = math.gcd(tile_count, 4)
    packed_shape = (tile_count, capacity * chunks + 1, atom_orb, LANES)
    packed = pl.pallas_call(
        functools.partial(pack_kernel, capacity, chunks, float(list_blk), groups),
        out_shape=jax.ShapeDtypeStruct(packed_shape, jnp.bfloat16),
        in_specs=[HBM_SPEC] * 3,
        out_specs=HBM_SPEC,
        scratch_shapes=[
            pltpu.SMEM((slab_count,), jnp.int32),
            pltpu.SMEM((slab_count,), jnp.int32),
            pltpu.VMEM(dm_slabs.shape, dm_slabs.dtype),
            counts,
            pltpu.SMEM((tile_count * capacity,), jnp.int32),
            pltpu.VMEM((tile_count, atom_orb, LANES), jnp.float32),
            pltpu.VMEM(packed_shape, jnp.bfloat16),
            pltpu.SemaphoreType.DMA((3,)),
            pltpu.SemaphoreType.DMA((groups,)),
        ],
        compiler_params=grant(4),
        name="pack",
    )(in_hbm(slab_tile), in_hbm(slab_place), in_hbm(dm_slabs))
    arrived = lax.all_to_all(packed, ("gx", "gy"), split_axis=0, concat_axis=0, tiled=True)
    half = plane // 2
    half_points = tile_points // 2
    piece = 4 * half
    bf16 = lambda *shape: jax.ShapeDtypeStruct(shape, jnp.bfloat16)
    f32 = lambda *shape: jax.ShapeDtypeStruct(shape, jnp.float32)
    near, far = pl.pallas_call(
        functools.partial(turn_kernel, size_x),
        out_shape=(
            pltpu.VMEM((list_orb, half_points), jnp.bfloat16),
            bf16(list_orb, half_points),
        ),
        in_specs=[HBM_SPEC],
        out_specs=(VMEM_SPEC, HBM_SPEC),
        scratch_shapes=[
            pltpu.VMEM((tile_points, list_orb), jnp.bfloat16),
            pltpu.VMEM((list_orb, half_points), jnp.bfloat16),
            pltpu.SemaphoreType.DMA((size_x // 2,)),
            pltpu.SemaphoreType.DMA((1,)),
        ],
        compiler_params=grant(20),
        cost_estimate=cost(0, 4 * tile_points * list_orb),
        name="turn",
    )(in_hbm(orbital_values.reshape(tile_points, list_orb)))

    slots = LANES * ((tile_count * capacity + LANES - 1) // LANES)
    product = 2 * half_points * list_orb * list_orb
    near_y, places, square, last, far = pl.pallas_call(
        functools.partial(near_kernel, capacity, chunks, piece),
        out_shape=(
            f32(size_x, half),
            jax.ShapeDtypeStruct((1, slots), jnp.int32),
            bf16(list_orb - LANES, list_orb - LANES),
            bf16(list_orb, 2 * LANES),
            pltpu.VMEM((list_orb, half_points), jnp.bfloat16),
        ),
        in_specs=[VMEM_SPEC, VMEM_SPEC, HBM_SPEC],
        out_specs=(VMEM_SPEC,) * 5,
        scratch_shapes=[
            pltpu.VMEM((tile_count * capacity * atom_orb, LANES), jnp.float32),
            pltpu.VMEM((list_orb, list_orb), jnp.float32),
            pltpu.SemaphoreType.DMA((1,)),
        ],
        compiler_params=grant(20),
        cost_estimate=cost(product, 2 * half_points * list_orb),
        name="near",
    )(arrived, near, in_hbm(far))
    rows = lax.axis_size("gy")
    pair = [(i, i ^ 1) for i in range(rows)]
    wrap = [(i, (i - 1 + 2 * (i % 2)) % rows) for i in range(rows)]
    from_wrap = lax.ppermute(near_y, "gy", wrap)
    far_y = pl.pallas_call(
        functools.partial(far_kernel, piece),
        out_shape=f32(size_x, half),
        in_specs=[VMEM_SPEC] * 3,
        out_specs=VMEM_SPEC,
        compiler_params=grant(20),
        cost_estimate=cost(product, 2 * half_points * list_orb),
        name="far",
    )(square, last, far)
    from_pair = lax.ppermute(far_y, "gy", pair)

    wide = 2 * plane
    own, top, bottom = pl.pallas_call(
        join_kernel,
        out_shape=(f32(size_x, wide), f32(RADIUS, wide), f32(RADIUS, wide)),
        in_specs=[VMEM_SPEC] * 4,
        out_specs=(VMEM_SPEC,) * 3,
        compiler_params=grant(2),
        name="join",
    )(near_y, far_y, from_wrap, from_pair)
    layers = lax.axis_size("gz")
    blocks = []
    for shift in {1: [0], 2: [0, 1]}.get(layers, [0, 1, -1]):
        blocks.append(moved(bottom, {"gx": 1, "gz": shift}))
        blocks.append(moved(own, {"gz": shift}) if shift else own)
        blocks.append(moved(top, {"gx": -1, "gz": shift}))
    parts = len(blocks) // 3
    tables = band_tables(size_z, parts - 1)
    lanes = tables[0].shape[1]
    wide_x, wide_y = size_x + 2 * RADIUS, size_y + 2 * RADIUS
    potential, field = pl.pallas_call(
        functools.partial(filter_kernel, parts),
        out_shape=(pltpu.VMEM((size_x, size_y, size_z), jnp.float32), f32(size_x, plane)),
        in_specs=[VMEM_SPEC] * (len(tables) + len(blocks)),
        out_specs=(VMEM_SPEC,) * 2,
        scratch_shapes=[
            pltpu.VMEM((wide_y, wide_x, parts * size_z), jnp.float32),
            pltpu.VMEM((wide_y, wide_x, lanes), jnp.float32),
            pltpu.VMEM((size_y, wide_x, lanes), jnp.float32),
            pltpu.VMEM((size_y, size_x, lanes), jnp.float32),
        ],
        compiler_params=grant(12),
        name="filter",
    )(*map(jnp.asarray, tables), *blocks)

    returned, potential = pl.pallas_call(
        functools.partial(
            potential_kernel, capacity, float(tile_points) ** (-0.5), 2 * piece
        ),
        out_shape=(
            bf16(tile_count, capacity, atom_orb, list_orb),
            f32(size_x, size_y, size_z),
        ),
        in_specs=[VMEM_SPEC] * 5,
        out_specs=(VMEM_SPEC, HBM_SPEC),
        scratch_shapes=[
            pltpu.VMEM((list_orb, list_orb - LANES), jnp.float32),
            pltpu.VMEM((LANES, LANES), jnp.float32),
            pltpu.VMEM((list_blk, atom_orb, list_orb), jnp.bfloat16),
            pltpu.SMEM((1, slots), jnp.int32),
            pltpu.SemaphoreType.DMA((2,)),
        ],
        compiler_params=grant(20),
        name="potential",
    )(places, potential, field, near, far)
    back = lax.all_to_all(returned, ("gx", "gy"), split_axis=0, concat_axis=0, tiled=True)
    own_rows = pl.pallas_call(
        functools.partial(unpack_kernel, tile_count),
        out_shape=bf16(slab_count, atom_orb, list_orb),
        in_specs=[SMEM_SPEC, VMEM_SPEC],
        out_specs=HBM_SPEC,
        scratch_shapes=[counts, pltpu.SemaphoreType.DMA((1,))],
        compiler_params=grant(4),
        name="unpack",
    )(slab_tile, back)
    return (potential, own_rows)


def solution(mesh):
    placed = (
        P("gx", "gy", "gz", None),
        P(("gx", "gy", "gz"), None, None),
        P(("gx", "gy", "gz")),
        P(("gx", "gy", "gz")),
    )

    return jax.shard_map(
        local,
        mesh=mesh,
        in_specs=placed,
        out_specs=(P("gx", "gy", "gz"), P(("gx", "gy", "gz"), None, None)),
        check_vma=False,
    )
```

```python
import functools
import math

import jax
import jax.numpy as jnp
import numpy as np
from jax import lax
from jax.experimental import pallas as pl
from jax.experimental.pallas import tpu as pltpu
from jax.sharding import PartitionSpec as P


RADIUS = 8
LANES = 128

ALPHAS = (0.012, 0.025, 0.05, 0.1, 0.2, 0.4, 0.8, 1.6)
MIXES = (0.3, 0.3, 0.32, 0.34, 0.36, 0.38, 0.4, 0.42)

VMEM_SPEC = pl.BlockSpec(memory_space=pltpu.VMEM)
SMEM_SPEC = pl.BlockSpec(memory_space=pltpu.SMEM)
HBM_SPEC = pl.BlockSpec(memory_space=pltpu.HBM)


def in_hbm(array):
    return pltpu.with_memory_space_constraint(array, pltpu.HBM)


def grant(mebibytes):
    return pltpu.CompilerParams(vmem_limit_bytes=mebibytes << 20)


def kernel_tables(radius):
    tap_table = [
        [math.exp(-alpha * offset * offset) for offset in range(-radius, radius + 1)]
        for alpha in ALPHAS
    ]
    mix = [
        MIXES[term] / sum((tap * tap for tap in tap_table[term])) ** 1.5
        for term in range(len(ALPHAS))
    ]
    return (tap_table, mix)


def cost(flops, moved_bytes):
    return pl.CostEstimate(flops=flops, bytes_accessed=moved_bytes, transcendentals=0)


def for_each_slab(tile_ref, count_ref, tile_count, slab_count, visit):
    for t in range(tile_count):
        count_ref[t] = 0

    def step(i, carry):
        t = tile_ref[i]
        slot = count_ref[t]
        count_ref[t] = slot + 1
        visit(i, t, slot)
        return carry

    lax.fori_loop(0, slab_count, step, 0, unroll=4)


def pack_kernel(
    capacity, chunks, empty, groups, tile_hbm, place_hbm, slab_hbm, out_hbm,
    tile_ref, place_ref, slab_ref, count_ref, index_ref, label_ref, out_ref, sems, out_sems,
):
    copies = [
        pltpu.make_async_copy(tile_hbm, tile_ref, sems.at[0]),
        pltpu.make_async_copy(place_hbm, place_ref, sems.at[1]),
    ]
    slab_share = slab_ref.shape[0] // groups
    for g in range(groups):
        part = slice(g * slab_share, (g + 1) * slab_share)
        copies.append(
            pltpu.make_async_copy(slab_hbm.at[part], slab_ref.at[part], sems.at[2 + g])
        )
    for copy in copies:
        copy.start()
    tile_count = out_ref.shape[0]
    label_ref[...] = jnp.full(label_ref.shape, empty, jnp.float32)
    for j in range(tile_count * capacity):
        index_ref[j] = 0
    for copy in copies[:2]:
        copy.wait()

    def rank(i, t, slot):
        index_ref[t * capacity + slot] = i
        label = place_ref[i].astype(jnp.float32)
        label_ref[t, pl.ds(slot, 1), :] = jnp.full((1, LANES), label, jnp.float32)

    for_each_slab(tile_ref, count_ref, tile_count, slab_ref.shape[0], rank)
    for copy in copies[2:]:
        copy.wait()
    sent = []

    def fill(t, carry):
        for k in range(capacity):
            slab = slab_ref[index_ref[t * capacity + k]]
            for c in range(chunks):
                out_ref[t, k * chunks + c] = slab[:, c * LANES : (c + 1) * LANES]
        out_ref[t, capacity * chunks] = label_ref[t].astype(jnp.bfloat16)
        return carry

    share = tile_count // groups
    for g in range(groups):
        lax.fori_loop(g * share, (g + 1) * share, fill, 0, unroll=min(share, 4))
        part = slice(g * share, (g + 1) * share)
        sent.append(pltpu.make_async_copy(out_ref.at[part], out_hbm.at[part], out_sems.at[g]))
        sent[-1].start()
    for copy in sent:
        copy.wait()


def odd_row():
    return lax.rem(lax.axis_index("gy"), 2)


def turn_kernel(planes, values_hbm, near_ref, far_hbm, values_ref, far_ref, sems, out_sem):
    points = values_ref.shape[0]
    plane = points // planes
    half = plane // 2
    copies = []
    for x in range(0, planes, 2):
        part = slice(x * plane, (x + 2) * plane)
        copies.append(
            pltpu.make_async_copy(values_hbm.at[part], values_ref.at[part], sems.at[x // 2])
        )
        copies[-1].start()
    near_start = odd_row() * half
    for x in range(0, planes, 2):
        copies[x // 2].wait()
        for start, out_ref in ((near_start, near_ref), (half - near_start, far_ref)):
            rows = [
                values_ref[pl.ds(pl.multiple_of((x + i) * plane + start, half), half), :]
                for i in range(2)
            ]
            out_ref[:, x * half : (x + 2) * half] = jnp.concatenate(rows, axis=0).T
    copy = pltpu.make_async_copy(far_ref, far_hbm, out_sem.at[0])
    copy.start()
    copy.wait()


def arrange(capacity, chunks, arrived_ref, place_ref, square_ref, last_ref, wide_ref, turned_ref):
    tile_count, _, rows, _ = arrived_ref.shape
    slots = tile_count * capacity
    labels = arrived_ref[:, capacity * chunks].astype(jnp.float32)[:, :capacity]
    labels = labels.reshape(slots, LANES)
    width = place_ref.shape[1]
    for g in range(width // LANES):
        group = labels[g * LANES : (g + 1) * LANES]
        here = lax.broadcasted_iota(jnp.int32, group.shape, 0) == lax.broadcasted_iota(
            jnp.int32, group.shape, 1
        )
        place_ref[:, g * LANES : (g + 1) * LANES] = jnp.sum(
            jnp.where(here, group, 0.0), axis=0, keepdims=True
        ).astype(jnp.int32)
    first_row = jnp.broadcast_to(labels.reshape(slots, 1, LANES) * rows, (slots, rows, LANES))
    source = first_row + lax.broadcasted_iota(jnp.int32, (slots, rows, LANES), 1).astype(
        jnp.float32
    )
    lane = lax.broadcasted_iota(jnp.int32, (slots, rows, LANES), 2).astype(jnp.float32)
    hot = []
    for c in range(chunks):
        match = jnp.where(source == lane + float(c * LANES), 1.0, 0.0)
        hot.append(match.reshape(slots * rows, LANES).astype(jnp.bfloat16))
    hot = jnp.concatenate(hot, axis=1)
    for c in range(chunks):
        for t in range(tile_count):
            for k in range(capacity):
                row = (t * capacity + k) * rows
                wide_ref[row : row + rows, :] = arrived_ref[t, k * chunks + c].astype(jnp.float32)
        across = wide_ref[...].T.astype(jnp.bfloat16)
        turned_ref[c * LANES : (c + 1) * LANES, :] = jnp.dot(
            across, hot, preferred_element_type=jnp.float32
        )
    size = square_ref.shape[0]
    square_ref[...] = turned_ref[:size, :size].astype(jnp.bfloat16)
    column = turned_ref[:size, size:] + turned_ref[size:, :size].T
    high = column.astype(jnp.bfloat16)
    last_ref[:size, :LANES] = high
    last_ref[:size, LANES:] = (column - high.astype(jnp.float32)).astype(jnp.bfloat16)
    last_ref[size:, :LANES] = turned_ref[size:, size:].astype(jnp.bfloat16)
    last_ref[size:, LANES:] = jnp.zeros((LANES, LANES), jnp.bfloat16)


def half_density(piece, square_ref, last_ref, values_ref, out_ref):
    half = out_ref.shape[1]
    size = square_ref.shape[0]
    for q in range(values_ref.shape[1] // piece):
        lanes = slice(q * piece, (q + 1) * piece)
        block, end = values_ref[:size, lanes], values_ref[size:, lanes]
        mixed = jnp.dot(
            last_ref[...],
            jnp.concatenate([end, end], axis=0),
            preferred_element_type=jnp.float32,
        )
        inner = mixed[:size] + jnp.dot(
            square_ref[...], block, preferred_element_type=jnp.float32
        )
        density = jnp.sum(inner * block.astype(jnp.float32), axis=0, keepdims=True)
        density += jnp.sum(mixed[size:] * end.astype(jnp.float32), axis=0, keepdims=True)
        for p in range(piece // half):
            row = q * (piece // half) + p
            out_ref[row : row + 1, :] = density[:, p * half : (p + 1) * half]


def near_kernel(
    capacity, chunks, piece, arrived_ref, near_ref, far_hbm,
    out_ref, place_ref, square_ref, last_ref, far_ref, wide_ref, turned_ref, sem,
):
    copy = pltpu.make_async_copy(far_hbm, far_ref, sem.at[0])
    copy.start()
    arrange(capacity, chunks, arrived_ref, place_ref, square_ref, last_ref, wide_ref, turned_ref)
    half_density(piece, square_ref, last_ref, near_ref, out_ref)
    copy.wait()


def far_kernel(piece, square_ref, last_ref, far_ref, out_ref):
    half_density(piece, square_ref, last_ref, far_ref, out_ref)


def join_kernel(near_ref, far_ref, wrap_ref, pair_ref, out_ref, top_ref, bottom_ref):
    half = near_ref.shape[1]
    odd = odd_row() == 1
    blocks = (
        jnp.where(odd, pair_ref[...], wrap_ref[...]),
        jnp.where(odd, far_ref[...], near_ref[...]),
        jnp.where(odd, near_ref[...], far_ref[...]),
        jnp.where(odd, wrap_ref[...], pair_ref[...]),
    )
    for i, block in enumerate(blocks):
        out_ref[:, i * half : (i + 1) * half] = block
    top_ref[...] = out_ref[: top_ref.shape[0], :]
    bottom_ref[...] = out_ref[out_ref.shape[0] - bottom_ref.shape[0] :, :]


def split_dot(left, high, low):
    left_high = left.astype(jnp.bfloat16)
    left_low = (left - left_high.astype(jnp.float32)).astype(jnp.bfloat16)
    out = jnp.dot(left_high, high, preferred_element_type=jnp.float32)
    out = out + jnp.dot(left_low, high, preferred_element_type=jnp.float32)
    return out + jnp.dot(left_high, low, preferred_element_type=jnp.float32)


def filter_kernel(parts, *refs):
    taps_ref, band_ref, fold_high, fold_low = refs[:4]
    blocks = refs[4 : 4 + 3 * parts]
    out_ref, field_ref, grid_ref, first_ref, second_ref, third_ref = refs[4 + 3 * parts :]
    size_x, size_y, size_z = out_ref.shape
    wide_y, wide_x, lanes = first_ref.shape
    for part in range(parts):
        start = 0
        for block in blocks[3 * part : 3 * part + 3]:
            rows = block.shape[0]
            for y in range(wide_y):
                grid_ref[y, start : start + rows, part * size_z : (part + 1) * size_z] = block[
                    :, y * size_z : (y + 1) * size_z
                ]
            start += rows
    grid = grid_ref[...].reshape(wide_y * wide_x, parts * size_z)
    high = grid.astype(jnp.bfloat16)
    low = (grid - high.astype(jnp.float32)).astype(jnp.bfloat16)
    first_ref[...] = jnp.dot(
        jnp.concatenate([high, low, high], axis=1),
        band_ref[...],
        preferred_element_type=jnp.float32,
    ).reshape(wide_y, wide_x, lanes)

    def tap(distance, rows):
        return jnp.broadcast_to(taps_ref[distance : distance + 1, :], (rows, lanes))

    def smooth(y, carry):
        run = tap(0, wide_x) * first_ref[y + RADIUS]
        for d in range(1, RADIUS + 1):
            pair = first_ref[y + (RADIUS - d)] + first_ref[y + (RADIUS + d)]
            run = run + tap(d, wide_x) * pair
        second_ref[y] = run
        run = tap(0, size_x) * second_ref[y, RADIUS : RADIUS + size_x, :]
        for d in range(1, RADIUS + 1):
            pair = (
                second_ref[y, RADIUS - d : RADIUS - d + size_x, :]
                + second_ref[y, RADIUS + d : RADIUS + d + size_x, :]
            )
            run = run + tap(d, size_x) * pair
        third_ref[y] = run
        return carry

    lax.fori_loop(0, size_y, smooth, 0, unroll=4)
    filtered = third_ref[...].reshape(size_y * size_x, lanes)
    folded = split_dot(filtered, fold_high[...], fold_low[...]).reshape(size_y, size_x, size_z)
    for y in range(size_y):
        out_ref[:, y, :] = folded[y]
        field_ref[:, y * size_z : (y + 1) * size_z] = folded[y]


def potential_kernel(
    capacity, weight, piece, place_vmem, grid_ref, field_ref, near_ref, far_ref,
    out_ref, grid_hbm, right_ref, corner_ref, whole_ref, place_ref, sems,
):
    copies = [
        pltpu.make_async_copy(place_vmem, place_ref, sems.at[0]),
        pltpu.make_async_copy(grid_ref, grid_hbm, sems.at[1]),
    ]
    for copy in copies:
        copy.start()
    points = near_ref.shape[1]
    half = field_ref.shape[1] // 2
    odd = odd_row() == 1
    low, high = field_ref[:, :half] * weight, field_ref[:, half:] * weight
    first = True
    over_points = (((1,), (1,)), ((), ()))
    for values_ref, source in (
        (near_ref, jnp.where(odd, high, low)),
        (far_ref, jnp.where(odd, low, high)),
    ):
        for q in range(points // piece):
            field = jnp.concatenate(
                [
                    source[x : x + 1, :]
                    for x in range(q * piece // half, (q + 1) * piece // half)
                ],
                axis=1,
            )
            block = values_ref[:, q * piece : (q + 1) * piece]
            weighted = (field * block.astype(jnp.float32)).astype(jnp.bfloat16)
            right = lax.dot_general(
                block, weighted[LANES:], over_points, preferred_element_type=jnp.float32
            )
            corner = lax.dot_general(
                block[:LANES], weighted[:LANES], over_points, preferred_element_type=jnp.float32
            )
            right_ref[...] = right if first else right_ref[...] + right
            corner_ref[...] = corner if first else corner_ref[...] + corner
            first = False

    blocks, rows, _ = whole_ref.shape
    edge = LANES // rows
    whole_ref[:edge, :, :LANES] = corner_ref[...].reshape(edge, rows, -1).astype(jnp.bfloat16)
    whole_ref[edge:, :, :LANES] = (
        right_ref[:LANES].T.reshape(blocks - edge, rows, -1).astype(jnp.bfloat16)
    )
    whole_ref[:, :, LANES:] = right_ref[...].reshape(blocks, rows, -1).astype(jnp.bfloat16)
    for copy in copies:
        copy.wait()

    def visit(j, carry):
        t, k = j // capacity, j % capacity
        out_ref[t, k] = whole_ref[jnp.minimum(place_ref[0, j], blocks - 1)]
        return carry

    lax.fori_loop(0, out_ref.shape[0] * capacity, visit, 0, unroll=16)


def unpack_kernel(tile_count, tile_ref, back_ref, out_hbm, count_ref, sem):
    def visit(i, t, slot):
        pltpu.make_async_copy(back_ref.at[t, slot], out_hbm.at[i], sem.at[0]).start()

    for_each_slab(tile_ref, count_ref, tile_count, out_hbm.shape[0], visit)
    pltpu.make_async_copy(out_hbm, out_hbm, sem.at[0]).wait()


def moved(block, shifts):
    axes = tuple(shifts)
    sizes = [lax.axis_size(axis) for axis in axes]
    pairs = []
    for source in np.ndindex(*sizes):
        target = [(s + shifts[axis]) % n for s, axis, n in zip(source, axes, sizes)]
        pairs.append(
            (int(np.ravel_multi_index(source, sizes)), int(np.ravel_multi_index(target, sizes)))
        )
    return lax.ppermute(block, axes, pairs)


def band_tables(size_z, neighbours):
    tap_table, mix = kernel_tables(RADIUS)

    def band(shift):
        table = np.zeros((size_z, len(ALPHAS), size_z), np.float64)
        for m in range(len(ALPHAS)):
            for source in range(size_z):
                for target in range(size_z):
                    offset = source + shift - target
                    if abs(offset) <= RADIUS:
                        table[source, m, target] = tap_table[m][offset + RADIUS]
        return table.reshape(size_z, len(ALPHAS) * size_z)

    own, low, high = band(0), band(-size_z), band(size_z)
    bands = {0: [own + low + high], 1: [own, low + high], 2: [own, low, high]}[neighbours]
    taps = np.zeros((16, len(ALPHAS) * size_z), np.float64)
    for d in range(RADIUS + 1):
        taps[d] = np.repeat([row[RADIUS + d] for row in tap_table], size_z)
    fold = np.concatenate([mix[m] * np.eye(size_z) for m in range(len(ALPHAS))], axis=0)

    def split(table):
        high = table.astype(np.float32).astype(jnp.bfloat16)
        low = (table - high.astype(np.float64)).astype(np.float32).astype(jnp.bfloat16)
        return [high, low]

    band_high, band_low = split(np.concatenate(bands, axis=0))
    stacked = np.concatenate([band_high, band_high, band_low], axis=0)
    return [taps.astype(np.float32), stacked, *split(fold)]


def local(orbital_values, dm_slabs, slab_tile, slab_place):
    size_x, size_y, size_z, list_orb = orbital_values.shape
    slab_count, atom_orb, _ = dm_slabs.shape
    list_blk = list_orb // atom_orb
    tile_count = lax.axis_size("gx") * lax.axis_size("gy")
    capacity = max(2, 2 * ((list_blk + tile_count - 1) // tile_count))
    chunks = list_orb // LANES
    tile_points = size_x * size_y * size_z
    plane = size_y * size_z
    counts = pltpu.SMEM((tile_count,), jnp.int32)

    groups = math.gcd(math.gcd(tile_count, slab_count), 4)
    packed_shape = (tile_count, capacity * chunks + 1, atom_orb, LANES)
    packed = pl.pallas_call(
        functools.partial(pack_kernel, capacity, chunks, float(list_blk), groups),
        out_shape=jax.ShapeDtypeStruct(packed_shape, jnp.bfloat16),
        in_specs=[HBM_SPEC] * 3,
        out_specs=HBM_SPEC,
        scratch_shapes=[
            pltpu.SMEM((slab_count,), jnp.int32),
            pltpu.SMEM((slab_count,), jnp.int32),
            pltpu.VMEM(dm_slabs.shape, dm_slabs.dtype),
            counts,
            pltpu.SMEM((tile_count * capacity,), jnp.int32),
            pltpu.VMEM((tile_count, atom_orb, LANES), jnp.float32),
            pltpu.VMEM(packed_shape, jnp.bfloat16),
            pltpu.SemaphoreType.DMA((2 + groups,)),
            pltpu.SemaphoreType.DMA((groups,)),
        ],
        compiler_params=grant(4),
        name="pack",
    )(in_hbm(slab_tile), in_hbm(slab_place), in_hbm(dm_slabs))
    arrived = lax.all_to_all(packed, ("gx", "gy"), split_axis=0, concat_axis=0, tiled=True)
    half = plane // 2
    half_points = tile_points // 2
    piece = 4 * half
    bf16 = lambda *shape: jax.ShapeDtypeStruct(shape, jnp.bfloat16)
    f32 = lambda *shape: jax.ShapeDtypeStruct(shape, jnp.float32)
    near, far = pl.pallas_call(
        functools.partial(turn_kernel, size_x),
        out_shape=(
            pltpu.VMEM((list_orb, half_points), jnp.bfloat16),
            bf16(list_orb, half_points),
        ),
        in_specs=[HBM_SPEC],
        out_specs=(VMEM_SPEC, HBM_SPEC),
        scratch_shapes=[
            pltpu.VMEM((tile_points, list_orb), jnp.bfloat16),
            pltpu.VMEM((list_orb, half_points), jnp.bfloat16),
            pltpu.SemaphoreType.DMA((size_x // 2,)),
            pltpu.SemaphoreType.DMA((1,)),
        ],
        compiler_params=grant(20),
        cost_estimate=cost(0, 4 * tile_points * list_orb),
        name="turn",
    )(in_hbm(orbital_values.reshape(tile_points, list_orb)))

    slots = LANES * ((tile_count * capacity + LANES - 1) // LANES)
    product = 2 * half_points * list_orb * list_orb
    near_y, places, square, last, far = pl.pallas_call(
        functools.partial(near_kernel, capacity, chunks, piece),
        out_shape=(
            f32(size_x, half),
            jax.ShapeDtypeStruct((1, slots), jnp.int32),
            bf16(list_orb - LANES, list_orb - LANES),
            bf16(list_orb, 2 * LANES),
            pltpu.VMEM((list_orb, half_points), jnp.bfloat16),
        ),
        in_specs=[VMEM_SPEC, VMEM_SPEC, HBM_SPEC],
        out_specs=(VMEM_SPEC,) * 5,
        scratch_shapes=[
            pltpu.VMEM((tile_count * capacity * atom_orb, LANES), jnp.float32),
            pltpu.VMEM((list_orb, list_orb), jnp.float32),
            pltpu.SemaphoreType.DMA((1,)),
        ],
        compiler_params=grant(20),
        cost_estimate=cost(product, 2 * half_points * list_orb),
        name="near",
    )(arrived, near, in_hbm(far))
    rows = lax.axis_size("gy")
    pair = [(i, i ^ 1) for i in range(rows)]
    wrap = [(i, (i - 1 + 2 * (i % 2)) % rows) for i in range(rows)]
    from_wrap = lax.ppermute(near_y, "gy", wrap)
    far_y = pl.pallas_call(
        functools.partial(far_kernel, piece),
        out_shape=f32(size_x, half),
        in_specs=[VMEM_SPEC] * 3,
        out_specs=VMEM_SPEC,
        compiler_params=grant(20),
        cost_estimate=cost(product, 2 * half_points * list_orb),
        name="far",
    )(square, last, far)
    from_pair = lax.ppermute(far_y, "gy", pair)

    wide = 2 * plane
    own, top, bottom = pl.pallas_call(
        join_kernel,
        out_shape=(f32(size_x, wide), f32(RADIUS, wide), f32(RADIUS, wide)),
        in_specs=[VMEM_SPEC] * 4,
        out_specs=(VMEM_SPEC,) * 3,
        compiler_params=grant(2),
        name="join",
    )(near_y, far_y, from_wrap, from_pair)
    layers = lax.axis_size("gz")
    blocks = []
    for shift in {1: [0], 2: [0, 1]}.get(layers, [0, 1, -1]):
        blocks.append(moved(bottom, {"gx": 1, "gz": shift}))
        blocks.append(moved(own, {"gz": shift}) if shift else own)
        blocks.append(moved(top, {"gx": -1, "gz": shift}))
    parts = len(blocks) // 3
    tables = band_tables(size_z, parts - 1)
    lanes = tables[0].shape[1]
    wide_x, wide_y = size_x + 2 * RADIUS, size_y + 2 * RADIUS
    potential, field = pl.pallas_call(
        functools.partial(filter_kernel, parts),
        out_shape=(pltpu.VMEM((size_x, size_y, size_z), jnp.float32), f32(size_x, plane)),
        in_specs=[VMEM_SPEC] * (len(tables) + len(blocks)),
        out_specs=(VMEM_SPEC,) * 2,
        scratch_shapes=[
            pltpu.VMEM((wide_y, wide_x, parts * size_z), jnp.float32),
            pltpu.VMEM((wide_y, wide_x, lanes), jnp.float32),
            pltpu.VMEM((size_y, wide_x, lanes), jnp.float32),
            pltpu.VMEM((size_y, size_x, lanes), jnp.float32),
        ],
        compiler_params=grant(12),
        name="filter",
    )(*map(jnp.asarray, tables), *blocks)

    returned, potential = pl.pallas_call(
        functools.partial(
            potential_kernel, capacity, float(tile_points) ** (-0.5), 2 * piece
        ),
        out_shape=(
            bf16(tile_count, capacity, atom_orb, list_orb),
            f32(size_x, size_y, size_z),
        ),
        in_specs=[VMEM_SPEC] * 5,
        out_specs=(VMEM_SPEC, HBM_SPEC),
        scratch_shapes=[
            pltpu.VMEM((list_orb, list_orb - LANES), jnp.float32),
            pltpu.VMEM((LANES, LANES), jnp.float32),
            pltpu.VMEM((list_blk, atom_orb, list_orb), jnp.bfloat16),
            pltpu.SMEM((1, slots), jnp.int32),
            pltpu.SemaphoreType.DMA((2,)),
        ],
        compiler_params=grant(20),
        name="potential",
    )(places, potential, field, near, far)
    back = lax.all_to_all(returned, ("gx", "gy"), split_axis=0, concat_axis=0, tiled=True)
    own_rows = pl.pallas_call(
        functools.partial(unpack_kernel, tile_count),
        out_shape=bf16(slab_count, atom_orb, list_orb),
        in_specs=[SMEM_SPEC, VMEM_SPEC],
        out_specs=HBM_SPEC,
        scratch_shapes=[counts, pltpu.SemaphoreType.DMA((1,))],
        compiler_params=grant(4),
        name="unpack",
    )(slab_tile, back)
    return (potential, own_rows)


def solution(mesh):
    placed = (
        P("gx", "gy", "gz", None),
        P(("gx", "gy", "gz"), None, None),
        P(("gx", "gy", "gz")),
        P(("gx", "gy", "gz")),
    )

    return jax.shard_map(
        local,
        mesh=mesh,
        in_specs=placed,
        out_specs=(P("gx", "gy", "gz"), P(("gx", "gy", "gz"), None, None)),
        check_vma=False,
    )
```

```python
import functools
import math

import jax
import jax.numpy as jnp
import numpy as np
from jax import lax
from jax.experimental import pallas as pl
from jax.experimental.pallas import tpu as pltpu
from jax.sharding import PartitionSpec as P


RADIUS = 8
LANES = 128

ALPHAS = (0.012, 0.025, 0.05, 0.1, 0.2, 0.4, 0.8, 1.6)
MIXES = (0.3, 0.3, 0.32, 0.34, 0.36, 0.38, 0.4, 0.42)

VMEM_SPEC = pl.BlockSpec(memory_space=pltpu.VMEM)
SMEM_SPEC = pl.BlockSpec(memory_space=pltpu.SMEM)
HBM_SPEC = pl.BlockSpec(memory_space=pltpu.HBM)


def in_hbm(array):
    return pltpu.with_memory_space_constraint(array, pltpu.HBM)


def grant(mebibytes):
    return pltpu.CompilerParams(vmem_limit_bytes=mebibytes << 20)


def kernel_tables(radius):
    tap_table = [
        [math.exp(-alpha * offset * offset) for offset in range(-radius, radius + 1)]
        for alpha in ALPHAS
    ]
    mix = [
        MIXES[term] / sum((tap * tap for tap in tap_table[term])) ** 1.5
        for term in range(len(ALPHAS))
    ]
    return (tap_table, mix)


def cost(flops, moved_bytes):
    return pl.CostEstimate(flops=flops, bytes_accessed=moved_bytes, transcendentals=0)


def for_each_slab(tile_ref, count_ref, tile_count, slab_count, visit):
    for t in range(tile_count):
        count_ref[t] = 0

    def step(i, carry):
        t = tile_ref[i]
        slot = count_ref[t]
        count_ref[t] = slot + 1
        visit(i, t, slot)
        return carry

    lax.fori_loop(0, slab_count, step, 0, unroll=4)


def pack_kernel(
    capacity, chunks, empty, groups, tile_hbm, place_hbm, slab_hbm, out_hbm,
    tile_ref, place_ref, slab_ref, count_ref, index_ref, label_ref, out_ref, sems, out_sems,
):
    copies = [
        pltpu.make_async_copy(tile_hbm, tile_ref, sems.at[0]),
        pltpu.make_async_copy(place_hbm, place_ref, sems.at[1]),
        pltpu.make_async_copy(slab_hbm, slab_ref, sems.at[2]),
    ]
    for copy in copies:
        copy.start()
    tile_count = out_ref.shape[0]
    label_ref[...] = jnp.full(label_ref.shape, empty, jnp.float32)
    for j in range(tile_count * capacity):
        index_ref[j] = 0
    for copy in copies[:2]:
        copy.wait()

    def rank(i, t, slot):
        index_ref[t * capacity + slot] = i
        label = place_ref[i].astype(jnp.float32)
        label_ref[t, pl.ds(slot, 1), :] = jnp.full((1, LANES), label, jnp.float32)

    for_each_slab(tile_ref, count_ref, tile_count, slab_ref.shape[0], rank)
    copies[2].wait()

    def fill(t, carry):
        for k in range(capacity):
            slab = slab_ref[index_ref[t * capacity + k]]
            for c in range(chunks):
                out_ref[t, k * chunks + c] = slab[:, c * LANES : (c + 1) * LANES]
        out_ref[t, capacity * chunks] = label_ref[t].astype(jnp.bfloat16)
        return carry

    share = tile_count // groups
    for g in range(groups):
        lax.fori_loop(g * share, (g + 1) * share, fill, 0, unroll=min(share, 4))
        part = slice(g * share, (g + 1) * share)
        copies.append(pltpu.make_async_copy(out_ref.at[part], out_hbm.at[part], out_sems.at[g]))
        copies[-1].start()
    for copy in copies[3:]:
        copy.wait()


def odd_row():
    return lax.rem(lax.axis_index("gy"), 2)


def turn_kernel(planes, values_hbm, near_ref, far_hbm, values_ref, far_ref, sems, out_sem):
    points = values_ref.shape[0]
    plane = points // planes
    half = plane // 2
    copies = []
    for x in range(0, planes, 2):
        part = slice(x * plane, (x + 2) * plane)
        copies.append(
            pltpu.make_async_copy(values_hbm.at[part], values_ref.at[part], sems.at[x // 2])
        )
        copies[-1].start()
    near_start = odd_row() * half
    for x in range(0, planes, 2):
        copies[x // 2].wait()
        for start, out_ref in ((near_start, near_ref), (half - near_start, far_ref)):
            rows = [
                values_ref[pl.ds(pl.multiple_of((x + i) * plane + start, half), half), :]
                for i in range(2)
            ]
            out_ref[:, x * half : (x + 2) * half] = jnp.concatenate(rows, axis=0).T
    copy = pltpu.make_async_copy(far_ref, far_hbm, out_sem.at[0])
    copy.start()
    copy.wait()


def arrange(capacity, chunks, arrived_ref, place_ref, square_ref, last_ref, wide_ref, turned_ref):
    tile_count, _, rows, _ = arrived_ref.shape
    slots = tile_count * capacity
    labels = arrived_ref[:, capacity * chunks].astype(jnp.float32)[:, :capacity]
    labels = labels.reshape(slots, LANES)
    width = place_ref.shape[1]
    for g in range(width // LANES):
        group = labels[g * LANES : (g + 1) * LANES]
        here = lax.broadcasted_iota(jnp.int32, group.shape, 0) == lax.broadcasted_iota(
            jnp.int32, group.shape, 1
        )
        place_ref[:, g * LANES : (g + 1) * LANES] = jnp.sum(
            jnp.where(here, group, 0.0), axis=0, keepdims=True
        ).astype(jnp.int32)
    first_row = jnp.broadcast_to(labels.reshape(slots, 1, LANES) * rows, (slots, rows, LANES))
    source = first_row + lax.broadcasted_iota(jnp.int32, (slots, rows, LANES), 1).astype(
        jnp.float32
    )
    lane = lax.broadcasted_iota(jnp.int32, (slots, rows, LANES), 2).astype(jnp.float32)
    hot = []
    for c in range(chunks):
        match = jnp.where(source == lane + float(c * LANES), 1.0, 0.0)
        hot.append(match.reshape(slots * rows, LANES).astype(jnp.bfloat16))
    hot = jnp.concatenate(hot, axis=1)
    for c in range(chunks):
        for t in range(tile_count):
            for k in range(capacity):
                row = (t * capacity + k) * rows
                wide_ref[row : row + rows, :] = arrived_ref[t, k * chunks + c].astype(jnp.float32)
        across = wide_ref[...].T.astype(jnp.bfloat16)
        turned_ref[c * LANES : (c + 1) * LANES, :] = jnp.dot(
            across, hot, preferred_element_type=jnp.float32
        )
    size = square_ref.shape[0]
    square_ref[...] = turned_ref[:size, :size].astype(jnp.bfloat16)
    column = turned_ref[:size, size:] + turned_ref[size:, :size].T
    high = column.astype(jnp.bfloat16)
    last_ref[:size, :LANES] = high
    last_ref[:size, LANES:] = (column - high.astype(jnp.float32)).astype(jnp.bfloat16)
    last_ref[size:, :LANES] = turned_ref[size:, size:].astype(jnp.bfloat16)
    last_ref[size:, LANES:] = jnp.zeros((LANES, LANES), jnp.bfloat16)


def half_density(piece, square_ref, last_ref, values_ref, out_ref):
    half = out_ref.shape[1]
    size = square_ref.shape[0]
    width = 256
    for q in range(values_ref.shape[1] // piece):
        runs = []
        for start in range(q * piece, (q + 1) * piece, width):
            lanes = slice(start, start + width)
            block, end = values_ref[:size, lanes], values_ref[size:, lanes]
            mixed = jnp.dot(
                last_ref[...],
                jnp.concatenate([end, end], axis=0),
                preferred_element_type=jnp.float32,
            )
            inner = mixed[:size] + jnp.dot(
                square_ref[...], block, preferred_element_type=jnp.float32
            )
            run = jnp.sum(inner * block.astype(jnp.float32), axis=0, keepdims=True)
            runs.append(
                run + jnp.sum(mixed[size:] * end.astype(jnp.float32), axis=0, keepdims=True)
            )
        density = jnp.concatenate(runs, axis=1)
        for p in range(piece // half):
            row = q * (piece // half) + p
            out_ref[row : row + 1, :] = density[:, p * half : (p + 1) * half]


def near_kernel(
    capacity, chunks, piece, arrived_ref, near_ref, far_hbm,
    out_ref, place_ref, square_ref, last_ref, far_ref, wide_ref, turned_ref, sem,
):
    copy = pltpu.make_async_copy(far_hbm, far_ref, sem.at[0])
    copy.start()
    arrange(capacity, chunks, arrived_ref, place_ref, square_ref, last_ref, wide_ref, turned_ref)
    half_density(piece, square_ref, last_ref, near_ref, out_ref)
    copy.wait()


def far_kernel(piece, square_ref, last_ref, far_ref, out_ref):
    half_density(piece, square_ref, last_ref, far_ref, out_ref)


def join_kernel(near_ref, far_ref, wrap_ref, pair_ref, out_ref, top_ref, bottom_ref):
    half = near_ref.shape[1]
    odd = odd_row() == 1
    blocks = (
        jnp.where(odd, pair_ref[...], wrap_ref[...]),
        jnp.where(odd, far_ref[...], near_ref[...]),
        jnp.where(odd, near_ref[...], far_ref[...]),
        jnp.where(odd, wrap_ref[...], pair_ref[...]),
    )
    for i, block in enumerate(blocks):
        out_ref[:, i * half : (i + 1) * half] = block
    top_ref[...] = out_ref[: top_ref.shape[0], :]
    bottom_ref[...] = out_ref[out_ref.shape[0] - bottom_ref.shape[0] :, :]


def split_dot(left, high, low):
    left_high = left.astype(jnp.bfloat16)
    left_low = (left - left_high.astype(jnp.float32)).astype(jnp.bfloat16)
    out = jnp.dot(left_high, high, preferred_element_type=jnp.float32)
    out = out + jnp.dot(left_low, high, preferred_element_type=jnp.float32)
    return out + jnp.dot(left_high, low, preferred_element_type=jnp.float32)


def filter_kernel(parts, *refs):
    taps_ref, band_high, band_low, fold_high, fold_low = refs[:5]
    blocks = refs[5 : 5 + 3 * parts]
    out_ref, field_ref, grid_ref, first_ref, second_ref, third_ref = refs[5 + 3 * parts :]
    size_x, size_y, size_z = out_ref.shape
    wide_y, wide_x, lanes = first_ref.shape
    share = wide_y // 8
    for y_start in range(0, wide_y, share):
        for part in range(parts):
            start = 0
            for block in blocks[3 * part : 3 * part + 3]:
                rows = block.shape[0]
                for y in range(y_start, y_start + share):
                    grid_ref[y, start : start + rows, part * size_z : (part + 1) * size_z] = (
                        block[:, y * size_z : (y + 1) * size_z]
                    )
                start += rows
        chosen = slice(y_start, y_start + share)
        grid = grid_ref[chosen].reshape(share * wide_x, parts * size_z)
        first_ref[chosen] = split_dot(grid, band_high[...], band_low[...]).reshape(
            share, wide_x, lanes
        )

    def tap(distance, rows):
        return jnp.broadcast_to(taps_ref[distance : distance + 1, :], (rows, lanes))

    def smooth(y, carry):
        run = tap(0, wide_x) * first_ref[y + RADIUS]
        for d in range(1, RADIUS + 1):
            pair = first_ref[y + (RADIUS - d)] + first_ref[y + (RADIUS + d)]
            run = run + tap(d, wide_x) * pair
        second_ref[y] = run
        run = tap(0, size_x) * second_ref[y, RADIUS : RADIUS + size_x, :]
        for d in range(1, RADIUS + 1):
            pair = (
                second_ref[y, RADIUS - d : RADIUS - d + size_x, :]
                + second_ref[y, RADIUS + d : RADIUS + d + size_x, :]
            )
            run = run + tap(d, size_x) * pair
        third_ref[y] = run
        return carry

    lax.fori_loop(0, size_y, smooth, 0, unroll=4)
    filtered = third_ref[...].reshape(size_y * size_x, lanes)
    folded = split_dot(filtered, fold_high[...], fold_low[...]).reshape(size_y, size_x, size_z)
    for y in range(size_y):
        out_ref[:, y, :] = folded[y]
        field_ref[:, y * size_z : (y + 1) * size_z] = folded[y]


def potential_kernel(
    capacity, weight, piece, place_vmem, grid_ref, field_ref, near_ref, far_ref,
    out_ref, grid_hbm, right_ref, corner_ref, whole_ref, place_ref, sems,
):
    copies = [
        pltpu.make_async_copy(place_vmem, place_ref, sems.at[0]),
        pltpu.make_async_copy(grid_ref, grid_hbm, sems.at[1]),
    ]
    for copy in copies:
        copy.start()
    points = near_ref.shape[1]
    half = field_ref.shape[1] // 2
    odd = odd_row() == 1
    low, high = field_ref[:, :half] * weight, field_ref[:, half:] * weight
    first = True
    over_points = (((1,), (1,)), ((), ()))
    for values_ref, source in (
        (near_ref, jnp.where(odd, high, low)),
        (far_ref, jnp.where(odd, low, high)),
    ):
        for q in range(points // piece):
            field = jnp.concatenate(
                [
                    source[x : x + 1, :]
                    for x in range(q * piece // half, (q + 1) * piece // half)
                ],
                axis=1,
            )
            block = values_ref[:, q * piece : (q + 1) * piece]
            weighted = (field * block.astype(jnp.float32)).astype(jnp.bfloat16)
            right = lax.dot_general(
                block, weighted[LANES:], over_points, preferred_element_type=jnp.float32
            )
            corner = lax.dot_general(
                block[:LANES], weighted[:LANES], over_points, preferred_element_type=jnp.float32
            )
            right_ref[...] = right if first else right_ref[...] + right
            corner_ref[...] = corner if first else corner_ref[...] + corner
            first = False

    blocks, rows, _ = whole_ref.shape
    edge = LANES // rows
    whole_ref[:edge, :, :LANES] = corner_ref[...].reshape(edge, rows, -1).astype(jnp.bfloat16)
    whole_ref[edge:, :, :LANES] = (
        right_ref[:LANES].T.reshape(blocks - edge, rows, -1).astype(jnp.bfloat16)
    )
    whole_ref[:, :, LANES:] = right_ref[...].reshape(blocks, rows, -1).astype(jnp.bfloat16)
    for copy in copies:
        copy.wait()

    def visit(j, carry):
        t, k = j // capacity, j % capacity
        out_ref[t, k] = whole_ref[jnp.minimum(place_ref[0, j], blocks - 1)]
        return carry

    lax.fori_loop(0, out_ref.shape[0] * capacity, visit, 0, unroll=16)


def unpack_kernel(tile_count, tile_ref, back_ref, out_hbm, count_ref, sem):
    def visit(i, t, slot):
        pltpu.make_async_copy(back_ref.at[t, slot], out_hbm.at[i], sem.at[0]).start()

    for_each_slab(tile_ref, count_ref, tile_count, out_hbm.shape[0], visit)
    pltpu.make_async_copy(out_hbm, out_hbm, sem.at[0]).wait()


def moved(block, shifts):
    axes = tuple(shifts)
    sizes = [lax.axis_size(axis) for axis in axes]
    pairs = []
    for source in np.ndindex(*sizes):
        target = [(s + shifts[axis]) % n for s, axis, n in zip(source, axes, sizes)]
        pairs.append(
            (int(np.ravel_multi_index(source, sizes)), int(np.ravel_multi_index(target, sizes)))
        )
    return lax.ppermute(block, axes, pairs)


def band_tables(size_z, neighbours):
    tap_table, mix = kernel_tables(RADIUS)

    def band(shift):
        table = np.zeros((size_z, len(ALPHAS), size_z), np.float64)
        for m in range(len(ALPHAS)):
            for source in range(size_z):
                for target in range(size_z):
                    offset = source + shift - target
                    if abs(offset) <= RADIUS:
                        table[source, m, target] = tap_table[m][offset + RADIUS]
        return table.reshape(size_z, len(ALPHAS) * size_z)

    own, low, high = band(0), band(-size_z), band(size_z)
    bands = {0: [own + low + high], 1: [own, low + high], 2: [own, low, high]}[neighbours]
    taps = np.zeros((16, len(ALPHAS) * size_z), np.float64)
    for d in range(RADIUS + 1):
        taps[d] = np.repeat([row[RADIUS + d] for row in tap_table], size_z)
    fold = np.concatenate([mix[m] * np.eye(size_z) for m in range(len(ALPHAS))], axis=0)

    def split(table):
        high = table.astype(np.float32).astype(jnp.bfloat16)
        low = (table - high.astype(np.float64)).astype(np.float32).astype(jnp.bfloat16)
        return [high, low]

    return [taps.astype(np.float32), *split(np.concatenate(bands, axis=0)), *split(fold)]


def local(orbital_values, dm_slabs, slab_tile, slab_place):
    size_x, size_y, size_z, list_orb = orbital_values.shape
    slab_count, atom_orb, _ = dm_slabs.shape
    list_blk = list_orb // atom_orb
    tile_count = lax.axis_size("gx") * lax.axis_size("gy")
    capacity = max(2, 2 * ((list_blk + tile_count - 1) // tile_count))
    chunks = list_orb // LANES
    tile_points = size_x * size_y * size_z
    plane = size_y * size_z
    counts = pltpu.SMEM((tile_count,), jnp.int32)

    groups = math.gcd(tile_count, 4)
    packed_shape = (tile_count, capacity * chunks + 1, atom_orb, LANES)
    packed = pl.pallas_call(
        functools.partial(pack_kernel, capacity, chunks, float(list_blk), groups),
        out_shape=jax.ShapeDtypeStruct(packed_shape, jnp.bfloat16),
        in_specs=[HBM_SPEC] * 3,
        out_specs=HBM_SPEC,
        scratch_shapes=[
            pltpu.SMEM((slab_count,), jnp.int32),
            pltpu.SMEM((slab_count,), jnp.int32),
            pltpu.VMEM(dm_slabs.shape, dm_slabs.dtype),
            counts,
            pltpu.SMEM((tile_count * capacity,), jnp.int32),
            pltpu.VMEM((tile_count, atom_orb, LANES), jnp.float32),
            pltpu.VMEM(packed_shape, jnp.bfloat16),
            pltpu.SemaphoreType.DMA((3,)),
            pltpu.SemaphoreType.DMA((groups,)),
        ],
        compiler_params=grant(4),
        name="pack",
    )(in_hbm(slab_tile), in_hbm(slab_place), in_hbm(dm_slabs))
    arrived = lax.all_to_all(packed, ("gx", "gy"), split_axis=0, concat_axis=0, tiled=True)
    half = plane // 2
    half_points = tile_points // 2
    piece = 4 * half
    bf16 = lambda *shape: jax.ShapeDtypeStruct(shape, jnp.bfloat16)
    f32 = lambda *shape: jax.ShapeDtypeStruct(shape, jnp.float32)
    near, far = pl.pallas_call(
        functools.partial(turn_kernel, size_x),
        out_shape=(
            pltpu.VMEM((list_orb, half_points), jnp.bfloat16),
            bf16(list_orb, half_points),
        ),
        in_specs=[HBM_SPEC],
        out_specs=(VMEM_SPEC, HBM_SPEC),
        scratch_shapes=[
            pltpu.VMEM((tile_points, list_orb), jnp.bfloat16),
            pltpu.VMEM((list_orb, half_points), jnp.bfloat16),
            pltpu.SemaphoreType.DMA((size_x // 2,)),
            pltpu.SemaphoreType.DMA((1,)),
        ],
        compiler_params=grant(20),
        cost_estimate=cost(0, 4 * tile_points * list_orb),
        name="turn",
    )(in_hbm(orbital_values.reshape(tile_points, list_orb)))

    slots = LANES * ((tile_count * capacity + LANES - 1) // LANES)
    product = 2 * half_points * list_orb * list_orb
    near_y, places, square, last, far = pl.pallas_call(
        functools.partial(near_kernel, capacity, chunks, piece),
        out_shape=(
            f32(size_x, half),
            jax.ShapeDtypeStruct((1, slots), jnp.int32),
            bf16(list_orb - LANES, list_orb - LANES),
            bf16(list_orb, 2 * LANES),
            pltpu.VMEM((list_orb, half_points), jnp.bfloat16),
        ),
        in_specs=[VMEM_SPEC, VMEM_SPEC, HBM_SPEC],
        out_specs=(VMEM_SPEC,) * 5,
        scratch_shapes=[
            pltpu.VMEM((tile_count * capacity * atom_orb, LANES), jnp.float32),
            pltpu.VMEM((list_orb, list_orb), jnp.float32),
            pltpu.SemaphoreType.DMA((1,)),
        ],
        compiler_params=grant(20),
        cost_estimate=cost(product, 2 * half_points * list_orb),
        name="near",
    )(arrived, near, in_hbm(far))
    rows = lax.axis_size("gy")
    pair = [(i, i ^ 1) for i in range(rows)]
    wrap = [(i, (i - 1 + 2 * (i % 2)) % rows) for i in range(rows)]
    from_wrap = lax.ppermute(near_y, "gy", wrap)
    far_y = pl.pallas_call(
        functools.partial(far_kernel, piece),
        out_shape=f32(size_x, half),
        in_specs=[VMEM_SPEC] * 3,
        out_specs=VMEM_SPEC,
        compiler_params=grant(20),
        cost_estimate=cost(product, 2 * half_points * list_orb),
        name="far",
    )(square, last, far)
    from_pair = lax.ppermute(far_y, "gy", pair)

    wide = 2 * plane
    own, top, bottom = pl.pallas_call(
        join_kernel,
        out_shape=(f32(size_x, wide), f32(RADIUS, wide), f32(RADIUS, wide)),
        in_specs=[VMEM_SPEC] * 4,
        out_specs=(VMEM_SPEC,) * 3,
        compiler_params=grant(2),
        name="join",
    )(near_y, far_y, from_wrap, from_pair)
    layers = lax.axis_size("gz")
    blocks = []
    for shift in {1: [0], 2: [0, 1]}.get(layers, [0, 1, -1]):
        blocks.append(moved(bottom, {"gx": 1, "gz": shift}))
        blocks.append(moved(own, {"gz": shift}) if shift else own)
        blocks.append(moved(top, {"gx": -1, "gz": shift}))
    parts = len(blocks) // 3
    tables = band_tables(size_z, parts - 1)
    lanes = tables[0].shape[1]
    wide_x, wide_y = size_x + 2 * RADIUS, size_y + 2 * RADIUS
    potential, field = pl.pallas_call(
        functools.partial(filter_kernel, parts),
        out_shape=(pltpu.VMEM((size_x, size_y, size_z), jnp.float32), f32(size_x, plane)),
        in_specs=[VMEM_SPEC] * (len(tables) + len(blocks)),
        out_specs=(VMEM_SPEC,) * 2,
        scratch_shapes=[
            pltpu.VMEM((wide_y, wide_x, parts * size_z), jnp.float32),
            pltpu.VMEM((wide_y, wide_x, lanes), jnp.float32),
            pltpu.VMEM((size_y, wide_x, lanes), jnp.float32),
            pltpu.VMEM((size_y, size_x, lanes), jnp.float32),
        ],
        compiler_params=grant(12),
        name="filter",
    )(*map(jnp.asarray, tables), *blocks)

    returned, potential = pl.pallas_call(
        functools.partial(
            potential_kernel, capacity, float(tile_points) ** (-0.5), 4 * piece
        ),
        out_shape=(
            bf16(tile_count, capacity, atom_orb, list_orb),
            f32(size_x, size_y, size_z),
        ),
        in_specs=[VMEM_SPEC] * 5,
        out_specs=(VMEM_SPEC, HBM_SPEC),
        scratch_shapes=[
            pltpu.VMEM((list_orb, list_orb - LANES), jnp.float32),
            pltpu.VMEM((LANES, LANES), jnp.float32),
            pltpu.VMEM((list_blk, atom_orb, list_orb), jnp.bfloat16),
            pltpu.SMEM((1, slots), jnp.int32),
            pltpu.SemaphoreType.DMA((2,)),
        ],
        compiler_params=grant(20),
        name="potential",
    )(places, potential, field, near, far)
    back = lax.all_to_all(returned, ("gx", "gy"), split_axis=0, concat_axis=0, tiled=True)
    own_rows = pl.pallas_call(
        functools.partial(unpack_kernel, tile_count),
        out_shape=bf16(slab_count, atom_orb, list_orb),
        in_specs=[SMEM_SPEC, VMEM_SPEC],
        out_specs=HBM_SPEC,
        scratch_shapes=[counts, pltpu.SemaphoreType.DMA((1,))],
        compiler_params=grant(4),
        name="unpack",
    )(slab_tile, back)
    return (potential, own_rows)


def solution(mesh):
    placed = (
        P("gx", "gy", "gz", None),
        P(("gx", "gy", "gz"), None, None),
        P(("gx", "gy", "gz")),
        P(("gx", "gy", "gz")),
    )

    return jax.shard_map(
        local,
        mesh=mesh,
        in_specs=placed,
        out_specs=(P("gx", "gy", "gz"), P(("gx", "gy", "gz"), None, None)),
        check_vma=False,
    )
```

```python
import functools
import math

import jax
import jax.numpy as jnp
import numpy as np
from jax import lax
from jax.experimental import pallas as pl
from jax.experimental.pallas import tpu as pltpu
from jax.sharding import PartitionSpec as P


RADIUS = 8
LANES = 128

ALPHAS = (0.012, 0.025, 0.05, 0.1, 0.2, 0.4, 0.8, 1.6)
MIXES = (0.3, 0.3, 0.32, 0.34, 0.36, 0.38, 0.4, 0.42)

VMEM_SPEC = pl.BlockSpec(memory_space=pltpu.VMEM)
SMEM_SPEC = pl.BlockSpec(memory_space=pltpu.SMEM)
HBM_SPEC = pl.BlockSpec(memory_space=pltpu.HBM)


def in_hbm(array):
    return pltpu.with_memory_space_constraint(array, pltpu.HBM)


def grant(mebibytes):
    return pltpu.CompilerParams(vmem_limit_bytes=mebibytes << 20)


def kernel_tables(radius):
    tap_table = [
        [math.exp(-alpha * offset * offset) for offset in range(-radius, radius + 1)]
        for alpha in ALPHAS
    ]
    mix = [
        MIXES[term] / sum((tap * tap for tap in tap_table[term])) ** 1.5
        for term in range(len(ALPHAS))
    ]
    return (tap_table, mix)


def cost(flops, moved_bytes):
    return pl.CostEstimate(flops=flops, bytes_accessed=moved_bytes, transcendentals=0)


def for_each_slab(tile_ref, count_ref, tile_count, slab_count, visit):
    for t in range(tile_count):
        count_ref[t] = 0

    def step(i, carry):
        t = tile_ref[i]
        slot = count_ref[t]
        count_ref[t] = slot + 1
        visit(i, t, slot)
        return carry

    lax.fori_loop(0, slab_count, step, 0, unroll=4)


def pack_kernel(
    capacity, chunks, empty, groups, tile_hbm, place_hbm, slab_hbm, out_hbm,
    tile_ref, place_ref, slab_ref, count_ref, index_ref, label_ref, out_ref, sems, out_sems,
):
    copies = [
        pltpu.make_async_copy(tile_hbm, tile_ref, sems.at[0]),
        pltpu.make_async_copy(place_hbm, place_ref, sems.at[1]),
        pltpu.make_async_copy(slab_hbm, slab_ref, sems.at[2]),
    ]
    for copy in copies:
        copy.start()
    tile_count = out_ref.shape[0]
    label_ref[...] = jnp.full(label_ref.shape, empty, jnp.float32)
    for j in range(tile_count * capacity):
        index_ref[j] = 0
    for copy in copies[:2]:
        copy.wait()

    def rank(i, t, slot):
        index_ref[t * capacity + slot] = i
        label = place_ref[i].astype(jnp.float32)
        label_ref[t, pl.ds(slot, 1), :] = jnp.full((1, LANES), label, jnp.float32)

    for_each_slab(tile_ref, count_ref, tile_count, slab_ref.shape[0], rank)
    copies[2].wait()

    def fill(t, carry):
        for k in range(capacity):
            slab = slab_ref[index_ref[t * capacity + k]]
            for c in range(chunks):
                out_ref[t, k * chunks + c] = slab[:, c * LANES : (c + 1) * LANES]
        out_ref[t, capacity * chunks] = label_ref[t].astype(jnp.bfloat16)
        return carry

    share = tile_count // groups
    for g in range(groups):
        lax.fori_loop(g * share, (g + 1) * share, fill, 0, unroll=min(share, 4))
        part = slice(g * share, (g + 1) * share)
        copies.append(pltpu.make_async_copy(out_ref.at[part], out_hbm.at[part], out_sems.at[g]))
        copies[-1].start()
    for copy in copies[3:]:
        copy.wait()


def odd_row():
    return lax.rem(lax.axis_index("gy"), 2)


def odd_column():
    return lax.rem(lax.axis_index("gx"), 2) == 1


def turn_kernel(planes, values_hbm, near_ref, far_hbm, values_ref, far_ref, sems, out_sem):
    points = values_ref.shape[0]
    plane = points // planes
    half = plane // 2
    copies = []
    for x in range(0, planes, 2):
        part = slice(x * plane, (x + 2) * plane)
        copies.append(
            pltpu.make_async_copy(values_hbm.at[part], values_ref.at[part], sems.at[x // 2])
        )
        copies[-1].start()
    near_start = (1 - odd_row()) * half
    for x in range(0, planes, 2):
        copies[x // 2].wait()
        for start, out_ref in ((near_start, near_ref), (half - near_start, far_ref)):
            rows = [
                values_ref[pl.ds(pl.multiple_of((x + i) * plane + start, half), half), :]
                for i in range(2)
            ]
            out_ref[:, x * half : (x + 2) * half] = jnp.concatenate(rows, axis=0).T
    copy = pltpu.make_async_copy(far_ref, far_hbm, out_sem.at[0])
    copy.start()
    copy.wait()


def arrange(capacity, chunks, arrived_ref, place_ref, square_ref, last_ref, wide_ref, turned_ref):
    tile_count, _, rows, _ = arrived_ref.shape
    slots = tile_count * capacity
    labels = arrived_ref[:, capacity * chunks].astype(jnp.float32)[:, :capacity]
    labels = labels.reshape(slots, LANES)
    width = place_ref.shape[1]
    for g in range(width // LANES):
        group = labels[g * LANES : (g + 1) * LANES]
        here = lax.broadcasted_iota(jnp.int32, group.shape, 0) == lax.broadcasted_iota(
            jnp.int32, group.shape, 1
        )
        place_ref[:, g * LANES : (g + 1) * LANES] = jnp.sum(
            jnp.where(here, group, 0.0), axis=0, keepdims=True
        ).astype(jnp.int32)
    first_row = jnp.broadcast_to(labels.reshape(slots, 1, LANES) * rows, (slots, rows, LANES))
    source = first_row + lax.broadcasted_iota(jnp.int32, (slots, rows, LANES), 1).astype(
        jnp.float32
    )
    lane = lax.broadcasted_iota(jnp.int32, (slots, rows, LANES), 2).astype(jnp.float32)
    hot = []
    for c in range(chunks):
        match = jnp.where(source == lane + float(c * LANES), 1.0, 0.0)
        hot.append(match.reshape(slots * rows, LANES).astype(jnp.bfloat16))
    hot = jnp.concatenate(hot, axis=1)
    for c in range(chunks):
        for t in range(tile_count):
            for k in range(capacity):
                row = (t * capacity + k) * rows
                wide_ref[row : row + rows, :] = arrived_ref[t, k * chunks + c].astype(jnp.float32)
        across = wide_ref[...].T.astype(jnp.bfloat16)
        turned_ref[c * LANES : (c + 1) * LANES, :] = jnp.dot(
            across, hot, preferred_element_type=jnp.float32
        )
    size = square_ref.shape[0]
    square_ref[...] = turned_ref[:size, :size].astype(jnp.bfloat16)
    column = turned_ref[:size, size:] + turned_ref[size:, :size].T
    high = column.astype(jnp.bfloat16)
    last_ref[:size, :LANES] = high
    last_ref[:size, LANES:] = (column - high.astype(jnp.float32)).astype(jnp.bfloat16)
    last_ref[size:, :LANES] = turned_ref[size:, size:].astype(jnp.bfloat16)
    last_ref[size:, LANES:] = jnp.zeros((LANES, LANES), jnp.bfloat16)


def half_density(piece, square_ref, last_ref, values_ref, out_ref):
    half = out_ref.shape[1]
    size = square_ref.shape[0]
    width = 256
    for q in range(values_ref.shape[1] // piece):
        runs = []
        for start in range(q * piece, (q + 1) * piece, width):
            lanes = slice(start, start + width)
            block, end = values_ref[:size, lanes], values_ref[size:, lanes]
            mixed = jnp.dot(
                last_ref[...],
                jnp.concatenate([end, end], axis=0),
                preferred_element_type=jnp.float32,
            )
            inner = mixed[:size] + jnp.dot(
                square_ref[...], block, preferred_element_type=jnp.float32
            )
            run = jnp.sum(inner * block.astype(jnp.float32), axis=0, keepdims=True)
            runs.append(
                run + jnp.sum(mixed[size:] * end.astype(jnp.float32), axis=0, keepdims=True)
            )
        density = jnp.concatenate(runs, axis=1)
        for p in range(piece // half):
            row = q * (piece // half) + p
            out_ref[row : row + 1, :] = density[:, p * half : (p + 1) * half]


def near_kernel(
    capacity, chunks, piece, arrived_ref, near_ref, far_hbm,
    out_ref, place_ref, square_ref, last_ref, far_ref, wide_ref, turned_ref, sem,
):
    copy = pltpu.make_async_copy(far_hbm, far_ref, sem.at[0])
    copy.start()
    arrange(capacity, chunks, arrived_ref, place_ref, square_ref, last_ref, wide_ref, turned_ref)
    half_density(piece, square_ref, last_ref, near_ref, out_ref)
    copy.wait()


def far_kernel(piece, square_ref, last_ref, far_ref, out_ref):
    half_density(piece, square_ref, last_ref, far_ref, out_ref)


def join_kernel(near_ref, far_ref, wrap_ref, pair_ref, out_ref, to_wrap_ref, to_pair_ref):
    half = near_ref.shape[1]
    odd = odd_row() == 1
    blocks = (
        jnp.where(odd, pair_ref[...], wrap_ref[...]),
        jnp.where(odd, near_ref[...], far_ref[...]),
        jnp.where(odd, far_ref[...], near_ref[...]),
        jnp.where(odd, wrap_ref[...], pair_ref[...]),
    )
    for i, block in enumerate(blocks):
        out_ref[:, i * half : (i + 1) * half] = block
    rows = to_wrap_ref.shape[0]
    top, bottom = out_ref[:rows, :], out_ref[out_ref.shape[0] - rows :, :]
    to_wrap_ref[...] = jnp.where(odd_column(), bottom, top)
    to_pair_ref[...] = jnp.where(odd_column(), top, bottom)


def split_dot(left, high, low):
    left_high = left.astype(jnp.bfloat16)
    left_low = (left - left_high.astype(jnp.float32)).astype(jnp.bfloat16)
    out = jnp.dot(left_high, high, preferred_element_type=jnp.float32)
    out = out + jnp.dot(left_low, high, preferred_element_type=jnp.float32)
    return out + jnp.dot(left_high, low, preferred_element_type=jnp.float32)


def filter_kernel(parts, *refs):
    taps_ref, band_high, band_low, fold_high, fold_low = refs[:5]
    blocks = refs[5 : 5 + 3 * parts]
    out_ref, field_ref, grid_ref, first_ref, second_ref, third_ref = refs[5 + 3 * parts :]
    size_x, size_y, size_z = out_ref.shape
    wide_y, wide_x, lanes = first_ref.shape
    odd = odd_column()
    grids = []
    for part in range(parts):
        wrap, own, pair = (block[...] for block in blocks[3 * part : 3 * part + 3])
        grids.append((jnp.where(odd, pair, wrap), own, jnp.where(odd, wrap, pair)))
    share = wide_y // 8
    for y_start in range(0, wide_y, share):
        for part in range(parts):
            start = 0
            for block in grids[part]:
                rows = block.shape[0]
                for y in range(y_start, y_start + share):
                    grid_ref[y, start : start + rows, part * size_z : (part + 1) * size_z] = (
                        block[:, y * size_z : (y + 1) * size_z]
                    )
                start += rows
        chosen = slice(y_start, y_start + share)
        grid = grid_ref[chosen].reshape(share * wide_x, parts * size_z)
        first_ref[chosen] = split_dot(grid, band_high[...], band_low[...]).reshape(
            share, wide_x, lanes
        )

    def tap(distance, rows):
        return jnp.broadcast_to(taps_ref[distance : distance + 1, :], (rows, lanes))

    def smooth(y, carry):
        run = tap(0, wide_x) * first_ref[y + RADIUS]
        for d in range(1, RADIUS + 1):
            pair = first_ref[y + (RADIUS - d)] + first_ref[y + (RADIUS + d)]
            run = run + tap(d, wide_x) * pair
        second_ref[y] = run
        run = tap(0, size_x) * second_ref[y, RADIUS : RADIUS + size_x, :]
        for d in range(1, RADIUS + 1):
            pair = (
                second_ref[y, RADIUS - d : RADIUS - d + size_x, :]
                + second_ref[y, RADIUS + d : RADIUS + d + size_x, :]
            )
            run = run + tap(d, size_x) * pair
        third_ref[y] = run
        return carry

    lax.fori_loop(0, size_y, smooth, 0, unroll=4)
    filtered = third_ref[...].reshape(size_y * size_x, lanes)
    folded = split_dot(filtered, fold_high[...], fold_low[...]).reshape(size_y, size_x, size_z)
    for y in range(size_y):
        out_ref[:, y, :] = folded[y]
        field_ref[:, y * size_z : (y + 1) * size_z] = folded[y]


def potential_kernel(
    capacity, weight, piece, place_vmem, grid_ref, field_ref, near_ref, far_ref,
    out_ref, grid_hbm, right_ref, corner_ref, whole_ref, place_ref, sems,
):
    copies = [
        pltpu.make_async_copy(place_vmem, place_ref, sems.at[0]),
        pltpu.make_async_copy(grid_ref, grid_hbm, sems.at[1]),
    ]
    for copy in copies:
        copy.start()
    points = near_ref.shape[1]
    half = field_ref.shape[1] // 2
    odd = odd_row() == 1
    low, high = field_ref[:, :half] * weight, field_ref[:, half:] * weight
    first = True
    over_points = (((1,), (1,)), ((), ()))
    for values_ref, source in (
        (near_ref, jnp.where(odd, low, high)),
        (far_ref, jnp.where(odd, high, low)),
    ):
        for q in range(points // piece):
            field = jnp.concatenate(
                [
                    source[x : x + 1, :]
                    for x in range(q * piece // half, (q + 1) * piece // half)
                ],
                axis=1,
            )
            block = values_ref[:, q * piece : (q + 1) * piece]
            weighted = (field * block.astype(jnp.float32)).astype(jnp.bfloat16)
            right = lax.dot_general(
                block, weighted[LANES:], over_points, preferred_element_type=jnp.float32
            )
            corner = lax.dot_general(
                block[:LANES], weighted[:LANES], over_points, preferred_element_type=jnp.float32
            )
            right_ref[...] = right if first else right_ref[...] + right
            corner_ref[...] = corner if first else corner_ref[...] + corner
            first = False

    blocks, rows, _ = whole_ref.shape
    edge = LANES // rows
    whole_ref[:edge, :, :LANES] = corner_ref[...].reshape(edge, rows, -1).astype(jnp.bfloat16)
    whole_ref[edge:, :, :LANES] = (
        right_ref[:LANES].T.reshape(blocks - edge, rows, -1).astype(jnp.bfloat16)
    )
    whole_ref[:, :, LANES:] = right_ref[...].reshape(blocks, rows, -1).astype(jnp.bfloat16)
    for copy in copies:
        copy.wait()

    def visit(j, carry):
        t, k = j // capacity, j % capacity
        out_ref[t, k] = whole_ref[jnp.minimum(place_ref[0, j], blocks - 1)]
        return carry

    lax.fori_loop(0, out_ref.shape[0] * capacity, visit, 0, unroll=16)


def unpack_kernel(tile_count, tile_ref, back_ref, out_hbm, count_ref, sem):
    def visit(i, t, slot):
        pltpu.make_async_copy(back_ref.at[t, slot], out_hbm.at[i], sem.at[0]).start()

    for_each_slab(tile_ref, count_ref, tile_count, out_hbm.shape[0], visit)
    pltpu.make_async_copy(out_hbm, out_hbm, sem.at[0]).wait()


def wrap_of(i):
    return i - 1 + 2 * (i % 2)


def pair_of(i):
    return i + 1 - 2 * (i % 2)


def moved(block, targets):
    axes = tuple(targets)
    sizes = [lax.axis_size(axis) for axis in axes]
    pairs = []
    for source in np.ndindex(*sizes):
        target = [targets[axis](i) % n for i, axis, n in zip(source, axes, sizes)]
        pairs.append(
            (int(np.ravel_multi_index(source, sizes)), int(np.ravel_multi_index(target, sizes)))
        )
    return lax.ppermute(block, axes, pairs)


def band_tables(size_z, neighbours):
    tap_table, mix = kernel_tables(RADIUS)

    def band(shift):
        table = np.zeros((size_z, len(ALPHAS), size_z), np.float64)
        for m in range(len(ALPHAS)):
            for source in range(size_z):
                for target in range(size_z):
                    offset = source + shift - target
                    if abs(offset) <= RADIUS:
                        table[source, m, target] = tap_table[m][offset + RADIUS]
        return table.reshape(size_z, len(ALPHAS) * size_z)

    own, low, high = band(0), band(-size_z), band(size_z)
    bands = {0: [own + low + high], 1: [own, low + high], 2: [own, low, high]}[neighbours]
    taps = np.zeros((16, len(ALPHAS) * size_z), np.float64)
    for d in range(RADIUS + 1):
        taps[d] = np.repeat([row[RADIUS + d] for row in tap_table], size_z)
    fold = np.concatenate([mix[m] * np.eye(size_z) for m in range(len(ALPHAS))], axis=0)

    def split(table):
        high = table.astype(np.float32).astype(jnp.bfloat16)
        low = (table - high.astype(np.float64)).astype(np.float32).astype(jnp.bfloat16)
        return [high, low]

    return [taps.astype(np.float32), *split(np.concatenate(bands, axis=0)), *split(fold)]


def local(orbital_values, dm_slabs, slab_tile, slab_place):
    size_x, size_y, size_z, list_orb = orbital_values.shape
    slab_count, atom_orb, _ = dm_slabs.shape
    list_blk = list_orb // atom_orb
    tile_count = lax.axis_size("gx") * lax.axis_size("gy")
    capacity = max(2, 2 * ((list_blk + tile_count - 1) // tile_count))
    chunks = list_orb // LANES
    tile_points = size_x * size_y * size_z
    plane = size_y * size_z
    counts = pltpu.SMEM((tile_count,), jnp.int32)

    groups = math.gcd(tile_count, 4)
    packed_shape = (tile_count, capacity * chunks + 1, atom_orb, LANES)
    packed = pl.pallas_call(
        functools.partial(pack_kernel, capacity, chunks, float(list_blk), groups),
        out_shape=jax.ShapeDtypeStruct(packed_shape, jnp.bfloat16),
        in_specs=[HBM_SPEC] * 3,
        out_specs=HBM_SPEC,
        scratch_shapes=[
            pltpu.SMEM((slab_count,), jnp.int32),
            pltpu.SMEM((slab_count,), jnp.int32),
            pltpu.VMEM(dm_slabs.shape, dm_slabs.dtype),
            counts,
            pltpu.SMEM((tile_count * capacity,), jnp.int32),
            pltpu.VMEM((tile_count, atom_orb, LANES), jnp.float32),
            pltpu.VMEM(packed_shape, jnp.bfloat16),
            pltpu.SemaphoreType.DMA((3,)),
            pltpu.SemaphoreType.DMA((groups,)),
        ],
        compiler_params=grant(4),
        name="pack",
    )(in_hbm(slab_tile), in_hbm(slab_place), in_hbm(dm_slabs))
    arrived = lax.all_to_all(packed, ("gx", "gy"), split_axis=0, concat_axis=0, tiled=True)
    half = plane // 2
    half_points = tile_points // 2
    piece = 4 * half
    bf16 = lambda *shape: jax.ShapeDtypeStruct(shape, jnp.bfloat16)
    f32 = lambda *shape: jax.ShapeDtypeStruct(shape, jnp.float32)
    near, far = pl.pallas_call(
        functools.partial(turn_kernel, size_x),
        out_shape=(
            pltpu.VMEM((list_orb, half_points), jnp.bfloat16),
            bf16(list_orb, half_points),
        ),
        in_specs=[HBM_SPEC],
        out_specs=(VMEM_SPEC, HBM_SPEC),
        scratch_shapes=[
            pltpu.VMEM((tile_points, list_orb), jnp.bfloat16),
            pltpu.VMEM((list_orb, half_points), jnp.bfloat16),
            pltpu.SemaphoreType.DMA((size_x // 2,)),
            pltpu.SemaphoreType.DMA((1,)),
        ],
        compiler_params=grant(20),
        cost_estimate=cost(0, 4 * tile_points * list_orb),
        name="turn",
    )(in_hbm(orbital_values.reshape(tile_points, list_orb)))

    slots = LANES * ((tile_count * capacity + LANES - 1) // LANES)
    product = 2 * half_points * list_orb * list_orb
    near_y, places, square, last, far = pl.pallas_call(
        functools.partial(near_kernel, capacity, chunks, piece),
        out_shape=(
            f32(size_x, half),
            jax.ShapeDtypeStruct((1, slots), jnp.int32),
            bf16(list_orb - LANES, list_orb - LANES),
            bf16(list_orb, 2 * LANES),
            pltpu.VMEM((list_orb, half_points), jnp.bfloat16),
        ),
        in_specs=[VMEM_SPEC, VMEM_SPEC, HBM_SPEC],
        out_specs=(VMEM_SPEC,) * 5,
        scratch_shapes=[
            pltpu.VMEM((tile_count * capacity * atom_orb, LANES), jnp.float32),
            pltpu.VMEM((list_orb, list_orb), jnp.float32),
            pltpu.SemaphoreType.DMA((1,)),
        ],
        compiler_params=grant(20),
        cost_estimate=cost(product, 2 * half_points * list_orb),
        name="near",
    )(arrived, near, in_hbm(far))
    from_pair = moved(near_y, {"gy": pair_of})
    far_y = pl.pallas_call(
        functools.partial(far_kernel, piece),
        out_shape=f32(size_x, half),
        in_specs=[VMEM_SPEC] * 3,
        out_specs=VMEM_SPEC,
        compiler_params=grant(20),
        cost_estimate=cost(product, 2 * half_points * list_orb),
        name="far",
    )(square, last, far)
    from_wrap = moved(far_y, {"gy": wrap_of})

    wide = 2 * plane
    own, to_wrap, to_pair = pl.pallas_call(
        join_kernel,
        out_shape=(f32(size_x, wide), f32(RADIUS, wide), f32(RADIUS, wide)),
        in_specs=[VMEM_SPEC] * 4,
        out_specs=(VMEM_SPEC,) * 3,
        compiler_params=grant(2),
        name="join",
    )(near_y, far_y, from_wrap, from_pair)
    layers = lax.axis_size("gz")
    blocks = []
    for shift in {1: [0], 2: [0, 1]}.get(layers, [0, 1, -1]):
        along = {"gz": lambda layer: layer + shift} if shift else {}
        blocks.append(moved(to_wrap, {"gx": wrap_of, **along}))
        blocks.append(moved(own, along) if shift else own)
        blocks.append(moved(to_pair, {"gx": pair_of, **along}))
    parts = len(blocks) // 3
    tables = band_tables(size_z, parts - 1)
    lanes = tables[0].shape[1]
    wide_x, wide_y = size_x + 2 * RADIUS, size_y + 2 * RADIUS
    potential, field = pl.pallas_call(
        functools.partial(filter_kernel, parts),
        out_shape=(pltpu.VMEM((size_x, size_y, size_z), jnp.float32), f32(size_x, plane)),
        in_specs=[VMEM_SPEC] * (len(tables) + len(blocks)),
        out_specs=(VMEM_SPEC,) * 2,
        scratch_shapes=[
            pltpu.VMEM((wide_y, wide_x, parts * size_z), jnp.float32),
            pltpu.VMEM((wide_y, wide_x, lanes), jnp.float32),
            pltpu.VMEM((size_y, wide_x, lanes), jnp.float32),
            pltpu.VMEM((size_y, size_x, lanes), jnp.float32),
        ],
        compiler_params=grant(12),
        name="filter",
    )(*map(jnp.asarray, tables), *blocks)

    returned, potential = pl.pallas_call(
        functools.partial(
            potential_kernel, capacity, float(tile_points) ** (-0.5), 4 * piece
        ),
        out_shape=(
            bf16(tile_count, capacity, atom_orb, list_orb),
            f32(size_x, size_y, size_z),
        ),
        in_specs=[VMEM_SPEC] * 5,
        out_specs=(VMEM_SPEC, HBM_SPEC),
        scratch_shapes=[
            pltpu.VMEM((list_orb, list_orb - LANES), jnp.float32),
            pltpu.VMEM((LANES, LANES), jnp.float32),
            pltpu.VMEM((list_blk, atom_orb, list_orb), jnp.bfloat16),
            pltpu.SMEM((1, slots), jnp.int32),
            pltpu.SemaphoreType.DMA((2,)),
        ],
        compiler_params=grant(20),
        name="potential",
    )(places, potential, field, near, far)
    back = lax.all_to_all(returned, ("gx", "gy"), split_axis=0, concat_axis=0, tiled=True)
    own_rows = pl.pallas_call(
        functools.partial(unpack_kernel, tile_count),
        out_shape=bf16(slab_count, atom_orb, list_orb),
        in_specs=[SMEM_SPEC, VMEM_SPEC],
        out_specs=HBM_SPEC,
        scratch_shapes=[counts, pltpu.SemaphoreType.DMA((1,))],
        compiler_params=grant(4),
        name="unpack",
    )(slab_tile, back)
    return (potential, own_rows)


def solution(mesh):
    placed = (
        P("gx", "gy", "gz", None),
        P(("gx", "gy", "gz"), None, None),
        P(("gx", "gy", "gz")),
        P(("gx", "gy", "gz")),
    )

    return jax.shard_map(
        local,
        mesh=mesh,
        in_specs=placed,
        out_specs=(P("gx", "gy", "gz"), P(("gx", "gy", "gz"), None, None)),
        check_vma=False,
    )
```

```python
import functools
import math

import jax
import jax.numpy as jnp
import numpy as np
from jax import lax
from jax.experimental import pallas as pl
from jax.experimental.pallas import tpu as pltpu
from jax.sharding import PartitionSpec as P


RADIUS = 8
LANES = 128

ALPHAS = (0.012, 0.025, 0.05, 0.1, 0.2, 0.4, 0.8, 1.6)
MIXES = (0.3, 0.3, 0.32, 0.34, 0.36, 0.38, 0.4, 0.42)

VMEM_SPEC = pl.BlockSpec(memory_space=pltpu.VMEM)
SMEM_SPEC = pl.BlockSpec(memory_space=pltpu.SMEM)
HBM_SPEC = pl.BlockSpec(memory_space=pltpu.HBM)


def in_hbm(array):
    return pltpu.with_memory_space_constraint(array, pltpu.HBM)


def grant(mebibytes):
    return pltpu.CompilerParams(vmem_limit_bytes=mebibytes << 20)


def kernel_tables(radius):
    tap_table = [
        [math.exp(-alpha * offset * offset) for offset in range(-radius, radius + 1)]
        for alpha in ALPHAS
    ]
    mix = [
        MIXES[term] / sum((tap * tap for tap in tap_table[term])) ** 1.5
        for term in range(len(ALPHAS))
    ]
    return (tap_table, mix)


def cost(flops, moved_bytes):
    return pl.CostEstimate(flops=flops, bytes_accessed=moved_bytes, transcendentals=0)


def for_each_slab(tile_ref, count_ref, tile_count, slab_count, visit):
    for t in range(tile_count):
        count_ref[t] = 0

    def step(i, carry):
        t = tile_ref[i]
        slot = count_ref[t]
        count_ref[t] = slot + 1
        visit(i, t, slot)
        return carry

    lax.fori_loop(0, slab_count, step, 0, unroll=16)


def pack_kernel(
    capacity, chunks, empty, groups, tile_hbm, place_hbm, slab_hbm, out_hbm,
    tile_ref, place_ref, slab_ref, count_ref, index_ref, label_ref, out_ref, sems, out_sems,
):
    copies = [
        pltpu.make_async_copy(tile_hbm, tile_ref, sems.at[0]),
        pltpu.make_async_copy(place_hbm, place_ref, sems.at[1]),
        pltpu.make_async_copy(slab_hbm, slab_ref, sems.at[2]),
    ]
    for copy in copies:
        copy.start()
    tile_count = out_ref.shape[0]
    label_ref[...] = jnp.full(label_ref.shape, empty, jnp.float32)
    for j in range(tile_count * capacity):
        index_ref[j] = 0
    for copy in copies[:2]:
        copy.wait()

    def rank(i, t, slot):
        index_ref[t * capacity + slot] = i
        label = place_ref[i].astype(jnp.float32)
        label_ref[t, pl.ds(slot, 1), :] = jnp.full((1, LANES), label, jnp.float32)

    for_each_slab(tile_ref, count_ref, tile_count, slab_ref.shape[0], rank)
    copies[2].wait()

    def fill(t, carry):
        for k in range(capacity):
            slab = slab_ref[index_ref[t * capacity + k]]
            for c in range(chunks):
                out_ref[t, k * chunks + c] = slab[:, c * LANES : (c + 1) * LANES]
        out_ref[t, capacity * chunks] = label_ref[t].astype(jnp.bfloat16)
        return carry

    share = tile_count // groups
    for g in range(groups):
        lax.fori_loop(g * share, (g + 1) * share, fill, 0, unroll=min(share, 4))
        part = slice(g * share, (g + 1) * share)
        copies.append(pltpu.make_async_copy(out_ref.at[part], out_hbm.at[part], out_sems.at[g]))
        copies[-1].start()
    for copy in copies[3:]:
        copy.wait()


def odd_row():
    return lax.rem(lax.axis_index("gy"), 2)


def odd_column():
    return lax.rem(lax.axis_index("gx"), 2) == 1


def turn_kernel(planes, values_hbm, near_ref, far_hbm, values_ref, far_ref, sems, out_sem):
    points = values_ref.shape[0]
    plane = points // planes
    half = plane // 2
    copies = []
    for x in range(0, planes, 2):
        part = slice(x * plane, (x + 2) * plane)
        copies.append(
            pltpu.make_async_copy(values_hbm.at[part], values_ref.at[part], sems.at[x // 2])
        )
        copies[-1].start()
    near_start = odd_row() * half
    for x in range(0, planes, 2):
        copies[x // 2].wait()
        for start, out_ref in ((near_start, near_ref), (half - near_start, far_ref)):
            rows = [
                values_ref[pl.ds(pl.multiple_of((x + i) * plane + start, half), half), :]
                for i in range(2)
            ]
            out_ref[:, x * half : (x + 2) * half] = jnp.concatenate(rows, axis=0).T
    copy = pltpu.make_async_copy(far_ref, far_hbm, out_sem.at[0])
    copy.start()
    copy.wait()


def arrange(capacity, chunks, arrived_ref, place_ref, square_ref, last_ref, wide_ref, turned_ref):
    tile_count, _, rows, _ = arrived_ref.shape
    slots = tile_count * capacity
    labels = arrived_ref[:, capacity * chunks].astype(jnp.float32)[:, :capacity]
    labels = labels.reshape(slots, LANES)
    width = place_ref.shape[1]
    for g in range(width // LANES):
        group = labels[g * LANES : (g + 1) * LANES]
        here = lax.broadcasted_iota(jnp.int32, group.shape, 0) == lax.broadcasted_iota(
            jnp.int32, group.shape, 1
        )
        place_ref[:, g * LANES : (g + 1) * LANES] = jnp.sum(
            jnp.where(here, group, 0.0), axis=0, keepdims=True
        ).astype(jnp.int32)
    first_row = jnp.broadcast_to(labels.reshape(slots, 1, LANES) * rows, (slots, rows, LANES))
    source = first_row + lax.broadcasted_iota(jnp.int32, (slots, rows, LANES), 1).astype(
        jnp.float32
    )
    lane = lax.broadcasted_iota(jnp.int32, (slots, rows, LANES), 2).astype(jnp.float32)
    hot = []
    for c in range(chunks):
        match = jnp.where(source == lane + float(c * LANES), 1.0, 0.0)
        hot.append(match.reshape(slots * rows, LANES).astype(jnp.bfloat16))
    hot = jnp.concatenate(hot, axis=1)
    for c in range(chunks):
        for t in range(tile_count):
            for k in range(capacity):
                row = (t * capacity + k) * rows
                wide_ref[row : row + rows, :] = arrived_ref[t, k * chunks + c].astype(jnp.float32)
        across = wide_ref[...].T.astype(jnp.bfloat16)
        turned_ref[c * LANES : (c + 1) * LANES, :] = jnp.dot(
            across, hot, preferred_element_type=jnp.float32
        )
    size = square_ref.shape[0]
    square_ref[...] = turned_ref[:size, :size].astype(jnp.bfloat16)
    column = turned_ref[:size, size:] + turned_ref[size:, :size].T
    high = column.astype(jnp.bfloat16)
    last_ref[:size, :LANES] = high
    last_ref[:size, LANES:] = (column - high.astype(jnp.float32)).astype(jnp.bfloat16)
    last_ref[size:, :LANES] = turned_ref[size:, size:].astype(jnp.bfloat16)
    last_ref[size:, LANES:] = jnp.zeros((LANES, LANES), jnp.bfloat16)


def half_density(piece, square_ref, last_ref, values_ref, out_ref):
    half = out_ref.shape[1]
    size = square_ref.shape[0]
    width = 256
    for q in range(values_ref.shape[1] // piece):
        runs = []
        for start in range(q * piece, (q + 1) * piece, width):
            lanes = slice(start, start + width)
            block, end = values_ref[:size, lanes], values_ref[size:, lanes]
            mixed = jnp.dot(
                last_ref[...],
                jnp.concatenate([end, end], axis=0),
                preferred_element_type=jnp.float32,
            )
            inner = mixed[:size] + jnp.dot(
                square_ref[...], block, preferred_element_type=jnp.float32
            )
            run = jnp.sum(inner * block.astype(jnp.float32), axis=0, keepdims=True)
            runs.append(
                run + jnp.sum(mixed[size:] * end.astype(jnp.float32), axis=0, keepdims=True)
            )
        density = jnp.concatenate(runs, axis=1)
        for p in range(piece // half):
            row = q * (piece // half) + p
            out_ref[row : row + 1, :] = density[:, p * half : (p + 1) * half]


def near_kernel(
    capacity, chunks, piece, arrived_ref, near_ref, far_hbm,
    out_ref, place_ref, square_ref, last_ref, far_ref, wide_ref, turned_ref, sem,
):
    copy = pltpu.make_async_copy(far_hbm, far_ref, sem.at[0])
    copy.start()
    arrange(capacity, chunks, arrived_ref, place_ref, square_ref, last_ref, wide_ref, turned_ref)
    half_density(piece, square_ref, last_ref, near_ref, out_ref)
    copy.wait()


def far_kernel(piece, square_ref, last_ref, far_ref, out_ref):
    half_density(piece, square_ref, last_ref, far_ref, out_ref)


def join_kernel(near_ref, far_ref, wrap_ref, pair_ref, out_ref, to_wrap_ref, to_pair_ref):
    half = near_ref.shape[1]
    odd = odd_row() == 1
    blocks = (
        jnp.where(odd, pair_ref[...], wrap_ref[...]),
        jnp.where(odd, far_ref[...], near_ref[...]),
        jnp.where(odd, near_ref[...], far_ref[...]),
        jnp.where(odd, wrap_ref[...], pair_ref[...]),
    )
    for i, block in enumerate(blocks):
        out_ref[:, i * half : (i + 1) * half] = block
    rows = to_wrap_ref.shape[0]
    top, bottom = out_ref[:rows, :], out_ref[out_ref.shape[0] - rows :, :]
    to_wrap_ref[...] = jnp.where(odd_column(), bottom, top)
    to_pair_ref[...] = jnp.where(odd_column(), top, bottom)


def split_dot(left, high, low):
    left_high = left.astype(jnp.bfloat16)
    left_low = (left - left_high.astype(jnp.float32)).astype(jnp.bfloat16)
    out = jnp.dot(left_high, high, preferred_element_type=jnp.float32)
    out = out + jnp.dot(left_low, high, preferred_element_type=jnp.float32)
    return out + jnp.dot(left_high, low, preferred_element_type=jnp.float32)


def filter_kernel(parts, *refs):
    taps_ref, band_high, band_low, fold_high, fold_low = refs[:5]
    blocks = refs[5 : 5 + 3 * parts]
    out_ref, field_ref, grid_ref, first_ref, second_ref, third_ref = refs[5 + 3 * parts :]
    size_x, size_y, size_z = out_ref.shape
    wide_y, wide_x, lanes = first_ref.shape
    odd = odd_column()
    grids = []
    for part in range(parts):
        wrap, own, pair = (block[...] for block in blocks[3 * part : 3 * part + 3])
        grids.append((jnp.where(odd, pair, wrap), own, jnp.where(odd, wrap, pair)))
    share = wide_y // 16
    for y_start in range(0, wide_y, share):
        for part in range(parts):
            start = 0
            for block in grids[part]:
                rows = block.shape[0]
                for y in range(y_start, y_start + share):
                    grid_ref[y, start : start + rows, part * size_z : (part + 1) * size_z] = (
                        block[:, y * size_z : (y + 1) * size_z]
                    )
                start += rows
        chosen = slice(y_start, y_start + share)
        grid = grid_ref[chosen].reshape(share * wide_x, parts * size_z)
        first_ref[chosen] = split_dot(grid, band_high[...], band_low[...]).reshape(
            share, wide_x, lanes
        )

    def tap(distance, rows):
        return jnp.broadcast_to(taps_ref[distance : distance + 1, :], (rows, lanes))

    def smooth(y, carry):
        run = tap(0, wide_x) * first_ref[y + RADIUS]
        for d in range(1, RADIUS + 1):
            pair = first_ref[y + (RADIUS - d)] + first_ref[y + (RADIUS + d)]
            run = run + tap(d, wide_x) * pair
        second_ref[y] = run
        run = tap(0, size_x) * second_ref[y, RADIUS : RADIUS + size_x, :]
        for d in range(1, RADIUS + 1):
            pair = (
                second_ref[y, RADIUS - d : RADIUS - d + size_x, :]
                + second_ref[y, RADIUS + d : RADIUS + d + size_x, :]
            )
            run = run + tap(d, size_x) * pair
        third_ref[y] = run
        return carry

    lax.fori_loop(0, size_y, smooth, 0, unroll=4)
    filtered = third_ref[...].reshape(size_y * size_x, lanes)
    folded = split_dot(filtered, fold_high[...], fold_low[...]).reshape(size_y, size_x, size_z)
    for y in range(size_y):
        out_ref[:, y, :] = folded[y]
        field_ref[:, y * size_z : (y + 1) * size_z] = folded[y]


def potential_kernel(
    capacity, weight, piece, place_vmem, grid_ref, field_ref, near_ref, far_ref,
    out_ref, grid_hbm, right_ref, corner_ref, whole_ref, place_ref, sems,
):
    copies = [
        pltpu.make_async_copy(place_vmem, place_ref, sems.at[0]),
        pltpu.make_async_copy(grid_ref, grid_hbm, sems.at[1]),
    ]
    for copy in copies:
        copy.start()
    points = near_ref.shape[1]
    half = field_ref.shape[1] // 2
    odd = odd_row() == 1
    low, high = field_ref[:, :half] * weight, field_ref[:, half:] * weight
    first = True
    over_points = (((1,), (1,)), ((), ()))
    for values_ref, source in (
        (near_ref, jnp.where(odd, high, low)),
        (far_ref, jnp.where(odd, low, high)),
    ):
        for q in range(points // piece):
            field = jnp.concatenate(
                [
                    source[x : x + 1, :]
                    for x in range(q * piece // half, (q + 1) * piece // half)
                ],
                axis=1,
            )
            block = values_ref[:, q * piece : (q + 1) * piece]
            weighted = (field * block.astype(jnp.float32)).astype(jnp.bfloat16)
            right = lax.dot_general(
                block, weighted[LANES:], over_points, preferred_element_type=jnp.float32
            )
            corner = lax.dot_general(
                block[:LANES], weighted[:LANES], over_points, preferred_element_type=jnp.float32
            )
            right_ref[...] = right if first else right_ref[...] + right
            corner_ref[...] = corner if first else corner_ref[...] + corner
            first = False

    blocks, rows, _ = whole_ref.shape
    edge = LANES // rows
    whole_ref[:edge, :, :LANES] = corner_ref[...].reshape(edge, rows, -1).astype(jnp.bfloat16)
    whole_ref[edge:, :, :LANES] = (
        right_ref[:LANES].T.reshape(blocks - edge, rows, -1).astype(jnp.bfloat16)
    )
    whole_ref[:, :, LANES:] = right_ref[...].reshape(blocks, rows, -1).astype(jnp.bfloat16)
    for copy in copies:
        copy.wait()

    def visit(j, carry):
        t, k = j // capacity, j % capacity
        out_ref[t, k] = whole_ref[jnp.minimum(place_ref[0, j], blocks - 1)]
        return carry

    lax.fori_loop(0, out_ref.shape[0] * capacity, visit, 0, unroll=16)


def unpack_kernel(tile_count, tile_ref, back_ref, out_hbm, count_ref, sem):
    def visit(i, t, slot):
        pltpu.make_async_copy(back_ref.at[t, slot], out_hbm.at[i], sem.at[0]).start()

    for_each_slab(tile_ref, count_ref, tile_count, out_hbm.shape[0], visit)
    pltpu.make_async_copy(out_hbm, out_hbm, sem.at[0]).wait()


def wrap_of(i):
    return i - 1 + 2 * (i % 2)


def pair_of(i):
    return i + 1 - 2 * (i % 2)


def moved(block, targets):
    axes = tuple(targets)
    sizes = [lax.axis_size(axis) for axis in axes]
    pairs = []
    for source in np.ndindex(*sizes):
        target = [targets[axis](i) % n for i, axis, n in zip(source, axes, sizes)]
        pairs.append(
            (int(np.ravel_multi_index(source, sizes)), int(np.ravel_multi_index(target, sizes)))
        )
    return lax.ppermute(block, axes, pairs)


def band_tables(size_z, neighbours):
    tap_table, mix = kernel_tables(RADIUS)

    def band(shift):
        table = np.zeros((size_z, len(ALPHAS), size_z), np.float64)
        for m in range(len(ALPHAS)):
            for source in range(size_z):
                for target in range(size_z):
                    offset = source + shift - target
                    if abs(offset) <= RADIUS:
                        table[source, m, target] = tap_table[m][offset + RADIUS]
        return table.reshape(size_z, len(ALPHAS) * size_z)

    own, low, high = band(0), band(-size_z), band(size_z)
    bands = {0: [own + low + high], 1: [own, low + high], 2: [own, low, high]}[neighbours]
    taps = np.zeros((16, len(ALPHAS) * size_z), np.float64)
    for d in range(RADIUS + 1):
        taps[d] = np.repeat([row[RADIUS + d] for row in tap_table], size_z)
    fold = np.concatenate([mix[m] * np.eye(size_z) for m in range(len(ALPHAS))], axis=0)

    def split(table):
        high = table.astype(np.float32).astype(jnp.bfloat16)
        low = (table - high.astype(np.float64)).astype(np.float32).astype(jnp.bfloat16)
        return [high, low]

    return [taps.astype(np.float32), *split(np.concatenate(bands, axis=0)), *split(fold)]


def local(orbital_values, dm_slabs, slab_tile, slab_place):
    size_x, size_y, size_z, list_orb = orbital_values.shape
    slab_count, atom_orb, _ = dm_slabs.shape
    list_blk = list_orb // atom_orb
    tile_count = lax.axis_size("gx") * lax.axis_size("gy")
    capacity = max(2, 2 * ((list_blk + tile_count - 1) // tile_count))
    chunks = list_orb // LANES
    tile_points = size_x * size_y * size_z
    plane = size_y * size_z
    counts = pltpu.SMEM((tile_count,), jnp.int32)

    groups = math.gcd(tile_count, 4)
    packed_shape = (tile_count, capacity * chunks + 1, atom_orb, LANES)
    packed = pl.pallas_call(
        functools.partial(pack_kernel, capacity, chunks, float(list_blk), groups),
        out_shape=jax.ShapeDtypeStruct(packed_shape, jnp.bfloat16),
        in_specs=[HBM_SPEC] * 3,
        out_specs=HBM_SPEC,
        scratch_shapes=[
            pltpu.SMEM((slab_count,), jnp.int32),
            pltpu.SMEM((slab_count,), jnp.int32),
            pltpu.VMEM(dm_slabs.shape, dm_slabs.dtype),
            counts,
            pltpu.SMEM((tile_count * capacity,), jnp.int32),
            pltpu.VMEM((tile_count, atom_orb, LANES), jnp.float32),
            pltpu.VMEM(packed_shape, jnp.bfloat16),
            pltpu.SemaphoreType.DMA((3,)),
            pltpu.SemaphoreType.DMA((groups,)),
        ],
        compiler_params=grant(4),
        name="pack",
    )(in_hbm(slab_tile), in_hbm(slab_place), in_hbm(dm_slabs))
    arrived = lax.all_to_all(packed, ("gx", "gy"), split_axis=0, concat_axis=0, tiled=True)
    half = plane // 2
    half_points = tile_points // 2
    piece = 4 * half
    bf16 = lambda *shape: jax.ShapeDtypeStruct(shape, jnp.bfloat16)
    f32 = lambda *shape: jax.ShapeDtypeStruct(shape, jnp.float32)
    near, far = pl.pallas_call(
        functools.partial(turn_kernel, size_x),
        out_shape=(
            pltpu.VMEM((list_orb, half_points), jnp.bfloat16),
            bf16(list_orb, half_points),
        ),
        in_specs=[HBM_SPEC],
        out_specs=(VMEM_SPEC, HBM_SPEC),
        scratch_shapes=[
            pltpu.VMEM((tile_points, list_orb), jnp.bfloat16),
            pltpu.VMEM((list_orb, half_points), jnp.bfloat16),
            pltpu.SemaphoreType.DMA((size_x // 2,)),
            pltpu.SemaphoreType.DMA((1,)),
        ],
        compiler_params=grant(20),
        cost_estimate=cost(0, 4 * tile_points * list_orb),
        name="turn",
    )(in_hbm(orbital_values.reshape(tile_points, list_orb)))

    slots = LANES * ((tile_count * capacity + LANES - 1) // LANES)
    product = 2 * half_points * list_orb * list_orb
    near_y, places, square, last, far = pl.pallas_call(
        functools.partial(near_kernel, capacity, chunks, piece),
        out_shape=(
            f32(size_x, half),
            jax.ShapeDtypeStruct((1, slots), jnp.int32),
            bf16(list_orb - LANES, list_orb - LANES),
            bf16(list_orb, 2 * LANES),
            pltpu.VMEM((list_orb, half_points), jnp.bfloat16),
        ),
        in_specs=[VMEM_SPEC, VMEM_SPEC, HBM_SPEC],
        out_specs=(VMEM_SPEC,) * 5,
        scratch_shapes=[
            pltpu.VMEM((tile_count * capacity * atom_orb, LANES), jnp.float32),
            pltpu.VMEM((list_orb, list_orb), jnp.float32),
            pltpu.SemaphoreType.DMA((1,)),
        ],
        compiler_params=grant(20),
        cost_estimate=cost(product, 2 * half_points * list_orb),
        name="near",
    )(arrived, near, in_hbm(far))
    from_wrap = moved(near_y, {"gy": wrap_of})
    far_y = pl.pallas_call(
        functools.partial(far_kernel, piece),
        out_shape=f32(size_x, half),
        in_specs=[VMEM_SPEC] * 3,
        out_specs=VMEM_SPEC,
        compiler_params=grant(20),
        cost_estimate=cost(product, 2 * half_points * list_orb),
        name="far",
    )(square, last, far)
    from_pair = moved(far_y, {"gy": pair_of})

    wide = 2 * plane
    own, to_wrap, to_pair = pl.pallas_call(
        join_kernel,
        out_shape=(f32(size_x, wide), f32(RADIUS, wide), f32(RADIUS, wide)),
        in_specs=[VMEM_SPEC] * 4,
        out_specs=(VMEM_SPEC,) * 3,
        compiler_params=grant(2),
        name="join",
    )(near_y, far_y, from_wrap, from_pair)
    layers = lax.axis_size("gz")
    blocks = []
    for shift in {1: [0], 2: [0, 1]}.get(layers, [0, 1, -1]):
        along = {"gz": lambda layer: layer + shift} if shift else {}
        blocks.append(moved(to_wrap, {"gx": wrap_of, **along}))
        blocks.append(moved(own, along) if shift else own)
        blocks.append(moved(to_pair, {"gx": pair_of, **along}))
    parts = len(blocks) // 3
    tables = band_tables(size_z, parts - 1)
    lanes = tables[0].shape[1]
    wide_x, wide_y = size_x + 2 * RADIUS, size_y + 2 * RADIUS
    potential, field = pl.pallas_call(
        functools.partial(filter_kernel, parts),
        out_shape=(pltpu.VMEM((size_x, size_y, size_z), jnp.float32), f32(size_x, plane)),
        in_specs=[VMEM_SPEC] * (len(tables) + len(blocks)),
        out_specs=(VMEM_SPEC,) * 2,
        scratch_shapes=[
            pltpu.VMEM((wide_y, wide_x, parts * size_z), jnp.float32),
            pltpu.VMEM((wide_y, wide_x, lanes), jnp.float32),
            pltpu.VMEM((size_y, wide_x, lanes), jnp.float32),
            pltpu.VMEM((size_y, size_x, lanes), jnp.float32),
        ],
        compiler_params=grant(12),
        name="filter",
    )(*map(jnp.asarray, tables), *blocks)

    returned, potential = pl.pallas_call(
        functools.partial(
            potential_kernel, capacity, float(tile_points) ** (-0.5), 4 * piece
        ),
        out_shape=(
            bf16(tile_count, capacity, atom_orb, list_orb),
            f32(size_x, size_y, size_z),
        ),
        in_specs=[VMEM_SPEC] * 5,
        out_specs=(VMEM_SPEC, HBM_SPEC),
        scratch_shapes=[
            pltpu.VMEM((list_orb, list_orb - LANES), jnp.float32),
            pltpu.VMEM((LANES, LANES), jnp.float32),
            pltpu.VMEM((list_blk, atom_orb, list_orb), jnp.bfloat16),
            pltpu.SMEM((1, slots), jnp.int32),
            pltpu.SemaphoreType.DMA((2,)),
        ],
        compiler_params=grant(20),
        name="potential",
    )(places, potential, field, near, far)
    back = lax.all_to_all(returned, ("gx", "gy"), split_axis=0, concat_axis=0, tiled=True)
    own_rows = pl.pallas_call(
        functools.partial(unpack_kernel, tile_count),
        out_shape=bf16(slab_count, atom_orb, list_orb),
        in_specs=[SMEM_SPEC, VMEM_SPEC],
        out_specs=HBM_SPEC,
        scratch_shapes=[counts, pltpu.SemaphoreType.DMA((1,))],
        compiler_params=grant(4),
        name="unpack",
    )(slab_tile, back)
    return (potential, own_rows)


def solution(mesh):
    placed = (
        P("gx", "gy", "gz", None),
        P(("gx", "gy", "gz"), None, None),
        P(("gx", "gy", "gz")),
        P(("gx", "gy", "gz")),
    )

    return jax.shard_map(
        local,
        mesh=mesh,
        in_specs=placed,
        out_specs=(P("gx", "gy", "gz"), P(("gx", "gy", "gz"), None, None)),
        check_vma=False,
    )
```
